128 devices in a mesh: row: 16 (over x, z), col: 8 (over y, core).
Axes of the slice: x: 4, y: 4, z: 4, core: 2. Of those that a mesh axis runs over, the one named last changes fastest.
Arguments:
- trailing: bfloat16 [49152, 16384], P('row', 'col'), may hold values from -6 to 6
- panels: bfloat16 [2, 256, 49152], P(None, 'col', 'row'), as said below
- diag_lower: bfloat16 [2, 256, 256], P(None, 'col'), as said below
- pivot_src: int32 [2, 256], replicated, may hold values from 0 to 49151, as said below
- pivot_dst: int32 [2, 256], replicated, may hold values from 256 to 49152, as said below
Outputs:
- matrix: bfloat16 [49152, 16384], P('row', 'col')
The draws below stay inside these ranges and needn't reach their ends.
Inputs may be any that keep to these rules, and one draw needn't show every extreme that they name: The entries of pivot_src[k] are distinct rows, none below 256 * k. Entries of pivot_dst[k] under 49152 are distinct, not below 256 * (k + 1), and are exactly the entries of pivot_src[k] that are not below 256 * (k + 1); an entry equal to 49152 marks an old row t + j that is itself one of pivot_src[k]. panels[k, c, r] is zero for r < 256 * (k + 1). diag_lower[k, r, c] is zero for c >= r.
All inputs are finite; a program needn't handle non-finite values.
Results may differ from the reference program's by a relative error of at most 0.0062.
Values may be sent and summed in bfloat16 or wider, within the bound.
No kernel may reach another device: no remote copies, remote signals or barrier semaphores. Data moves between devices by JAX's collectives and lax.ppermute only.
A program may use at most 128 MiB of HBM per device.

```python
import jax
import jax.numpy as jnp
from jax import lax

NB = 256
PANELS = 2
ROWS_DEV = 3072
M = 49152
C = 16384
N_ROW = 16


def pivot_lists(key):
    base = jax.random.fold_in(key, 5)
    sources = []
    targets = []
    top_count = NB // 8
    for panel_step in range(PANELS):
        step_key = jax.random.fold_in(base, panel_step)
        key_top, key_low, key_mix = jax.random.split(step_key, 3)
        top_order = jax.random.permutation(key_top, NB).astype(jnp.int32)
        low_rows = jax.random.permutation(key_low, M - (panel_step + 1) * NB)[:NB - top_count].astype(jnp.int32) + (panel_step + 1) * NB
        chosen = jnp.concatenate([top_order[:top_count] + panel_step * NB, low_rows])
        shuffle = jax.random.permutation(key_mix, NB)
        sources.append(chosen[shuffle])
        targets.append(jnp.full((NB,), M, jnp.int32).at[top_order[top_count:]].set(low_rows))
    return (jnp.stack(sources).astype(jnp.int32), jnp.stack(targets).astype(jnp.int32))


def draw_pivot_src(key, part):
    return pivot_lists(key)[0]


def draw_pivot_dst(key, part):
    return pivot_lists(key)[1]


def draw_panels(key, part):
    shape = (PANELS, NB, M)
    values = jax.random.normal(key, shape, jnp.float32)
    steps = lax.broadcasted_iota(jnp.int32, shape, 0)
    row_ids = lax.broadcasted_iota(jnp.int32, shape, 2)
    live = row_ids >= (steps + 1) * NB
    return jnp.where(live, values * NB ** (-0.5), 0.0).astype(jnp.bfloat16)


def draw_diag_lower(key, part):
    shape = (PANELS, NB, NB)
    key_values, key_signs, key_sizes = jax.random.split(key, 3)
    values = jax.random.normal(key_values, shape, jnp.float32)
    magnitude = jax.random.uniform(key_sizes, shape, jnp.float32, 0.85, 0.93)
    signs = jnp.where(jax.random.uniform(key_signs, shape, jnp.float32) < 0.5, -1.0, 1.0)
    row_ids = lax.broadcasted_iota(jnp.int32, shape, 1)
    col_ids = lax.broadcasted_iota(jnp.int32, shape, 2)
    lower_part = jnp.where(col_ids < row_ids, values * (0.05 * NB ** (-0.5)), 0.0)
    return jnp.where(col_ids == row_ids - 1, signs * magnitude, lower_part).astype(jnp.bfloat16)


def block_levels(own_key, dims, pieces, smallest, high):
    loudness, own = 1.0, jax.random.fold_in(own_key, 6)
    for axis_at, blocks in pieces:
        draws = jnp.exp(jax.random.uniform(jax.random.fold_in(own, axis_at), (blocks,), jnp.float32, smallest / len(pieces), high / len(pieces)))
        loudness = loudness * jnp.repeat(draws, dims[axis_at] // blocks).reshape([-1 if axis == axis_at else 1 for axis in range(len(dims))])
    return loudness


def centred(rng, shape, width, reach, cuts=(), kind=jnp.bfloat16):
    values = jax.random.normal(rng, shape, jnp.float32) * width
    if len(cuts) > 0:
        values = block_levels(rng, shape, cuts, -0.22, 0.18) * values
    return jnp.clip(values, min=-reach, max=reach).astype(kind)


def setup_inputs(seed: int = 0) -> dict:
    arg_keys = jax.random.split(jax.random.key(seed), 6)
    return {
        "trailing": centred(arg_keys[0], (M, C), 1.0, 6.0, ((0, 16), (1, 8))),
        "panels": draw_panels(jax.random.fold_in(arg_keys[5], 71), 0),
        "diag_lower": draw_diag_lower(jax.random.fold_in(arg_keys[5], 71), 0),
        "pivot_src": draw_pivot_src(jax.random.fold_in(arg_keys[5], 71), 0),
        "pivot_dst": draw_pivot_dst(jax.random.fold_in(arg_keys[5], 71), 0),
    }


def reference(trailing, panels, diag_lower, pivot_src, pivot_dst):
    matrix = trailing
    identity = jnp.eye(NB, dtype=jnp.float32)
    for panel_step in range(PANELS):
        start_row = panel_step * NB
        top_rows = matrix[start_row:start_row + NB]
        chosen = jnp.take(matrix, pivot_src[panel_step], axis=0).astype(jnp.float32)
        swapped = matrix.at[pivot_dst[panel_step]].set(top_rows, mode='drop')
        unit_lower = diag_lower[panel_step].astype(jnp.float32) + identity
        upper_rows = jax.scipy.linalg.solve_triangular(unit_lower, chosen, lower=True, unit_diagonal=True).astype(jnp.bfloat16)
        row_blocks = swapped.reshape(N_ROW, ROWS_DEV, C)
        col_blocks = panels[panel_step].reshape(NB, N_ROW, ROWS_DEV).transpose(1, 0, 2)

        def update(pairing):
            row_block, segment = pairing
            product = lax.dot_general(segment.astype(jnp.float32), upper_rows.astype(jnp.float32), (((0,), (0,)), ((), ())), preferred_element_type=jnp.float32)
            return (row_block.astype(jnp.float32) - product).astype(jnp.bfloat16)
        result = lax.map(update, (row_blocks, col_blocks)).reshape(M, C)
        matrix = result.at[start_row:start_row + NB].set(upper_rows)
    return matrix
```

```python
import functools

import jax
import jax.numpy as jnp
from jax import lax
from jax.experimental import pallas as pl
from jax.experimental.pallas import tpu as pltpu
from jax.sharding import PartitionSpec as P

F32, BF16 = jnp.float32, jnp.bfloat16
TN = (((0,), (0,)), ((), ()))
NN = (((1,), (0,)), ((), ()))


def dot(a, b, dims=NN):
    return lax.dot_general(a, b, dims, preferred_element_type=F32)


def solve_kernel(inv_ref, sel_ref, c_ref, u_ref):
    width = inv_ref.shape[1]

    def apply(k, rows):
        rest = inv_ref[k]
        total = None
        for _ in range(3):
            part = rest.astype(BF16)
            rest = rest - part.astype(F32)
            term = dot(part, rows)
            total = term if total is None else total + term
        return total.astype(BF16)

    first = apply(0, c_ref[:width, :])
    u_ref[:width, :] = first
    later = c_ref[width : 2 * width, :].astype(F32) - dot(sel_ref[...], first, TN)
    u_ref[width : 2 * width, :] = apply(1, later.astype(BF16))


def solve(inverse, selected, rows, tile=512):
    width, cols = inverse.shape[1], rows.shape[1]
    return pl.pallas_call(
        solve_kernel,
        out_shape=jax.ShapeDtypeStruct((2 * width, cols), BF16),
        grid=(cols // tile,),
        in_specs=[
            pl.BlockSpec(inverse.shape, lambda i: (0, 0, 0)),
            pl.BlockSpec(selected.shape, lambda i: (0, 0)),
            pl.BlockSpec((2 * width, tile), lambda i: (0, i)),
        ],
        out_specs=pl.BlockSpec((2 * width, tile), lambda i: (0, i)),
        compiler_params=pltpu.CompilerParams(vmem_limit_bytes=32 << 20),
    )(inverse, selected, rows)


def update_kernel(width, begin, hole, slot, place, a_ref, l0_ref, l1_ref, u_ref, d_ref, o_ref, x_ref, df_ref):
    step = pl.program_id(0)
    rows = a_ref.shape[0]

    @pl.when(step == 0)
    def _():
        df_ref[...] = d_ref[...].astype(F32)

    x_ref[...] = a_ref[...].astype(F32)

    def fill(j, carry):
        x_ref[pl.ds(hole[j] - step * rows, 1), :] = df_ref[pl.ds(slot[j], 1), :]
        return carry

    lax.fori_loop(begin[step], begin[step + 1], fill, 0)
    mid = (x_ref[...] - dot(l0_ref[...], u_ref[:width, :], TN)).astype(BF16).astype(F32)
    o_ref[...] = (mid - dot(l1_ref[...], u_ref[width:, :], TN)).astype(BF16)

    @pl.when((place[0] == 0) & (step < 2 * width // rows))
    def _():
        o_ref[...] = u_ref[pl.ds(pl.multiple_of(step * rows, rows), rows), :]


def update(slab, l0, l1, upper, displaced, begin, hole, slot, place, rows):
    height, cols = slab.shape
    width, n = l0.shape[0], displaced.shape[0]
    return pl.pallas_call(
        functools.partial(update_kernel, width),
        out_shape=jax.ShapeDtypeStruct(slab.shape, BF16),
        grid_spec=pltpu.PrefetchScalarGridSpec(
            num_scalar_prefetch=4,
            grid=(height // rows,),
            in_specs=[
                pl.BlockSpec((rows, cols), lambda i, *_: (i, 0)),
                pl.BlockSpec((width, rows), lambda i, *_: (0, i)),
                pl.BlockSpec((width, rows), lambda i, *_: (0, i)),
                pl.BlockSpec((2 * width, cols), lambda i, *_: (0, 0)),
                pl.BlockSpec((n, cols), lambda i, *_: (0, 0)),
            ],
            out_specs=pl.BlockSpec((rows, cols), lambda i, *_: (i, 0)),
            scratch_shapes=[pltpu.VMEM((rows, cols), F32), pltpu.VMEM((n, cols), F32)],
        ),
        compiler_params=pltpu.CompilerParams(vmem_limit_bytes=48 << 20),
        cost_estimate=pl.CostEstimate(
            flops=4 * height * cols * width, bytes_accessed=4 * height * cols, transcendentals=0
        ),
    )(begin, hole, slot, place, slab, l0, l1, upper, displaced)


def per_device(trailing, panels, diag_lower, pivot_src, pivot_dst):
    height, cols = trailing.shape
    width = diag_lower.shape[2]
    block = 256
    devices = lax.axis_size("row")
    place = lax.axis_index("row")
    offset = place * height
    count = jnp.arange(width, dtype=jnp.int32)
    here = jnp.arange(height, dtype=jnp.int32)
    src0, src1 = pivot_src[0], pivot_src[1]
    dst0, dst1 = pivot_dst[0], pivot_dst[1]

    def original(position):
        hit = dst0[None, :] == position[:, None]
        return jnp.where(hit.any(1), (hit * count).sum(1), position)

    wanted = jnp.concatenate([src0, original(src1)]) - offset
    onehot = (wanted[:, None] == here[None, :]).astype(BF16)
    picked = dot(onehot, trailing).astype(BF16)
    top = jnp.where(place == 0, trailing[: 2 * width], jnp.zeros((), BF16))
    moved = lax.psum((picked, top), "row")

    whole = lax.all_gather(panels, "col", axis=1, tiled=True)

    position = jnp.concatenate([src1, width + count]) - offset
    chosen = (here[:, None] == position[None, :]).astype(BF16)
    piece = dot(panels[0], chosen).astype(BF16)
    piece = lax.all_to_all(jnp.broadcast_to(piece[None], (devices,) + piece.shape), "row", 0, 0)
    piece = piece.astype(F32).sum(0).astype(BF16)
    small = lax.all_gather(
        jnp.concatenate([piece, diag_lower[0], diag_lower[1]], axis=1), "col", axis=0, tiled=True
    )
    selected, below = small[:, :width], small[:, width : 2 * width]
    unit = jnp.stack([small[:, 2 * width : 3 * width], small[:, 3 * width :]]).astype(F32)
    eye = jnp.eye(width, dtype=F32)
    inverse = jax.scipy.linalg.solve_triangular(
        unit + eye, jnp.broadcast_to(eye, unit.shape), lower=True, unit_diagonal=True
    )

    again = (dst0[:, None] == dst1[None, :]).any(1)
    rest = jnp.concatenate([jnp.where(again, devices * height, dst0), dst1]) - offset
    origin = jnp.concatenate([count, original(width + count)])
    rest = jnp.where((rest >= 0) & (rest < height), rest, height)
    key = rest * (2 * width) + jnp.arange(2 * width, dtype=jnp.int32)
    rank = (key[None, :] < key[:, None]).sum(1)
    place_of = rank[None, :] == jnp.arange(2 * width, dtype=jnp.int32)[:, None]
    hole = jnp.where(place_of, rest[None, :], 0).sum(1)
    slot = jnp.where(place_of, origin[None, :], 0).sum(1)
    edges = jnp.arange(height // block + 1, dtype=jnp.int32) * block
    begin = (rest[None, :] < edges[:, None]).sum(1).astype(jnp.int32)

    landing = (dst1 - offset)[:, None] == here[None, :]
    l0 = jnp.where(landing.any(0)[None, :], dot(below, landing.astype(BF16)).astype(BF16), whole[0])

    upper = solve(inverse, selected, moved[0])
    return update(
        trailing, l0, whole[1], upper, moved[1], begin, hole, slot, place[None].astype(jnp.int32), block
    )


def solution(mesh):
    placed = (P("row", "col"), P(None, "col", "row"), P(None, "col", None), P(), P())
    return jax.shard_map(
        per_device, mesh=mesh, in_specs=placed, out_specs=P("row", "col"), check_vma=False
    )
```

```python
import functools

import jax
import jax.numpy as jnp
from jax import lax
from jax.experimental import pallas as pl
from jax.experimental.pallas import tpu as pltpu
from jax.sharding import PartitionSpec as P

F32, BF16, I32 = jnp.float32, jnp.bfloat16, jnp.int32
TN = (((0,), (0,)), ((), ()))
NN = (((1,), (0,)), ((), ()))
CAP = 64
LANES = 128


def dot(a, b, dims=NN, precision=None):
    return lax.dot_general(a, b, dims, preferred_element_type=F32, precision=precision)


def params(mib):
    return pltpu.CompilerParams(vmem_limit_bytes=mib << 20)


def gather_kernel(index_ref, a_ref, o_ref, hot_ref):
    @pl.when(pl.program_id(0) == 0)
    def _():
        here = lax.broadcasted_iota(I32, hot_ref.shape, 1)
        hot_ref[...] = jnp.where(here == index_ref[...], 1.0, 0.0).astype(BF16)

    rows = dot(hot_ref[...], a_ref[...]).astype(BF16)
    part = o_ref.shape[2]
    for b in range(o_ref.shape[0]):
        o_ref[b] = rows[:, b * part : (b + 1) * part]


def gather(slab, index, devices):
    height, cols = slab.shape
    slots, part = index.shape[0], cols // devices
    two = 2
    return pl.pallas_call(
        gather_kernel,
        out_shape=jax.ShapeDtypeStruct((devices, slots, part), BF16),
        grid=(devices // two,),
        in_specs=[
            pl.BlockSpec((slots, 1), lambda i: (0, 0)),
            pl.BlockSpec((height, two * part), lambda i: (0, i)),
        ],
        out_specs=pl.BlockSpec((two, slots, part), lambda i: (i, 0, 0)),
        scratch_shapes=[pltpu.VMEM((slots, height), BF16)],
        compiler_params=params(32),
        cost_estimate=pl.CostEstimate(
            flops=2 * slots * height * cols, bytes_accessed=2 * cols * (height + slots), transcendentals=0
        ),
    )(index[:, None], slab)


def invert_kernel(base, d_ref, o_ref):
    panels, width, _ = d_ref.shape
    count = width // base
    blocks = []
    for k in range(panels):
        for b in range(count):
            at = slice(b * base, (b + 1) * base)
            blocks.append(d_ref[k, at, at].astype(F32))
    lower = jnp.stack(blocks)
    row = lax.broadcasted_iota(I32, lower.shape, 1)
    col = lax.broadcasted_iota(I32, lower.shape, 2)
    x = jnp.where(row == col, 1.0, 0.0).astype(F32)
    for c in range(base - 1):
        x = x - lower[:, :, c : c + 1] * x[:, c : c + 1, :]
    o_ref[...] = jnp.zeros(o_ref.shape, F32)
    for k in range(panels):
        for b in range(count):
            at = slice(b * base, (b + 1) * base)
            o_ref[k, at, at] = x[k * count + b]
    size = base
    while size < width:
        for k in range(panels):
            for o in range(0, width, 2 * size):
                up, down = slice(o, o + size), slice(o + size, o + 2 * size)
                inner = dot(d_ref[k, down, up].astype(F32), o_ref[k, up, up], NN, lax.Precision.HIGHEST)
                o_ref[k, down, up] = -dot(o_ref[k, down, down], inner, NN, lax.Precision.HIGHEST)
        size *= 2


def invert(lower):
    return pl.pallas_call(
        functools.partial(invert_kernel, min(32, lower.shape[1])),
        out_shape=jax.ShapeDtypeStruct(lower.shape, F32),
        compiler_params=params(16),
        cost_estimate=pl.CostEstimate(flops=1 << 31, bytes_accessed=1 << 20, transcendentals=0),
    )(lower)


def apply_inverse(inverse, rows):
    total = None
    for _ in range(3):
        part = inverse.astype(BF16)
        inverse = inverse - part.astype(F32)
        term = dot(part, rows)
        total = term if total is None else total + term
    return total.astype(BF16)


def first_kernel(width, inv_ref, own_ref, key_ref, r_ref, y_ref, u_ref, c_ref):
    devices, slots, part = r_ref.shape
    zero = r_ref[0]
    total = jnp.where(own_ref[...] > 0, zero.astype(F32), 0.0)
    for s in range(1, devices):
        total = total + r_ref[s].astype(F32)
    rows = total.astype(BF16)
    c_ref[...] = rows[width:]
    upper = apply_inverse(inv_ref[0], rows[:width])
    u_ref[...] = upper
    want = lax.broadcasted_iota(I32, (devices * CAP, slots), 0)
    want = (want // CAP) * slots + want % CAP
    hot = jnp.where(want == key_ref[...], 1.0, 0.0).astype(BF16)
    fill = dot(hot, zero).astype(BF16)
    for d in range(devices):
        y_ref[d, :width, :] = upper
        y_ref[d, width:, :] = fill[d * CAP : (d + 1) * CAP]


def first(inverse, own, key, received, width):
    devices, slots, part = received.shape
    return pl.pallas_call(
        functools.partial(first_kernel, width),
        out_shape=(
            jax.ShapeDtypeStruct((devices, width + CAP, part), BF16),
            jax.ShapeDtypeStruct((width, part), BF16),
            jax.ShapeDtypeStruct((slots - width, part), BF16),
        ),
        compiler_params=params(32),
        cost_estimate=pl.CostEstimate(flops=1 << 29, bytes_accessed=4 << 20, transcendentals=0),
    )(inverse, own[:, None], key[None, :], received)


def second_kernel(inv_ref, sel_ref, u_ref, c_ref, y_ref):
    later = c_ref[...].astype(F32) - dot(sel_ref[...], u_ref[...], TN)
    upper = apply_inverse(inv_ref[1], later.astype(BF16))
    for d in range(y_ref.shape[0]):
        y_ref[d] = upper


def second(inverse, selected, upper, rows, devices):
    width, part = rows.shape
    return pl.pallas_call(
        second_kernel,
        out_shape=jax.ShapeDtypeStruct((devices, width, part), BF16),
        compiler_params=params(16),
        cost_estimate=pl.CostEstimate(flops=1 << 28, bytes_accessed=2 << 20, transcendentals=0),
    )(inverse, selected, upper, rows)


def update_kernel(
    width, begin, hole, slot, place, a_ref, l_ref, y0_ref, y1_ref, slab_ref, rest_ref, o_ref, u_ref, d_ref, sem
):
    step = pl.program_id(0)
    rows = a_ref.shape[0]
    devices, _, part = y1_ref.shape
    more = begin[pl.num_programs(0)] > CAP

    @pl.when(step == 0)
    def _():
        for e in range(devices):
            at = slice(e * part, (e + 1) * part)
            u_ref[:width, at] = y0_ref[e, :width, :]
            u_ref[width:, at] = y1_ref[e]
            d_ref[:CAP, at] = y0_ref[e, width:, :]

    @pl.when((step == 0) & (place[0] == 0))
    def _():
        copy = pltpu.make_async_copy(slab_ref.at[: 2 * width], d_ref, sem)
        copy.start()
        copy.wait()

    @pl.when((step == 0) & (place[0] != 0) & more)
    def _():
        copy = pltpu.make_async_copy(rest_ref.at[CAP:], d_ref.at[CAP:], sem)
        copy.start()
        copy.wait()

    group = 16

    def fill(j, carry):
        to, source = hole[j] - step * rows, slot[j]
        taken = d_ref[pl.ds(pl.multiple_of(source // group * group, group), group), :].astype(F32)
        lane = lax.broadcasted_iota(I32, taken.shape, 0)
        row = jnp.where(lane == source % group, taken, 0.0).sum(0, keepdims=True)
        target = pl.ds(pl.multiple_of(to // group * group, group), group)
        a_ref[target, :] = jnp.where(lane == to % group, row, a_ref[target, :].astype(F32)).astype(BF16)
        return carry

    lax.fori_loop(begin[step], begin[step + 1], fill, 0)
    o_ref[...] = (a_ref[...].astype(F32) - dot(l_ref[...], u_ref[...], TN)).astype(BF16)

    @pl.when((place[0] == 0) & (step < 2 * width // rows))
    def _():
        o_ref[...] = u_ref[pl.ds(pl.multiple_of(step * rows, rows), rows), :]


def update(slab, lower, y0, y1, rest, begin, hole, slot, place, rows):
    height, cols = slab.shape
    width = lower.shape[0] // 2
    return pl.pallas_call(
        functools.partial(update_kernel, width),
        out_shape=jax.ShapeDtypeStruct(slab.shape, BF16),
        grid_spec=pltpu.PrefetchScalarGridSpec(
            num_scalar_prefetch=4,
            grid=(height // rows,),
            in_specs=[
                pl.BlockSpec((rows, cols), lambda i, *_: (i, 0)),
                pl.BlockSpec((2 * width, rows), lambda i, *_: (0, i)),
                pl.BlockSpec(y0.shape, lambda i, *_: (0, 0, 0)),
                pl.BlockSpec(y1.shape, lambda i, *_: (0, 0, 0)),
                pl.BlockSpec(memory_space=pl.ANY),
                pl.BlockSpec(memory_space=pl.ANY),
            ],
            out_specs=pl.BlockSpec((rows, cols), lambda i, *_: (i, 0)),
            scratch_shapes=[
                pltpu.VMEM((2 * width, cols), BF16),
                pltpu.VMEM((2 * width, cols), BF16),
                pltpu.SemaphoreType.DMA,
            ],
        ),
        compiler_params=params(48),
        cost_estimate=pl.CostEstimate(
            flops=4 * height * cols * width, bytes_accessed=4 * height * cols, transcendentals=0
        ),
    )(begin, hole, slot, place, slab, lower, y0, y1, slab, rest)


def exchange(x):
    return lax.all_to_all(x, "row", 0, 0)


def per_device(trailing, panels, diag_lower, pivot_src, pivot_dst):
    height, cols = trailing.shape
    width = diag_lower.shape[2]
    slots = 2 * width
    block = min(256, width)
    devices = lax.axis_size("row")
    place = lax.axis_index("row")
    offset = place * height
    count = jnp.arange(width, dtype=I32)
    every = jnp.arange(slots, dtype=I32)
    here = jnp.arange(height, dtype=I32)
    src0, src1 = pivot_src[0], pivot_src[1]
    dst0, dst1 = pivot_dst[0], pivot_dst[1]

    def original(position):
        hit = dst0[None, :] == position[:, None]
        return jnp.where(hit.any(1), jnp.where(hit, count[None, :], 0).sum(1), position)

    source = jnp.concatenate([src0, original(src1)])
    owner = source // height
    hit0 = dst0[None, :] == source[:, None]
    hit1 = dst1[None, :] == source[:, None]
    content = jnp.where(
        hit1.any(1),
        jnp.where(hit1, original(width + count)[None, :], 0).sum(1),
        jnp.where(hit0, count[None, :], 0).sum(1),
    )
    local = owner == place
    wanted = jnp.where(local, source - offset, jnp.where(place == 0, content, -1))
    received = exchange(gather(trailing, wanted.astype(I32), devices))

    whole = lax.all_gather(panels, "col", axis=1, tiled=True)

    position = jnp.concatenate([src1, width + count]) - offset
    chosen = (here[:, None] == position[None, :]).astype(BF16)
    piece = dot(panels[0], chosen).astype(BF16)
    piece = exchange(jnp.broadcast_to(piece[None], (devices,) + piece.shape))
    piece = piece.astype(F32).sum(0).astype(BF16)
    small = lax.all_gather(
        jnp.concatenate([piece, diag_lower[0], diag_lower[1]], axis=1), "col", axis=0, tiled=True
    )
    selected, below = small[:, :width], small[:, width:slots]
    inverse = invert(jnp.stack([small[:, slots : slots + width], small[:, slots + width :]]))

    same = owner[:, None] == owner[None, :]
    rank = (same & (every[None, :] < every[:, None])).sum(1).astype(I32)
    key = jnp.where(owner > 0, owner * slots + rank, -1)
    rounds = (jnp.where(owner > 0, rank, 0).max() + CAP) // CAP
    rest = jnp.where(local & (source >= slots), source - offset, height)
    order = (rest[None, :] * slots + every[None, :] < (rest * slots + every)[:, None]).sum(1)
    sort = order[None, :] == every[:, None]
    hole = jnp.where(sort, rest[None, :], 0).sum(1).astype(I32)
    slot = jnp.where(sort, jnp.where(place == 0, content, rank)[None, :], 0).sum(1).astype(I32)
    edges = jnp.arange(height // block + 1, dtype=I32) * block
    begin = (rest[None, :] < edges[:, None]).sum(1).astype(I32)

    landing = (dst1 - offset)[:, None] == here[None, :]
    moved = dot(below, landing.astype(BF16)).astype(BF16)
    lower = jnp.concatenate([jnp.where(landing.any(0)[None, :], moved, whole[0]), whole[1]])

    y0, upper, rows = first(inverse, (owner == 0).astype(I32), key.astype(I32), received, width)
    y1 = second(inverse, selected, upper, rows, devices)

    def fetch(state):
        r, found = state
        want = jnp.arange(devices * CAP, dtype=I32)
        want = want // CAP * slots + want % CAP + r * CAP
        part = dot((want[:, None] == key[None, :]).astype(BF16), received[0]).astype(BF16)
        part = exchange(part.reshape(devices, CAP, -1)).transpose(1, 0, 2).reshape(CAP, cols)
        return r + 1, lax.dynamic_update_slice(found, part, (r * CAP, 0))

    found = lax.while_loop(
        lambda state: state[0] < rounds, fetch, (jnp.ones((), I32), jnp.zeros((slots, cols), BF16))
    )[1]

    return update(
        trailing, lower, exchange(y0), exchange(y1), found, begin, hole, slot, place[None].astype(I32), block
    )


def solution(mesh):
    placed = (P("row", "col"), P(None, "col", "row"), P(None, "col", None), P(), P())
    return jax.shard_map(
        per_device, mesh=mesh, in_specs=placed, out_specs=P("row", "col"), check_vma=False
    )
```

```python
import functools

import jax
import jax.numpy as jnp
from jax import lax
from jax.experimental import pallas as pl
from jax.experimental.pallas import tpu as pltpu
from jax.sharding import PartitionSpec as P

F32, BF16, I32 = jnp.float32, jnp.bfloat16, jnp.int32
TN = (((0,), (0,)), ((), ()))
NN = (((1,), (0,)), ((), ()))
CAP = 64
LANES = 128


def dot(a, b, dims=NN, precision=None):
    return lax.dot_general(a, b, dims, preferred_element_type=F32, precision=precision)


def params(mib):
    return pltpu.CompilerParams(vmem_limit_bytes=mib << 20)


def as_column(row):
    size = row.shape[1]
    eye = lax.broadcasted_iota(I32, (size, size), 0) == lax.broadcasted_iota(I32, (size, size), 1)
    return jnp.where(eye, row, 0.0).sum(1, keepdims=True)


def lookup(keys, table, values, other):
    hit = keys == table
    found = jnp.where(hit, values, 0.0).sum(1, keepdims=True)
    return jnp.where(jnp.where(hit, 1.0, 0.0).sum(1, keepdims=True) > 0, found, other)


def as_row(column):
    size = column.shape[0]
    eye = lax.broadcasted_iota(I32, (size, size), 0) == lax.broadcasted_iota(I32, (size, size), 1)
    return jnp.where(eye, column, 0.0).sum(0, keepdims=True)


def slot_rows(height, me, src_ref, dst_ref):
    width = src_ref.shape[1]
    dst0, dst1 = dst_ref[0:1, :].astype(F32), dst_ref[1:2, :].astype(F32)
    lane = lax.broadcasted_iota(I32, (1, width), 1).astype(F32)
    late = as_column(lane + width)
    late = as_row(lookup(late, dst0, lane, late))
    src1 = as_column(src_ref[1:2, :].astype(F32))
    source = jnp.concatenate([as_column(src_ref[0:1, :].astype(F32)), lookup(src1, dst0, lane, src1)])
    return source, lookup(source, dst1, late, lookup(source, dst0, lane, -1.0))


def owned_first(src_ref, height):
    return src_ref[1:2, :] < height


def table_kernel(height, devices, block, place, src_ref, dst_ref, own_ref, key_ref, table_ref):
    slots = 2 * src_ref.shape[1]
    me = place[0].astype(F32)
    source, content = slot_rows(height, me, src_ref, dst_ref)
    owner = jnp.zeros_like(source)
    for d in range(1, devices):
        owner = owner + jnp.where(source >= float(d * height), 1.0, 0.0)
    own_ref[...] = jnp.where(owner == 0, 1.0, 0.0)
    lane = lax.broadcasted_iota(I32, (slots, slots), 1).astype(F32)
    line = lax.broadcasted_iota(I32, (slots, slots), 0).astype(F32)
    rank = jnp.where((owner == as_row(owner)) & (lane < line), 1.0, 0.0).sum(1, keepdims=True)
    key = as_row(jnp.where(owner > 0, owner * slots + rank, -1.0))
    first = jnp.where(owned_first(src_ref, height), 1.0, 0.0)
    key_ref[...] = jnp.concatenate([key, jnp.concatenate([first, first], 1)] * 4)
    rest = jnp.where((owner == me) & (source >= slots), source - me * height, float(height))
    order = (as_row(rest) * slots + lane < rest * slots + line).astype(F32).sum(1, keepdims=True)
    sort = order == lane
    hole = jnp.where(sort, rest, 0.0).sum(0, keepdims=True)
    slot = jnp.where(sort, jnp.where(me == 0, content, rank), 0.0).sum(0, keepdims=True)
    begin = jnp.where(rest < lane * block, 1.0, 0.0).sum(0, keepdims=True)
    most = jnp.where(owner > 0, rank + 1.0, 0.0).max(0, keepdims=True)
    most = jnp.broadcast_to(most, (1, slots))
    table_ref[...] = jnp.concatenate([hole, slot, begin, most] * 2).astype(I32)


def tables(pivot_src, pivot_dst, place, height, devices, block):
    slots = 2 * pivot_src.shape[1]
    whole = lambda i, *_: (0, 0)
    return pl.pallas_call(
        functools.partial(table_kernel, height, devices, block),
        out_shape=(
            jax.ShapeDtypeStruct((slots, 1), F32),
            jax.ShapeDtypeStruct((8, slots), F32),
            jax.ShapeDtypeStruct((8, slots), I32),
        ),
        grid_spec=pltpu.PrefetchScalarGridSpec(
            num_scalar_prefetch=1,
            grid=(1,),
            in_specs=[pl.BlockSpec(pivot_src.shape, whole), pl.BlockSpec(pivot_dst.shape, whole)],
            out_specs=(
                pl.BlockSpec((slots, 1), whole),
                pl.BlockSpec((8, slots), whole),
                pl.BlockSpec((8, slots), whole),
            ),
        ),
        compiler_params=params(24),
    )(place, pivot_src, pivot_dst)


def gather_kernel(
    height, chunk, place, src_ref, dst_ref, p_ref, a_ref, o_ref, top_ref, low_ref, spread_ref, rounds, acc_ref, extra_ref
):
    slots = 2 * src_ref.shape[1]

    @pl.when(pl.program_id(0) == 0)
    def _():
        me = place[0].astype(F32)
        source, content = slot_rows(height, me, src_ref, dst_ref)
        here = source - me * height
        wanted = jnp.where((here >= 0) & (here < height), here, jnp.where(me == 0, content, -1.0))
        column = lax.broadcasted_iota(I32, (slots, slots), 1).astype(F32)
        top_ref[...] = jnp.where(column == wanted, 1.0, 0.0).astype(BF16)
        low = wanted >= slots
        before = column < lax.broadcasted_iota(I32, (slots, slots), 0).astype(F32)
        flag = jnp.where(low, 1.0, 0.0)
        rank = dot(before.astype(F32).astype(BF16), jnp.broadcast_to(flag, (slots, LANES)).astype(BF16))[:, :1]
        rank = jnp.where(low, rank, -1.0)
        needed = flag.sum().astype(I32)
        rounds[0] = (needed + chunk - 1) // chunk

        def build(r, carry):
            spot = lax.broadcasted_iota(I32, (slots, chunk), 1).astype(F32) + (r * chunk).astype(F32)
            spread = rank == spot
            spread_ref[r] = jnp.where(spread, 1.0, 0.0).astype(BF16)
            row = jnp.where(spread, wanted, 0.0).sum(0, keepdims=True)
            row = as_column(row)
            below = lax.broadcasted_iota(I32, low_ref.shape[1:], 1).astype(F32) + float(slots)
            low_ref[r] = jnp.where(below == row, 1.0, 0.0).astype(BF16)
            return carry

        lax.fori_loop(0, rounds[0], build, 0)

        width, part = src_ref.shape[1], o_ref.shape[2]
        src1 = as_column(src_ref[1:2, :].astype(F32))
        lane = lax.broadcasted_iota(I32, (1, width), 1).astype(F32)
        here = src1 - me * height
        moving = lookup(src1, dst_ref[1:2, :].astype(F32), lane + width, -1.0)
        chosen = jnp.where((here >= 0) & (here < height), here, jnp.where(me == 0, moving, -1.0))
        row = lax.broadcasted_iota(I32, (width, height), 1).astype(F32)
        hot = jnp.where(row == chosen, 1.0, 0.0).astype(BF16)
        taken = dot(p_ref[0], hot, (((1,), (1,)), ((), ()))).astype(BF16)
        piece = taken.shape[0]
        for h in range(extra_ref.shape[0] // piece):
            have = min(part, width - h * part)
            extra_ref[h * piece : (h + 1) * piece, :have] = taken[:, h * part : h * part + have]

    acc_ref[...] = dot(top_ref[...], a_ref[:slots, :])

    def add(r, carry):
        found = dot(low_ref[r], a_ref[slots:, :]).astype(BF16)
        acc_ref[...] += dot(spread_ref[r], found)
        return carry

    lax.fori_loop(0, rounds[0], add, 0)
    part = o_ref.shape[2]
    for b in range(o_ref.shape[0]):
        o_ref[b, : acc_ref.shape[0], :] = acc_ref[:, b * part : (b + 1) * part].astype(BF16)
        o_ref[b, acc_ref.shape[0] :, :] = extra_ref[...]


def gather(slab, panels, pivot_src, pivot_dst, place, devices):
    height, cols = slab.shape
    width = pivot_src.shape[1]
    slots, part = 2 * width, cols // devices
    chunk = min(LANES, slots)
    most = slots // chunk
    many = min(4, devices)
    piece = panels.shape[1]
    extra = piece * pl.cdiv(width, part)
    return pl.pallas_call(
        functools.partial(gather_kernel, height, chunk),
        out_shape=jax.ShapeDtypeStruct((devices, slots + extra, part), BF16),
        grid_spec=pltpu.PrefetchScalarGridSpec(
            num_scalar_prefetch=1,
            grid=(devices // many,),
            in_specs=[
                pl.BlockSpec(pivot_src.shape, lambda i, *_: (0, 0)),
                pl.BlockSpec(pivot_dst.shape, lambda i, *_: (0, 0)),
                pl.BlockSpec((1, piece, height), lambda i, *_: (0, 0, 0)),
                pl.BlockSpec((height, many * part), lambda i, *_: (0, i)),
            ],
            out_specs=pl.BlockSpec((many, slots + extra, part), lambda i, *_: (i, 0, 0)),
            scratch_shapes=[
                pltpu.VMEM((slots, slots), BF16),
                pltpu.VMEM((most, chunk, height - slots), BF16),
                pltpu.VMEM((most, slots, chunk), BF16),
                pltpu.SMEM((1,), I32),
                pltpu.VMEM((slots, many * part), F32),
                pltpu.VMEM((extra, part), BF16),
            ],
        ),
        compiler_params=params(56),
        cost_estimate=pl.CostEstimate(
            flops=slots * height * cols, bytes_accessed=2 * cols * (height + slots), transcendentals=0
        ),
    )(place, pivot_src, pivot_dst, panels, slab)


def invert_kernel(base, d_ref, o_ref):
    panels, width, _ = o_ref.shape
    count = width // base
    blocks = []
    for k in range(panels):
        for b in range(count):
            at = slice(b * base, (b + 1) * base)
            blocks.append(d_ref[at, k * width + b * base : k * width + (b + 1) * base].astype(F32))
    lower = jnp.stack(blocks)
    row = lax.broadcasted_iota(I32, lower.shape, 1)
    col = lax.broadcasted_iota(I32, lower.shape, 2)
    x = jnp.where(row == col, 1.0, 0.0).astype(F32)
    for c in range(base - 1):
        x = x - lower[:, :, c : c + 1] * x[:, c : c + 1, :]
    o_ref[...] = jnp.zeros(o_ref.shape, F32)
    for k in range(panels):
        for b in range(count):
            at = slice(b * base, (b + 1) * base)
            o_ref[k, at, at] = x[k * count + b]
    size = base
    while size < width:
        for k in range(panels):
            for o in range(0, width, 2 * size):
                up, down = slice(o, o + size), slice(o + size, o + 2 * size)
                inner = dot(d_ref[down, k * width + o : k * width + o + size].astype(F32), o_ref[k, up, up], NN, lax.Precision.HIGHEST)
                o_ref[k, down, up] = -dot(o_ref[k, down, down], inner, NN, lax.Precision.HIGHEST)
        size *= 2


def invert(lower):
    width = lower.shape[0]
    return pl.pallas_call(
        functools.partial(invert_kernel, min(32, width)),
        out_shape=jax.ShapeDtypeStruct((lower.shape[1] // width, width, width), F32),
        compiler_params=params(16),
        cost_estimate=pl.CostEstimate(flops=1 << 20, bytes_accessed=1 << 18, transcendentals=0),
    )(lower)


def apply_inverse(inverse, rows):
    total = None
    for _ in range(3):
        part = inverse.astype(BF16)
        inverse = inverse - part.astype(F32)
        term = dot(part, rows)
        total = term if total is None else total + term
    return total.astype(BF16)


def solve_kernel(width, piece, inv_ref, own_ref, key_ref, r_ref, y_ref, small_ref):
    devices, _, part = r_ref.shape
    slots = 2 * width
    zero = r_ref[0, :slots, :]
    total = jnp.where(own_ref[...] > 0, zero.astype(F32), 0.0)
    for s in range(1, devices):
        total = total + r_ref[s, :slots, :].astype(F32)
    rows = total.astype(BF16)
    upper = apply_inverse(inv_ref[0], rows[:width])
    later = apply_inverse(inv_ref[1], rows[width:])
    want = lax.broadcasted_iota(I32, (devices * CAP, slots), 0)
    want = (want // CAP) * slots + want % CAP
    hot = jnp.where(want.astype(F32) == key_ref[0:1, :], 1.0, 0.0).astype(BF16)
    fill = dot(hot, zero).astype(BF16)
    for d in range(devices):
        y_ref[d, :width, :] = upper
        y_ref[d, width:slots, :] = later
        y_ref[d, slots:, :] = fill[d * CAP : (d + 1) * CAP]
    for h in range(pl.cdiv(width, part)):
        have = min(part, width - h * part)
        at = slice(slots + h * piece, slots + (h + 1) * piece)
        moving = r_ref[0, at, :have]
        picked = jnp.where(key_ref[1:2, h * part : h * part + have] > 0, moving.astype(F32), 0.0)
        for s in range(1, devices):
            picked = picked + r_ref[s, at, :have].astype(F32)
        small_ref[:, h * part : h * part + have] = picked.astype(BF16)
        small_ref[:, width + h * part : width + h * part + have] = moving


def solve(inverse, own, key, received, width, piece):
    devices, _, part = received.shape
    return pl.pallas_call(
        functools.partial(solve_kernel, width, piece),
        out_shape=(
            jax.ShapeDtypeStruct((devices, 2 * width + CAP, part), BF16),
            jax.ShapeDtypeStruct((piece, 2 * width), BF16),
        ),
        compiler_params=params(32),
        cost_estimate=pl.CostEstimate(flops=1 << 29, bytes_accessed=4 << 20, transcendentals=0),
    )(inverse, own, key, received)


def arrange_kernel(width, where, inv_ref, sel_ref, below_ref, land_ref, even_ref, odd_ref, l_ref, w_ref, moving_ref):
    shifts, panels, piece, cols = even_ref.shape
    step = pl.program_id(0)
    for s in range(shifts):
        across = lax.rem(where[1] - s + shifts, shifts)
        for k in range(panels):
            for core, ref in enumerate((even_ref, odd_ref)):
                at = pl.multiple_of(k * width + (2 * across + core) * piece, piece)
                l_ref[pl.ds(at, piece), :] = ref[s, k]

    @pl.when((step == 0) & (where[0] == 0))
    def _():
        moving_ref[...] = l_ref[:width, width : 2 * width]

    @pl.when((step == 0) & (where[0] != 0))
    def _():
        moving_ref[...] = below_ref[...]

    here = lax.broadcasted_iota(I32, (width, cols), 1) + where[0] + step * cols
    landing = jnp.where(land_ref[...] == here, 1.0, 0.0)
    moved = dot(moving_ref[...], landing.astype(BF16))
    l_ref[:width, :] = jnp.where(
        landing.sum(0, keepdims=True) > 0, moved, l_ref[:width, :].astype(F32)
    ).astype(BF16)

    @pl.when(step == 0)
    def _():
        coupling = lax.dot_general(
            inv_ref[1], sel_ref[...].astype(F32), (((1,), (1,)), ((), ())),
            preferred_element_type=F32, precision=lax.Precision.HIGHEST,
        )
        w_ref[...] = coupling


def arrange(inverse, selected, below, landing, even, odd, where):
    shifts, panels, piece, height = even.shape
    width = below.shape[0]
    cols = min(512, height)
    pieces = pl.BlockSpec((shifts, panels, piece, cols), lambda i, *_: (0, 0, 0, i))
    return pl.pallas_call(
        functools.partial(arrange_kernel, width),
        out_shape=(
            jax.ShapeDtypeStruct((panels * width, height), BF16),
            jax.ShapeDtypeStruct((width, width), F32),
        ),
        grid_spec=pltpu.PrefetchScalarGridSpec(
            num_scalar_prefetch=1,
            grid=(height // cols,),
            in_specs=[
                pl.BlockSpec(inverse.shape, lambda i, *_: (0, 0, 0)),
                pl.BlockSpec(selected.shape, lambda i, *_: (0, 0)),
                pl.BlockSpec(below.shape, lambda i, *_: (0, 0)),
                pl.BlockSpec((width, 1), lambda i, *_: (0, 0)),
                pieces,
                pieces,
            ],
            out_specs=(
                pl.BlockSpec((panels * width, cols), lambda i, *_: (0, i)),
                pl.BlockSpec((width, width), lambda i, *_: (0, 0)),
            ),
            scratch_shapes=[pltpu.VMEM((width, width), BF16)],
        ),
        compiler_params=params(32),
        cost_estimate=pl.CostEstimate(flops=1 << 24, bytes_accessed=1 << 20, transcendentals=0),
    )(where, inverse, selected, below, landing[:, None], even, odd)


def update_kernel(
    width, table, place, a_ref, l_ref, y_ref, w_ref, slab_ref, rest_ref, o_ref, u_ref, d_ref, sem
):
    step = pl.program_id(0)
    rows = a_ref.shape[0]
    devices, _, part = y_ref.shape
    more = table[2, pl.num_programs(0)] > CAP

    @pl.when(step == 0)
    def _():
        for e in range(devices):
            at = slice(e * part, (e + 1) * part)
            u_ref[:, at] = y_ref[e, : 2 * width, :]
            d_ref[:CAP, at] = y_ref[e, 2 * width :, :]
        high = w_ref[...].astype(BF16)
        rest = (w_ref[...] - high.astype(F32)).astype(BF16)
        for c in range(0, u_ref.shape[1], 512):
            at = slice(c, c + 512)
            upper = u_ref[:width, at]
            later = u_ref[width:, at].astype(F32) - (dot(high, upper) + dot(rest, upper))
            u_ref[width:, at] = later.astype(BF16)

    @pl.when((step == 0) & (place[0] == 0))
    def _():
        copy = pltpu.make_async_copy(slab_ref.at[: 2 * width], d_ref, sem)
        copy.start()
        copy.wait()

    @pl.when((step == 0) & (place[0] != 0) & more)
    def _():
        for e in range(devices):
            copy = pltpu.make_async_copy(
                rest_ref.at[e, CAP : 2 * width], d_ref.at[CAP:, e * part : (e + 1) * part], sem
            )
            copy.start()
            copy.wait()

    group = 16

    def fill(j, carry):
        to, source = table[0, j] - step * rows, table[1, j]
        taken = d_ref[pl.ds(pl.multiple_of(source // group * group, group), group), :].astype(F32)
        lane = lax.broadcasted_iota(I32, taken.shape, 0)
        row = jnp.where(lane == source % group, taken, 0.0).sum(0, keepdims=True)
        target = pl.ds(pl.multiple_of(to // group * group, group), group)
        a_ref[target, :] = jnp.where(lane == to % group, row, a_ref[target, :].astype(F32)).astype(BF16)
        return carry

    lax.fori_loop(table[2, step], table[2, step + 1], fill, 0)
    for c in range(0, o_ref.shape[1], 512):
        at = slice(c, c + 512)
        o_ref[:, at] = (a_ref[:, at].astype(F32) - dot(l_ref[...], u_ref[:, at], TN)).astype(BF16)

    @pl.when((place[0] == 0) & (step < 2 * width // rows))
    def _():
        o_ref[...] = u_ref[pl.ds(pl.multiple_of(step * rows, rows), rows), :]


def update(slab, lower, upper, coupling, rest, table, place, rows):
    height, cols = slab.shape
    width = lower.shape[0] // 2
    return pl.pallas_call(
        functools.partial(update_kernel, width),
        out_shape=jax.ShapeDtypeStruct(slab.shape, BF16),
        grid_spec=pltpu.PrefetchScalarGridSpec(
            num_scalar_prefetch=2,
            grid=(height // rows,),
            in_specs=[
                pl.BlockSpec((rows, cols), lambda i, *_: (i, 0)),
                pl.BlockSpec((2 * width, rows), lambda i, *_: (0, i)),
                pl.BlockSpec(memory_space=pltpu.VMEM),
                pl.BlockSpec(memory_space=pltpu.VMEM),
                pl.BlockSpec(memory_space=pl.ANY),
                pl.BlockSpec(memory_space=pl.ANY),
            ],
            out_specs=pl.BlockSpec((rows, cols), lambda i, *_: (i, 0)),
            scratch_shapes=[
                pltpu.VMEM((2 * width, cols), BF16),
                pltpu.VMEM((2 * width, cols), BF16),
                pltpu.SemaphoreType.DMA,
            ],
        ),
        compiler_params=params(54),
        cost_estimate=pl.CostEstimate(
            flops=4 * height * cols * width, bytes_accessed=4 * height * cols, transcendentals=0
        ),
    )(table, place, slab, lower, upper, coupling, slab, rest)


def exchange(x):
    return lax.all_to_all(x, "row", 0, 0)


def per_device(trailing, panels, diag_lower, pivot_src, pivot_dst):
    height, cols = trailing.shape
    width = diag_lower.shape[2]
    slots = 2 * width
    devices = lax.axis_size("row")
    place = lax.axis_index("row").astype(I32)
    offset = place * height
    received = gather(trailing, panels, pivot_src, pivot_dst, place[None], devices)
    received, diag_lower = lax.optimization_barrier((received, diag_lower))
    received = exchange(received)
    diagonal = lax.all_gather(
        jnp.concatenate([diag_lower[0], diag_lower[1]], axis=1), "col", axis=0, tiled=True
    )
    diagonal, panels, pivot_src, pivot_dst = lax.optimization_barrier(
        (diagonal, panels, pivot_src, pivot_dst)
    )
    inverse = invert(diagonal)
    own, key, table = tables(pivot_src, pivot_dst, place[None], height, devices, slots)

    sent, small = solve(inverse, own, key, received, width, panels.shape[1])

    small = lax.all_gather(small, "col", axis=0, tiled=True)

    columns = lax.axis_size("col")
    chips = columns // 2
    across, core = lax.axis_index("col") // 2, lax.axis_index("col") % 2
    pieces = [panels]
    for s in range(1, chips):
        pieces.append(lax.ppermute(panels, "col", [(i, (i + 2 * s) % columns) for i in range(columns)]))
    pieces = lax.optimization_barrier((pieces, small))[0]
    mine = jnp.stack(pieces)
    other = lax.ppermute(mine, "col", [(i, i ^ 1) for i in range(columns)])
    even, odd = jnp.where(core == 0, mine, other), jnp.where(core == 0, other, mine)

    selected, below = small[:, :width], small[:, width:slots]
    lower, coupling = arrange(
        inverse, selected, below, jnp.where(place == 0, pivot_dst[1], pivot_src[1]), even, odd, jnp.stack([offset, across]).astype(I32)
    )

    fills = received[0, :slots]
    rounds = (table[3, 0] + CAP - 1) // CAP

    def fetch(state):
        r, found = state
        want = jnp.arange(devices * CAP, dtype=I32)
        want = want // CAP * slots + want % CAP + r * CAP
        part = dot((want[:, None] == key[:1].astype(I32)).astype(BF16), fills).astype(BF16)
        part = exchange(part.reshape(devices, CAP, -1))
        return r + 1, lax.dynamic_update_slice(found, part, (0, r * CAP, 0))

    found = lax.while_loop(lambda state: state[0] < rounds, fetch, (jnp.ones((), I32), received))[1]

    return update(trailing, lower, exchange(sent), coupling, found, table, place[None], slots)


def solution(mesh):
    placed = (P("row", "col"), P(None, "col", "row"), P(None, "col", None), P(), P())
    return jax.shard_map(
        per_device, mesh=mesh, in_specs=placed, out_specs=P("row", "col"), check_vma=False
    )
```

```python
import functools

import jax
import jax.numpy as jnp
from jax import lax
from jax.experimental import pallas as pl
from jax.experimental.pallas import tpu as pltpu
from jax.sharding import PartitionSpec as P

F32, BF16, I32 = jnp.float32, jnp.bfloat16, jnp.int32
TN = (((0,), (0,)), ((), ()))
NN = (((1,), (0,)), ((), ()))
CAP = 64
LANES = 128


def dot(a, b, dims=NN, precision=None):
    return lax.dot_general(a, b, dims, preferred_element_type=F32, precision=precision)


def params(mib):
    return pltpu.CompilerParams(vmem_limit_bytes=mib << 20)


def as_column(row):
    size = row.shape[1]
    eye = lax.broadcasted_iota(I32, (size, size), 0) == lax.broadcasted_iota(I32, (size, size), 1)
    return jnp.where(eye, row, 0.0).sum(1, keepdims=True)


def lookup(keys, table, values, other):
    hit = keys == table
    found = jnp.where(hit, values, 0.0).sum(1, keepdims=True)
    return jnp.where(jnp.where(hit, 1.0, 0.0).sum(1, keepdims=True) > 0, found, other)


def as_row(column):
    size = column.shape[0]
    eye = lax.broadcasted_iota(I32, (size, size), 0) == lax.broadcasted_iota(I32, (size, size), 1)
    return jnp.where(eye, column, 0.0).sum(0, keepdims=True)


def slot_rows(height, me, src_ref, dst_ref):
    width = src_ref.shape[1]
    dst0, dst1 = dst_ref[0:1, :].astype(F32), dst_ref[1:2, :].astype(F32)
    lane = lax.broadcasted_iota(I32, (1, width), 1).astype(F32)
    late = as_column(lane + width)
    late = as_row(lookup(late, dst0, lane, late))
    src1 = as_column(src_ref[1:2, :].astype(F32))
    source = jnp.concatenate([as_column(src_ref[0:1, :].astype(F32)), lookup(src1, dst0, lane, src1)])
    return source, lookup(source, dst1, late, lookup(source, dst0, lane, -1.0))


def owned_first(src_ref, height):
    return src_ref[1:2, :] < height


def table_kernel(height, devices, block, place, src_ref, dst_ref, own_ref, key_ref, table_ref):
    slots = 2 * src_ref.shape[1]
    me = place[0].astype(F32)
    source, content = slot_rows(height, me, src_ref, dst_ref)
    owner = jnp.zeros_like(source)
    for d in range(1, devices):
        owner = owner + jnp.where(source >= float(d * height), 1.0, 0.0)
    own_ref[...] = jnp.where(owner == 0, 1.0, 0.0)
    lane = lax.broadcasted_iota(I32, (slots, slots), 1).astype(F32)
    line = lax.broadcasted_iota(I32, (slots, slots), 0).astype(F32)
    rank = jnp.where((owner == as_row(owner)) & (lane < line), 1.0, 0.0).sum(1, keepdims=True)
    key = as_row(jnp.where(owner > 0, owner * slots + rank, -1.0))
    first = jnp.where(owned_first(src_ref, height), 1.0, 0.0)
    key_ref[...] = jnp.concatenate([key, jnp.concatenate([first, first], 1)] * 4)
    rest = jnp.where((owner == me) & (source >= slots), source - me * height, float(height))
    order = (as_row(rest) * slots + lane < rest * slots + line).astype(F32).sum(1, keepdims=True)
    sort = order == lane
    hole = jnp.where(sort, rest, 0.0).sum(0, keepdims=True)
    slot = jnp.where(sort, jnp.where(me == 0, content, rank), 0.0).sum(0, keepdims=True)
    begin = jnp.where(rest < lane * block, 1.0, 0.0).sum(0, keepdims=True)
    most = jnp.where(owner > 0, rank + 1.0, 0.0).max(0, keepdims=True)
    most = jnp.broadcast_to(most, (1, slots))
    table_ref[...] = jnp.concatenate([hole, slot, begin, most] * 2).astype(I32)


def tables(pivot_src, pivot_dst, place, height, devices, block):
    slots = 2 * pivot_src.shape[1]
    whole = lambda i, *_: (0, 0)
    return pl.pallas_call(
        functools.partial(table_kernel, height, devices, block),
        out_shape=(
            jax.ShapeDtypeStruct((slots, 1), F32),
            jax.ShapeDtypeStruct((8, slots), F32),
            jax.ShapeDtypeStruct((8, slots), I32),
        ),
        grid_spec=pltpu.PrefetchScalarGridSpec(
            num_scalar_prefetch=1,
            grid=(1,),
            in_specs=[pl.BlockSpec(pivot_src.shape, whole), pl.BlockSpec(pivot_dst.shape, whole)],
            out_specs=(
                pl.BlockSpec((slots, 1), whole),
                pl.BlockSpec((8, slots), whole),
                pl.BlockSpec((8, slots), whole),
            ),
        ),
        compiler_params=params(24),
    )(place, pivot_src, pivot_dst)


def gather_kernel(
    height, chunk, place, src_ref, dst_ref, p_ref, slab_ref, o_ref, a_ref, top_ref, low_ref, spread_ref, acc_ref, extra_ref, sems
):
    width = src_ref.shape[1]
    slots = 2 * width
    tiles, _, cols = a_ref.shape
    part = o_ref.shape[2]
    copies = [
        pltpu.make_async_copy(slab_ref.at[:, t * cols : (t + 1) * cols], a_ref.at[t], sems.at[t]) for t in range(tiles)
    ]
    for copy in copies:
        copy.start()

    me = place[0].astype(F32)
    source, content = slot_rows(height, me, src_ref, dst_ref)
    here = source - me * height
    wanted = jnp.where((here >= 0) & (here < height), here, jnp.where(me == 0, content, -1.0))
    column = lax.broadcasted_iota(I32, (slots, slots), 1).astype(F32)
    top_ref[...] = jnp.where(column == wanted, 1.0, 0.0).astype(BF16)
    low = wanted >= slots
    before = jnp.where(column < lax.broadcasted_iota(I32, (slots, slots), 0).astype(F32), 1.0, 0.0)
    flag = jnp.where(low, 1.0, 0.0)
    rank = dot(before.astype(BF16), jnp.broadcast_to(flag, (slots, LANES)).astype(BF16))[:, :1]
    rank = jnp.where(low, rank, -1.0)
    rounds = (flag.sum().astype(I32) + chunk - 1) // chunk

    def build(r, carry):
        spot = lax.broadcasted_iota(I32, (slots, chunk), 1).astype(F32) + (r * chunk).astype(F32)
        spread = rank == spot
        spread_ref[r] = jnp.where(spread, 1.0, 0.0).astype(BF16)
        row = as_column(jnp.where(spread, wanted, 0.0).sum(0, keepdims=True))
        below = lax.broadcasted_iota(I32, low_ref.shape[1:], 1).astype(F32) + float(slots)
        low_ref[r] = jnp.where(below == row, 1.0, 0.0).astype(BF16)
        return carry

    lax.fori_loop(0, rounds, build, 0)

    src1 = as_column(src_ref[1:2, :].astype(F32))
    lane = lax.broadcasted_iota(I32, (1, width), 1).astype(F32)
    here = src1 - me * height
    moving = lookup(src1, dst_ref[1:2, :].astype(F32), lane + width, -1.0)
    chosen = jnp.where((here >= 0) & (here < height), here, jnp.where(me == 0, moving, -1.0))
    row = lax.broadcasted_iota(I32, (width, height), 1).astype(F32)
    hot = jnp.where(row == chosen, 1.0, 0.0).astype(BF16)
    taken = dot(p_ref[0], hot, (((1,), (1,)), ((), ()))).astype(BF16)
    piece = taken.shape[0]
    for h in range(extra_ref.shape[0] // piece):
        have = min(part, width - h * part)
        extra_ref[h * piece : (h + 1) * piece, :have] = taken[:, h * part : h * part + have]

    for t in range(tiles):
        copies[t].wait()
        acc_ref[...] = dot(top_ref[...], a_ref[t, :slots, :])

        def add(r, carry, t=t):
            found = dot(low_ref[r], a_ref[t, slots:, :]).astype(BF16)
            acc_ref[...] += dot(spread_ref[r], found)
            return carry

        lax.fori_loop(0, rounds, add, 0)
        for b in range(cols // part):
            o_ref[t * (cols // part) + b, :slots, :] = acc_ref[:, b * part : (b + 1) * part].astype(BF16)
            o_ref[t * (cols // part) + b, slots:, :] = extra_ref[...]


def gather(slab, panels, pivot_src, pivot_dst, place, devices):
    height, cols = slab.shape
    width = pivot_src.shape[1]
    slots, part = 2 * width, cols // devices
    chunk = min(LANES, slots)
    most = slots // chunk
    tiles = 4
    piece = panels.shape[1]
    extra = piece * pl.cdiv(width, part)
    return pl.pallas_call(
        functools.partial(gather_kernel, height, chunk),
        out_shape=jax.ShapeDtypeStruct((devices, slots + extra, part), BF16),
        grid_spec=pltpu.PrefetchScalarGridSpec(
            num_scalar_prefetch=1,
            grid=(1,),
            in_specs=[
                pl.BlockSpec(pivot_src.shape, lambda i, *_: (0, 0)),
                pl.BlockSpec(pivot_dst.shape, lambda i, *_: (0, 0)),
                pl.BlockSpec((1, piece, height), lambda i, *_: (0, 0, 0)),
                pl.BlockSpec(memory_space=pl.ANY),
            ],
            out_specs=pl.BlockSpec((devices, slots + extra, part), lambda i, *_: (0, 0, 0)),
            scratch_shapes=[
                pltpu.VMEM((tiles, height, cols // tiles), BF16),
                pltpu.VMEM((slots, slots), BF16),
                pltpu.VMEM((most, chunk, height - slots), BF16),
                pltpu.VMEM((most, slots, chunk), BF16),
                pltpu.VMEM((slots, cols // tiles), F32),
                pltpu.VMEM((extra, part), BF16),
                pltpu.SemaphoreType.DMA((tiles,)),
            ],
        ),
        compiler_params=params(58),
        cost_estimate=pl.CostEstimate(
            flops=slots * height * cols, bytes_accessed=2 * cols * (height + slots), transcendentals=0
        ),
    )(place, pivot_src, pivot_dst, panels, slab)


def invert_kernel(base, d_ref, o_ref):
    panels, width, _ = o_ref.shape
    count = width // base
    blocks = []
    for k in range(panels):
        for b in range(count):
            at = slice(b * base, (b + 1) * base)
            blocks.append(d_ref[at, k * width + b * base : k * width + (b + 1) * base].astype(F32))
    lower = jnp.stack(blocks)
    row = lax.broadcasted_iota(I32, lower.shape, 1)
    col = lax.broadcasted_iota(I32, lower.shape, 2)
    x = jnp.where(row == col, 1.0, 0.0).astype(F32)
    for c in range(base - 1):
        x = x - lower[:, :, c : c + 1] * x[:, c : c + 1, :]
    o_ref[...] = jnp.zeros(o_ref.shape, F32)
    for k in range(panels):
        for b in range(count):
            at = slice(b * base, (b + 1) * base)
            o_ref[k, at, at] = x[k * count + b]
    size = base
    while size < width:
        for k in range(panels):
            for o in range(0, width, 2 * size):
                up, down = slice(o, o + size), slice(o + size, o + 2 * size)
                inner = dot(d_ref[down, k * width + o : k * width + o + size].astype(F32), o_ref[k, up, up], NN, lax.Precision.HIGHEST)
                o_ref[k, down, up] = -dot(o_ref[k, down, down], inner, NN, lax.Precision.HIGHEST)
        size *= 2


def invert(lower):
    width = lower.shape[0]
    return pl.pallas_call(
        functools.partial(invert_kernel, min(32, width)),
        out_shape=jax.ShapeDtypeStruct((lower.shape[1] // width, width, width), F32),
        compiler_params=params(16),
        cost_estimate=pl.CostEstimate(flops=1 << 20, bytes_accessed=1 << 18, transcendentals=0),
    )(lower)


def apply_inverse(inverse, rows):
    total = None
    for _ in range(3):
        part = inverse.astype(BF16)
        inverse = inverse - part.astype(F32)
        term = dot(part, rows)
        total = term if total is None else total + term
    return total.astype(BF16)


def solve_kernel(width, piece, inv_ref, own_ref, key_ref, r_ref, y_ref, small_ref):
    devices, _, part = r_ref.shape
    slots = 2 * width
    zero = r_ref[0, :slots, :]
    total = jnp.where(own_ref[...] > 0, zero.astype(F32), 0.0)
    for s in range(1, devices):
        total = total + r_ref[s, :slots, :].astype(F32)
    rows = total.astype(BF16)
    upper = apply_inverse(inv_ref[0], rows[:width])
    later = apply_inverse(inv_ref[1], rows[width:])
    want = lax.broadcasted_iota(I32, (devices * CAP, slots), 0)
    want = (want // CAP) * slots + want % CAP
    hot = jnp.where(want.astype(F32) == key_ref[0:1, :], 1.0, 0.0).astype(BF16)
    fill = dot(hot, zero).astype(BF16)
    for d in range(devices):
        y_ref[d, :width, :] = upper
        y_ref[d, width:slots, :] = later
        y_ref[d, slots:, :] = fill[d * CAP : (d + 1) * CAP]
    for h in range(pl.cdiv(width, part)):
        have = min(part, width - h * part)
        at = slice(slots + h * piece, slots + (h + 1) * piece)
        moving = r_ref[0, at, :have]
        picked = jnp.where(key_ref[1:2, h * part : h * part + have] > 0, moving.astype(F32), 0.0)
        for s in range(1, devices):
            picked = picked + r_ref[s, at, :have].astype(F32)
        small_ref[:, h * part : h * part + have] = picked.astype(BF16)
        small_ref[:, width + h * part : width + h * part + have] = moving


def solve(inverse, own, key, received, width, piece):
    devices, _, part = received.shape
    return pl.pallas_call(
        functools.partial(solve_kernel, width, piece),
        out_shape=(
            jax.ShapeDtypeStruct((devices, 2 * width + CAP, part), BF16),
            jax.ShapeDtypeStruct((piece, 2 * width), BF16),
        ),
        compiler_params=params(32),
        cost_estimate=pl.CostEstimate(flops=1 << 29, bytes_accessed=4 << 20, transcendentals=0),
    )(inverse, own, key, received)


def arrange_kernel(width, where, inv_ref, sel_ref, below_ref, land_ref, *refs):
    *piece_refs, l_ref, w_ref, moving_ref = refs
    chips = len(piece_refs) // 2
    panels, piece, cols = piece_refs[0].shape
    step = pl.program_id(0)
    for i, ref in enumerate(piece_refs):
        across = lax.rem(where[1] - i % chips + chips, chips)
        column = 2 * across + lax.rem(where[2] + i // chips, 2)
        for k in range(panels):
            at = pl.multiple_of(k * width + column * piece, piece)
            l_ref[pl.ds(at, piece), :] = ref[k]

    @pl.when((step == 0) & (where[0] == 0))
    def _():
        moving_ref[...] = l_ref[:width, width : 2 * width]

    @pl.when((step == 0) & (where[0] != 0))
    def _():
        moving_ref[...] = below_ref[...]

    here = lax.broadcasted_iota(I32, (width, cols), 1) + where[0] + step * cols
    landing = jnp.where(land_ref[...] == here, 1.0, 0.0)
    moved = dot(moving_ref[...], landing.astype(BF16))
    l_ref[:width, :] = jnp.where(
        landing.sum(0, keepdims=True) > 0, moved, l_ref[:width, :].astype(F32)
    ).astype(BF16)

    @pl.when(step == 0)
    def _():
        coupling = lax.dot_general(
            inv_ref[1], sel_ref[...].astype(F32), (((1,), (1,)), ((), ())),
            preferred_element_type=F32, precision=lax.Precision.HIGHEST,
        )
        w_ref[...] = coupling


def arrange(inverse, selected, below, landing, parts, where):
    panels, piece, height = parts[0].shape
    width = below.shape[0]
    cols = min(512, height)
    pieces = pl.BlockSpec((panels, piece, cols), lambda i, *_: (0, 0, i))
    return pl.pallas_call(
        functools.partial(arrange_kernel, width),
        out_shape=(
            jax.ShapeDtypeStruct((panels * width, height), BF16),
            jax.ShapeDtypeStruct((width, width), F32),
        ),
        grid_spec=pltpu.PrefetchScalarGridSpec(
            num_scalar_prefetch=1,
            grid=(height // cols,),
            in_specs=[
                pl.BlockSpec(inverse.shape, lambda i, *_: (0, 0, 0)),
                pl.BlockSpec(selected.shape, lambda i, *_: (0, 0)),
                pl.BlockSpec(below.shape, lambda i, *_: (0, 0)),
                pl.BlockSpec((width, 1), lambda i, *_: (0, 0)),
            ]
            + [pieces] * len(parts),
            out_specs=(
                pl.BlockSpec((panels * width, cols), lambda i, *_: (0, i)),
                pl.BlockSpec((width, width), lambda i, *_: (0, 0)),
            ),
            scratch_shapes=[pltpu.VMEM((width, width), BF16)],
        ),
        compiler_params=params(32),
        cost_estimate=pl.CostEstimate(flops=1 << 24, bytes_accessed=1 << 20, transcendentals=0),
    )(where, inverse, selected, below, landing[:, None], *parts)


def update_kernel(
    width, table, place, a_ref, l_ref, y_ref, w_ref, slab_ref, rest_ref, o_ref, u_ref, d_ref, sem
):
    step = pl.program_id(0)
    rows = a_ref.shape[0]
    devices, _, part = y_ref.shape
    more = table[2, pl.num_programs(0)] > CAP

    @pl.when(step == 0)
    def _():
        for e in range(devices):
            at = slice(e * part, (e + 1) * part)
            u_ref[:, at] = y_ref[e, : 2 * width, :]
            d_ref[:CAP, at] = y_ref[e, 2 * width :, :]
        high = w_ref[...].astype(BF16)
        rest = (w_ref[...] - high.astype(F32)).astype(BF16)
        for c in range(0, u_ref.shape[1], 512):
            at = slice(c, c + 512)
            upper = u_ref[:width, at]
            later = u_ref[width:, at].astype(F32) - (dot(high, upper) + dot(rest, upper))
            u_ref[width:, at] = later.astype(BF16)

    @pl.when((step == 0) & (place[0] == 0))
    def _():
        copy = pltpu.make_async_copy(slab_ref.at[: 2 * width], d_ref, sem)
        copy.start()
        copy.wait()

    @pl.when((step == 0) & (place[0] != 0) & more)
    def _():
        for e in range(devices):
            copy = pltpu.make_async_copy(
                rest_ref.at[e, CAP : 2 * width], d_ref.at[CAP:, e * part : (e + 1) * part], sem
            )
            copy.start()
            copy.wait()

    group = 16

    def fill(j, carry):
        to, source = table[0, j] - step * rows, table[1, j]
        taken = d_ref[pl.ds(pl.multiple_of(source // group * group, group), group), :].astype(F32)
        lane = lax.broadcasted_iota(I32, taken.shape, 0)
        row = jnp.where(lane == source % group, taken, 0.0).sum(0, keepdims=True)
        target = pl.ds(pl.multiple_of(to // group * group, group), group)
        a_ref[target, :] = jnp.where(lane == to % group, row, a_ref[target, :].astype(F32)).astype(BF16)
        return carry

    lax.fori_loop(table[2, step], table[2, step + 1], fill, 0)
    for c in range(0, o_ref.shape[1], 512):
        at = slice(c, c + 512)
        o_ref[:, at] = (a_ref[:, at].astype(F32) - dot(l_ref[...], u_ref[:, at], TN)).astype(BF16)

    @pl.when((place[0] == 0) & (step < 2 * width // rows))
    def _():
        o_ref[...] = u_ref[pl.ds(pl.multiple_of(step * rows, rows), rows), :]


def update(slab, lower, upper, coupling, rest, table, place, rows):
    height, cols = slab.shape
    width = lower.shape[0] // 2
    return pl.pallas_call(
        functools.partial(update_kernel, width),
        out_shape=jax.ShapeDtypeStruct(slab.shape, BF16),
        grid_spec=pltpu.PrefetchScalarGridSpec(
            num_scalar_prefetch=2,
            grid=(height // rows,),
            in_specs=[
                pl.BlockSpec((rows, cols), lambda i, *_: (i, 0)),
                pl.BlockSpec((2 * width, rows), lambda i, *_: (0, i)),
                pl.BlockSpec(memory_space=pltpu.VMEM),
                pl.BlockSpec(memory_space=pltpu.VMEM),
                pl.BlockSpec(memory_space=pl.ANY),
                pl.BlockSpec(memory_space=pl.ANY),
            ],
            out_specs=pl.BlockSpec((rows, cols), lambda i, *_: (i, 0)),
            scratch_shapes=[
                pltpu.VMEM((2 * width, cols), BF16),
                pltpu.VMEM((2 * width, cols), BF16),
                pltpu.SemaphoreType.DMA,
            ],
        ),
        compiler_params=params(54),
        cost_estimate=pl.CostEstimate(
            flops=4 * height * cols * width, bytes_accessed=4 * height * cols, transcendentals=0
        ),
    )(table, place, slab, lower, upper, coupling, slab, rest)


def exchange(x):
    return lax.all_to_all(x, "row", 0, 0)


def per_device(trailing, panels, diag_lower, pivot_src, pivot_dst):
    height, cols = trailing.shape
    width = diag_lower.shape[2]
    slots = 2 * width
    devices = lax.axis_size("row")
    place = lax.axis_index("row").astype(I32)
    offset = place * height
    received = gather(trailing, panels, pivot_src, pivot_dst, place[None], devices)
    received, diag_lower, panels = lax.optimization_barrier((received, diag_lower, panels))
    received = exchange(received)

    columns = lax.axis_size("col")
    chips = columns // 2
    across, core = lax.axis_index("col") // 2, lax.axis_index("col") % 2
    parts = [panels]
    for s in range(1, chips):
        parts.append(lax.ppermute(panels, "col", [(d, (d + 2 * s) % columns) for d in range(columns)]))
    diagonal = lax.all_gather(
        jnp.concatenate([diag_lower[0], diag_lower[1]], axis=1), "col", axis=0, tiled=True
    )
    diagonal, pivot_src, pivot_dst = lax.optimization_barrier((diagonal, pivot_src, pivot_dst))
    inverse = invert(diagonal)
    own, key, table = tables(pivot_src, pivot_dst, place[None], height, devices, slots)

    received, parts = lax.optimization_barrier((received, parts))
    sent, small = solve(inverse, own, key, received, width, panels.shape[1])

    small = lax.all_gather(small, "col", axis=0, tiled=True)

    parts = parts + [lax.ppermute(part, "col", [(d, d ^ 1) for d in range(columns)]) for part in parts]

    selected, below = small[:, :width], small[:, width:slots]
    lower, coupling = arrange(
        inverse,
        selected,
        below,
        jnp.where(place == 0, pivot_dst[1], pivot_src[1]),
        parts,
        jnp.stack([offset, across, core]).astype(I32),
    )

    fills = received[0, :slots]
    rounds = (table[3, 0] + CAP - 1) // CAP

    def fetch(state):
        r, found = state
        want = jnp.arange(devices * CAP, dtype=I32)
        want = want // CAP * slots + want % CAP + r * CAP
        part = dot((want[:, None] == key[:1].astype(I32)).astype(BF16), fills).astype(BF16)
        part = exchange(part.reshape(devices, CAP, -1))
        return r + 1, lax.dynamic_update_slice(found, part, (0, r * CAP, 0))

    found = lax.while_loop(lambda state: state[0] < rounds, fetch, (jnp.ones((), I32), received))[1]

    return update(trailing, lower, exchange(sent), coupling, found, table, place[None], slots)


def solution(mesh):
    placed = (P("row", "col"), P(None, "col", "row"), P(None, "col", None), P(), P())
    return jax.shard_map(
        per_device, mesh=mesh, in_specs=placed, out_specs=P("row", "col"), check_vma=False
    )
```

```python
import functools

import jax
import jax.numpy as jnp
from jax import lax
from jax.experimental import pallas as pl
from jax.experimental.pallas import tpu as pltpu
from jax.sharding import PartitionSpec as P

F32, BF16, I32 = jnp.float32, jnp.bfloat16, jnp.int32
TN = (((0,), (0,)), ((), ()))
NN = (((1,), (0,)), ((), ()))
CAP = 64
LANES = 128


def dot(a, b, dims=NN, precision=None):
    return lax.dot_general(a, b, dims, preferred_element_type=F32, precision=precision)


def params(mib):
    return pltpu.CompilerParams(vmem_limit_bytes=mib << 20)


def as_column(row):
    size = row.shape[1]
    eye = lax.broadcasted_iota(I32, (size, size), 0) == lax.broadcasted_iota(I32, (size, size), 1)
    return jnp.where(eye, row, 0.0).sum(1, keepdims=True)


def lookup(keys, table, values, other):
    hit = keys == table
    found = jnp.where(hit, values, 0.0).sum(1, keepdims=True)
    return jnp.where(jnp.where(hit, 1.0, 0.0).sum(1, keepdims=True) > 0, found, other)


def as_row(column):
    size = column.shape[0]
    eye = lax.broadcasted_iota(I32, (size, size), 0) == lax.broadcasted_iota(I32, (size, size), 1)
    return jnp.where(eye, column, 0.0).sum(0, keepdims=True)


def slot_rows(height, me, src_ref, dst_ref):
    width = src_ref.shape[1]
    dst0, dst1 = dst_ref[0:1, :].astype(F32), dst_ref[1:2, :].astype(F32)
    lane = lax.broadcasted_iota(I32, (1, width), 1).astype(F32)
    late = as_column(lane + width)
    late = as_row(lookup(late, dst0, lane, late))
    src1 = as_column(src_ref[1:2, :].astype(F32))
    source = jnp.concatenate([as_column(src_ref[0:1, :].astype(F32)), lookup(src1, dst0, lane, src1)])
    return source, lookup(source, dst1, late, lookup(source, dst0, lane, -1.0))


def owned_first(src_ref, height):
    return src_ref[1:2, :] < height


def table_kernel(height, devices, block, place, src_ref, dst_ref, own_ref, key_ref, table_ref):
    slots = 2 * src_ref.shape[1]
    me = place[0].astype(F32)
    source, content = slot_rows(height, me, src_ref, dst_ref)
    owner = jnp.zeros_like(source)
    for d in range(1, devices):
        owner = owner + jnp.where(source >= float(d * height), 1.0, 0.0)
    own_ref[...] = jnp.where(owner == 0, 1.0, 0.0)
    lane = lax.broadcasted_iota(I32, (slots, slots), 1).astype(F32)
    line = lax.broadcasted_iota(I32, (slots, slots), 0).astype(F32)
    rank = jnp.where((owner == as_row(owner)) & (lane < line), 1.0, 0.0).sum(1, keepdims=True)
    key = as_row(jnp.where(owner > 0, owner * slots + rank, -1.0))
    first = jnp.where(owned_first(src_ref, height), 1.0, 0.0)
    key_ref[...] = jnp.concatenate([key, jnp.concatenate([first, first], 1)] * 4)
    rest = jnp.where((owner == me) & (source >= slots), source - me * height, float(height))
    order = (as_row(rest) * slots + lane < rest * slots + line).astype(F32).sum(1, keepdims=True)
    sort = order == lane
    hole = jnp.where(sort, rest, 0.0).sum(0, keepdims=True)
    slot = jnp.where(sort, jnp.where(me == 0, content, rank), 0.0).sum(0, keepdims=True)
    begin = jnp.where(rest < lane * block, 1.0, 0.0).sum(0, keepdims=True)
    most = jnp.where(owner > 0, rank + 1.0, 0.0).max(0, keepdims=True)
    most = jnp.broadcast_to(most, (1, slots))
    table_ref[...] = jnp.concatenate([hole, slot, begin, most] * 2).astype(I32)


def tables(pivot_src, pivot_dst, place, height, devices, block):
    slots = 2 * pivot_src.shape[1]
    whole = lambda i, *_: (0, 0)
    return pl.pallas_call(
        functools.partial(table_kernel, height, devices, block),
        out_shape=(
            jax.ShapeDtypeStruct((slots, 1), F32),
            jax.ShapeDtypeStruct((8, slots), F32),
            jax.ShapeDtypeStruct((8, slots), I32),
        ),
        grid_spec=pltpu.PrefetchScalarGridSpec(
            num_scalar_prefetch=1,
            grid=(1,),
            in_specs=[pl.BlockSpec(pivot_src.shape, whole), pl.BlockSpec(pivot_dst.shape, whole)],
            out_specs=(
                pl.BlockSpec((slots, 1), whole),
                pl.BlockSpec((8, slots), whole),
                pl.BlockSpec((8, slots), whole),
            ),
        ),
        compiler_params=params(24),
    )(place, pivot_src, pivot_dst)


def gather_kernel(
    height, chunk, tiles, place, src_ref, dst_ref, p_ref, slab_ref, o_ref, a_ref, top_ref, low_ref, spread_ref, acc_ref, extra_ref, sems
):
    width = src_ref.shape[1]
    slots = 2 * width
    cols = a_ref.shape[1] // tiles
    part = o_ref.shape[2]
    tile = [slice(t * cols, (t + 1) * cols) for t in range(tiles)]
    copies = [pltpu.make_async_copy(slab_ref.at[:, at], a_ref.at[:, at], sems.at[t]) for t, at in enumerate(tile)]
    for copy in copies[:2]:
        copy.start()

    me = place[0].astype(F32)
    source, content = slot_rows(height, me, src_ref, dst_ref)
    here = source - me * height
    wanted = jnp.where((here >= 0) & (here < height), here, jnp.where(me == 0, content, -1.0))
    column = lax.broadcasted_iota(I32, (slots, slots), 1).astype(F32)
    top_ref[...] = jnp.where(column == wanted, 1.0, 0.0).astype(BF16)
    low = wanted >= slots
    before = jnp.where(column < lax.broadcasted_iota(I32, (slots, slots), 0).astype(F32), 1.0, 0.0)
    flag = jnp.where(low, 1.0, 0.0)
    rank = dot(before.astype(BF16), jnp.broadcast_to(flag, (slots, LANES)).astype(BF16))[:, :1]
    rank = jnp.where(low, rank, -1.0)
    rounds = (flag.sum().astype(I32) + chunk - 1) // chunk

    def build(r, carry):
        spot = lax.broadcasted_iota(I32, (slots, chunk), 1).astype(F32) + (r * chunk).astype(F32)
        spread = rank == spot
        spread_ref[r] = jnp.where(spread, 1.0, 0.0).astype(BF16)
        row = as_column(jnp.where(spread, wanted, 0.0).sum(0, keepdims=True))
        below = lax.broadcasted_iota(I32, low_ref.shape[1:], 1).astype(F32) + float(slots)
        low_ref[r] = jnp.where(below == row, 1.0, 0.0).astype(BF16)
        return carry

    lax.fori_loop(0, rounds, build, 0)

    src1 = as_column(src_ref[1:2, :].astype(F32))
    lane = lax.broadcasted_iota(I32, (1, width), 1).astype(F32)
    here = src1 - me * height
    moving = lookup(src1, dst_ref[1:2, :].astype(F32), lane + width, -1.0)
    chosen = jnp.where((here >= 0) & (here < height), here, jnp.where(me == 0, moving, -1.0))
    row = lax.broadcasted_iota(I32, (width, height), 1).astype(F32)
    hot = jnp.where(row == chosen, 1.0, 0.0).astype(BF16)
    taken = dot(p_ref[0], hot, (((1,), (1,)), ((), ()))).astype(BF16)
    piece = taken.shape[0]
    for h in range(extra_ref.shape[0] // piece):
        have = min(part, width - h * part)
        extra_ref[h * piece : (h + 1) * piece, :have] = taken[:, h * part : h * part + have]

    for t in range(tiles):
        copies[t].wait()
        if t + 2 < tiles:
            copies[t + 2].start()
        at = tile[t]
        acc_ref[...] = dot(top_ref[...], a_ref[:slots, at])

        def add(r, carry, at=at):
            found = dot(low_ref[r], a_ref[slots:, at]).astype(BF16)
            acc_ref[...] += dot(spread_ref[r], found)
            return carry

        lax.fori_loop(0, rounds, add, 0)
        for b in range(cols // part):
            o_ref[t * (cols // part) + b, :slots, :] = acc_ref[:, b * part : (b + 1) * part].astype(BF16)
            o_ref[t * (cols // part) + b, slots:, :] = extra_ref[...]


def gather(slab, panels, pivot_src, pivot_dst, place, devices):
    height, cols = slab.shape
    width = pivot_src.shape[1]
    slots, part = 2 * width, cols // devices
    chunk = min(LANES, slots)
    most = slots // chunk
    tiles = min(4, devices)
    piece = panels.shape[1]
    extra = piece * pl.cdiv(width, part)
    return pl.pallas_call(
        functools.partial(gather_kernel, height, chunk, tiles),
        out_shape=jax.ShapeDtypeStruct((devices, slots + extra, part), BF16),
        grid_spec=pltpu.PrefetchScalarGridSpec(
            num_scalar_prefetch=1,
            grid=(1,),
            in_specs=[
                pl.BlockSpec(pivot_src.shape, lambda i, *_: (0, 0)),
                pl.BlockSpec(pivot_dst.shape, lambda i, *_: (0, 0)),
                pl.BlockSpec((1, piece, height), lambda i, *_: (0, 0, 0)),
                pl.BlockSpec(memory_space=pl.ANY),
            ],
            out_specs=pl.BlockSpec((devices, slots + extra, part), lambda i, *_: (0, 0, 0)),
            scratch_shapes=[
                pltpu.VMEM((height, cols), BF16),
                pltpu.VMEM((slots, slots), BF16),
                pltpu.VMEM((most, chunk, height - slots), BF16),
                pltpu.VMEM((most, slots, chunk), BF16),
                pltpu.VMEM((slots, cols // tiles), F32),
                pltpu.VMEM((extra, part), BF16),
                pltpu.SemaphoreType.DMA((tiles,)),
            ],
        ),
        compiler_params=params(58),
        cost_estimate=pl.CostEstimate(
            flops=slots * height * cols, bytes_accessed=2 * cols * (height + slots), transcendentals=0
        ),
    )(place, pivot_src, pivot_dst, panels, slab)


def invert_kernel(base, d_ref, o_ref):
    panels, width, _ = o_ref.shape
    count = width // base
    blocks = []
    for k in range(panels):
        for b in range(count):
            at = slice(b * base, (b + 1) * base)
            blocks.append(d_ref[at, k * width + b * base : k * width + (b + 1) * base].astype(F32))
    lower = jnp.stack(blocks)
    row = lax.broadcasted_iota(I32, lower.shape, 1)
    col = lax.broadcasted_iota(I32, lower.shape, 2)
    x = jnp.where(row == col, 1.0, 0.0).astype(F32)
    for c in range(base - 1):
        x = x - lower[:, :, c : c + 1] * x[:, c : c + 1, :]
    o_ref[...] = jnp.zeros(o_ref.shape, F32)
    for k in range(panels):
        for b in range(count):
            at = slice(b * base, (b + 1) * base)
            o_ref[k, at, at] = x[k * count + b]
    size = base
    while size < width:
        for k in range(panels):
            for o in range(0, width, 2 * size):
                up, down = slice(o, o + size), slice(o + size, o + 2 * size)
                inner = dot(d_ref[down, k * width + o : k * width + o + size].astype(F32), o_ref[k, up, up], NN, lax.Precision.HIGHEST)
                o_ref[k, down, up] = -dot(o_ref[k, down, down], inner, NN, lax.Precision.HIGHEST)
        size *= 2


def invert(lower):
    width = lower.shape[0]
    return pl.pallas_call(
        functools.partial(invert_kernel, min(32, width)),
        out_shape=jax.ShapeDtypeStruct((lower.shape[1] // width, width, width), F32),
        compiler_params=params(16),
        cost_estimate=pl.CostEstimate(flops=1 << 20, bytes_accessed=1 << 18, transcendentals=0),
    )(lower)


def apply_inverse(inverse, rows):
    total = None
    for _ in range(3):
        part = inverse.astype(BF16)
        inverse = inverse - part.astype(F32)
        term = dot(part, rows)
        total = term if total is None else total + term
    return total.astype(BF16)


def solve_kernel(width, piece, inv_ref, own_ref, key_ref, r_ref, y_ref, small_ref):
    devices, _, part = r_ref.shape
    slots = 2 * width
    zero = r_ref[0, :slots, :]
    total = jnp.where(own_ref[...] > 0, zero.astype(F32), 0.0)
    for s in range(1, devices):
        total = total + r_ref[s, :slots, :].astype(F32)
    rows = total.astype(BF16)
    upper = apply_inverse(inv_ref[0], rows[:width])
    later = apply_inverse(inv_ref[1], rows[width:])
    want = lax.broadcasted_iota(I32, (devices * CAP, slots), 0)
    want = (want // CAP) * slots + want % CAP
    hot = jnp.where(want.astype(F32) == key_ref[0:1, :], 1.0, 0.0).astype(BF16)
    fill = dot(hot, zero).astype(BF16)
    for d in range(devices):
        y_ref[d, :width, :] = upper
        y_ref[d, width:slots, :] = later
        y_ref[d, slots:, :] = fill[d * CAP : (d + 1) * CAP]
    for h in range(pl.cdiv(width, part)):
        have = min(part, width - h * part)
        at = slice(slots + h * piece, slots + (h + 1) * piece)
        moving = r_ref[0, at, :have]
        picked = jnp.where(key_ref[1:2, h * part : h * part + have] > 0, moving.astype(F32), 0.0)
        for s in range(1, devices):
            picked = picked + r_ref[s, at, :have].astype(F32)
        small_ref[:, h * part : h * part + have] = picked.astype(BF16)
        small_ref[:, width + h * part : width + h * part + have] = moving


def solve(inverse, own, key, received, width, piece):
    devices, _, part = received.shape
    return pl.pallas_call(
        functools.partial(solve_kernel, width, piece),
        out_shape=(
            jax.ShapeDtypeStruct((devices, 2 * width + CAP, part), BF16),
            jax.ShapeDtypeStruct((piece, 2 * width), BF16),
        ),
        compiler_params=params(32),
        cost_estimate=pl.CostEstimate(flops=1 << 29, bytes_accessed=4 << 20, transcendentals=0),
    )(inverse, own, key, received)


def arrange_kernel(width, chips, origins, where, inv_ref, sel_ref, below_ref, land_ref, *refs):
    *piece_refs, o_ref, w_ref, moving_ref, l_ref = refs
    _, piece, cols = piece_refs[0].shape
    step = pl.program_id(0)
    for ref, (back, flip, start) in zip(piece_refs, origins):
        across = lax.rem(where[1] - back + chips, chips)
        column = 2 * across + lax.rem(where[2] + flip, 2)
        for k in range(ref.shape[0]):
            at = pl.multiple_of((start + k) * width + column * piece, piece)
            l_ref[pl.ds(at, piece), :] = ref[k]

    @pl.when((step == 0) & (where[0] == 0))
    def _():
        moving_ref[...] = l_ref[:width, width : 2 * width]

    @pl.when((step == 0) & (where[0] != 0))
    def _():
        moving_ref[...] = below_ref[...]

    here = lax.broadcasted_iota(I32, (width, cols), 1) + where[0] + step * cols
    landing = jnp.where(land_ref[...] == here, 1.0, 0.0)
    moved = dot(moving_ref[...], landing.astype(BF16))
    l_ref[:width, :] = jnp.where(
        landing.sum(0, keepdims=True) > 0, moved, l_ref[:width, :].astype(F32)
    ).astype(BF16)
    o_ref[...] = l_ref[...].T

    @pl.when(step == 0)
    def _():
        coupling = lax.dot_general(
            inv_ref[1], sel_ref[...].astype(F32), (((1,), (1,)), ((), ())),
            preferred_element_type=F32, precision=lax.Precision.HIGHEST,
        )
        w_ref[...] = coupling


def arrange(inverse, selected, below, landing, chips, origins, parts, where):
    panels, piece, height = parts[0].shape
    width = below.shape[0]
    cols = min(512, height)
    pieces = [pl.BlockSpec((part.shape[0], piece, cols), lambda i, *_: (0, 0, i)) for part in parts]
    return pl.pallas_call(
        functools.partial(arrange_kernel, width, chips, origins),
        out_shape=(
            jax.ShapeDtypeStruct((height, panels * width), BF16),
            jax.ShapeDtypeStruct((width, width), F32),
        ),
        grid_spec=pltpu.PrefetchScalarGridSpec(
            num_scalar_prefetch=1,
            grid=(height // cols,),
            in_specs=[
                pl.BlockSpec(inverse.shape, lambda i, *_: (0, 0, 0)),
                pl.BlockSpec(selected.shape, lambda i, *_: (0, 0)),
                pl.BlockSpec(below.shape, lambda i, *_: (0, 0)),
                pl.BlockSpec((width, 1), lambda i, *_: (0, 0)),
            ]
            + pieces,
            out_specs=(
                pl.BlockSpec((cols, panels * width), lambda i, *_: (i, 0)),
                pl.BlockSpec((width, width), lambda i, *_: (0, 0)),
            ),
            scratch_shapes=[pltpu.VMEM((width, width), BF16), pltpu.VMEM((panels * width, cols), BF16)],
        ),
        compiler_params=params(32),
        cost_estimate=pl.CostEstimate(flops=1 << 24, bytes_accessed=1 << 20, transcendentals=0),
    )(where, inverse, selected, below, landing[:, None], *parts)


def update_kernel(
    width, rows, table, place, w_ref, slab_ref, l_hbm, y_ref, rest_ref, o_ref, a_ref, l_ref, u_ref, d_ref, out_ref, ins, sems, load
):
    devices, _, part = y_ref.shape
    height, cols = a_ref.shape
    steps = height // rows
    wide = min(512, cols)
    first = place[0] == 0
    block = [slice(i * rows, (i + 1) * rows) for i in range(steps)]
    uppers, fills, loads = [], [], []
    for e in range(devices):
        at = slice(e * part, (e + 1) * part)
        uppers.append(pltpu.make_async_copy(y_ref.at[e, : 2 * width], u_ref.at[:, at], load.at[e]))
        fills.append(pltpu.make_async_copy(y_ref.at[e, 2 * width :], d_ref.at[:CAP, at], load.at[devices + e]))
    for i, here in enumerate(block):
        loads.append(
            (
                pltpu.make_async_copy(slab_ref.at[here], a_ref.at[here], ins.at[0, i]),
                pltpu.make_async_copy(l_hbm.at[here], l_ref.at[here], ins.at[1, i]),
            )
        )
    for copy in (*uppers, *fills, *loads[0], *loads[min(1, steps - 1)][: 2 if steps > 1 else 0]):
        copy.start()
    for copy in uppers:
        copy.wait()
    high = w_ref[...].astype(BF16)
    rest = (w_ref[...] - high.astype(F32)).astype(BF16)
    for c in range(0, cols, wide):
        at = slice(c, c + wide)
        upper = u_ref[:width, at]
        later = u_ref[width:, at].astype(F32) - (dot(high, upper) + dot(rest, upper))
        u_ref[width:, at] = later.astype(BF16)

    @pl.when(jnp.logical_not(first) & (table[2, steps] > CAP))
    def _():
        for e in range(devices):
            copy = pltpu.make_async_copy(
                rest_ref.at[e, CAP : 2 * width], d_ref.at[CAP:, e * part : (e + 1) * part], sems.at[0]
            )
            copy.start()
            copy.wait()

    group = 16

    def fill(j, carry):
        to, source = table[0, j], table[1, j]
        at = pl.ds(pl.multiple_of(source // group * group, group), group)
        taken = jnp.where(first, a_ref[at, :].astype(F32), d_ref[at, :].astype(F32))
        lane = lax.broadcasted_iota(I32, taken.shape, 0)
        row = jnp.where(lane == source % group, taken, 0.0).sum(0, keepdims=True)
        target = pl.ds(pl.multiple_of(to // group * group, group), group)
        a_ref[target, :] = jnp.where(lane == to % group, row, a_ref[target, :].astype(F32)).astype(BF16)
        return carry

    for copy in fills:
        copy.wait()
    copies = []
    for i, here in enumerate(block):
        for copy in loads[i]:
            copy.wait()
        if i + 2 < steps:
            for copy in loads[i + 2]:
                copy.start()
        lax.fori_loop(table[2, i], table[2, i + 1], fill, 0)
        slot = i % 2
        if i >= 2:
            copies[i - 2].wait()
        for c in range(0, cols, wide):
            at = slice(c, c + wide)
            out_ref[slot, :, at] = (a_ref[here, at].astype(F32) - dot(l_ref[here, :], u_ref[:, at])).astype(BF16)
        if i == 0:

            @pl.when(first)
            def _():
                out_ref[0] = u_ref[...]

        copies.append(pltpu.make_async_copy(out_ref.at[slot], o_ref.at[here], sems.at[slot]))
        copies[i].start()
    for copy in copies[-2:]:
        copy.wait()


def update(slab, lower, upper, coupling, rest, table, place, rows):
    height, cols = slab.shape
    width = lower.shape[1] // 2
    devices, steps = upper.shape[0], height // rows
    return pl.pallas_call(
        functools.partial(update_kernel, width, rows),
        out_shape=jax.ShapeDtypeStruct(slab.shape, BF16),
        grid_spec=pltpu.PrefetchScalarGridSpec(
            num_scalar_prefetch=2,
            grid=(1,),
            in_specs=[pl.BlockSpec(coupling.shape, lambda i, *_: (0, 0))] + [pl.BlockSpec(memory_space=pl.ANY)] * 4,
            out_specs=pl.BlockSpec(memory_space=pl.ANY),
            scratch_shapes=[
                pltpu.VMEM((height, cols), BF16),
                pltpu.VMEM(lower.shape, BF16),
                pltpu.VMEM((2 * width, cols), BF16),
                pltpu.VMEM((2 * width, cols), BF16),
                pltpu.VMEM((2, rows, cols), BF16),
                pltpu.SemaphoreType.DMA((2, steps)),
                pltpu.SemaphoreType.DMA((2,)),
                pltpu.SemaphoreType.DMA((2 * devices,)),
            ],
        ),
        compiler_params=params(54),
        cost_estimate=pl.CostEstimate(
            flops=4 * height * cols * width, bytes_accessed=4 * height * cols, transcendentals=0
        ),
    )(table, place, coupling, slab, lower, upper, rest)


def exchange(x):
    return lax.all_to_all(x, "row", 0, 0)


def per_device(trailing, panels, diag_lower, pivot_src, pivot_dst):
    height, cols = trailing.shape
    width = diag_lower.shape[2]
    slots = 2 * width
    devices = lax.axis_size("row")
    place = lax.axis_index("row").astype(I32)
    offset = place * height
    received = gather(trailing, panels, pivot_src, pivot_dst, place[None], devices)
    received, diag_lower, panels = lax.optimization_barrier((received, diag_lower, panels))
    received = exchange(received)

    columns = lax.axis_size("col")
    chips = columns // 2
    across, core = lax.axis_index("col") // 2, lax.axis_index("col") % 2

    def forward(x, chips_on):
        return lax.ppermute(x, "col", [(d, (d + 2 * chips_on) % columns) for d in range(columns)])

    near = [forward(panels, s) for s in sorted({1, chips - 1} - {0} if chips > 1 else set())]
    diagonal = lax.all_gather(
        jnp.concatenate([diag_lower[0], diag_lower[1]], axis=1), "col", axis=0, tiled=True
    )
    diagonal, pivot_src, pivot_dst = lax.optimization_barrier((diagonal, pivot_src, pivot_dst))
    inverse = invert(diagonal)
    own, key, table = tables(pivot_src, pivot_dst, place[None], height, devices, slots)

    received, near = lax.optimization_barrier((received, near))
    sent, small = solve(inverse, own, key, received, width, panels.shape[1])

    small = lax.all_gather(small, "col", axis=0, tiled=True)

    parts = [panels] + near
    origins = [(0, 0, 0)] + [(s, 0, 0) for s in ((1, chips - 1) if chips > 2 else (1,) if chips > 1 else ())]
    if chips == 4:
        parts += [forward(near[0][:1], 1), forward(near[1][1:], 3)]
        origins += [(2, 0, 0), (2, 0, 1)]
    parts += [lax.ppermute(part, "col", [(d, d ^ 1) for d in range(columns)]) for part in parts]
    origins += [(back, 1, start) for back, _, start in origins]

    selected, below = small[:, :width], small[:, width:slots]
    lower, coupling = arrange(
        inverse,
        selected,
        below,
        jnp.where(place == 0, pivot_dst[1], pivot_src[1]),
        chips,
        tuple(origins),
        parts,
        jnp.stack([offset, across, core]).astype(I32),
    )

    fills = received[0, :slots]
    rounds = (table[3, 0] + CAP - 1) // CAP

    def fetch(state):
        r, found = state
        want = jnp.arange(devices * CAP, dtype=I32)
        want = want // CAP * slots + want % CAP + r * CAP
        part = dot((want[:, None] == key[:1].astype(I32)).astype(BF16), fills).astype(BF16)
        part = exchange(part.reshape(devices, CAP, -1))
        return r + 1, lax.dynamic_update_slice(found, part, (0, r * CAP, 0))

    found = lax.while_loop(lambda state: state[0] < rounds, fetch, (jnp.ones((), I32), received))[1]

    return update(trailing, lower, exchange(sent), coupling, found, table, place[None], slots)


def solution(mesh):
    placed = (P("row", "col"), P(None, "col", "row"), P(None, "col", None), P(), P())
    return jax.shard_map(
        per_device, mesh=mesh, in_specs=placed, out_specs=P("row", "col"), check_vma=False
    )
```

```python
import functools

import jax
import jax.numpy as jnp
from jax import lax
from jax.experimental import pallas as pl
from jax.experimental.pallas import tpu as pltpu
from jax.sharding import PartitionSpec as P

F32, BF16, I32 = jnp.float32, jnp.bfloat16, jnp.int32
TN = (((0,), (0,)), ((), ()))
NN = (((1,), (0,)), ((), ()))
CAP = 64
LANES = 128


def dot(a, b, dims=NN, precision=None):
    return lax.dot_general(a, b, dims, preferred_element_type=F32, precision=precision)


def params(mib):
    return pltpu.CompilerParams(vmem_limit_bytes=mib << 20)


def as_column(row):
    size = row.shape[1]
    eye = lax.broadcasted_iota(I32, (size, size), 0) == lax.broadcasted_iota(I32, (size, size), 1)
    return jnp.where(eye, row, 0.0).sum(1, keepdims=True)


def lookup(keys, table, values, other):
    hit = keys == table
    found = jnp.where(hit, values, 0.0).sum(1, keepdims=True)
    return jnp.where(jnp.where(hit, 1.0, 0.0).sum(1, keepdims=True) > 0, found, other)


def as_row(column):
    size = column.shape[0]
    eye = lax.broadcasted_iota(I32, (size, size), 0) == lax.broadcasted_iota(I32, (size, size), 1)
    return jnp.where(eye, column, 0.0).sum(0, keepdims=True)


def slot_rows(height, me, src_ref, dst_ref):
    width = src_ref.shape[1]
    dst0, dst1 = dst_ref[0:1, :].astype(F32), dst_ref[1:2, :].astype(F32)
    lane = lax.broadcasted_iota(I32, (1, width), 1).astype(F32)
    late = as_column(lane + width)
    late = as_row(lookup(late, dst0, lane, late))
    src1 = as_column(src_ref[1:2, :].astype(F32))
    source = jnp.concatenate([as_column(src_ref[0:1, :].astype(F32)), lookup(src1, dst0, lane, src1)])
    return source, lookup(source, dst1, late, lookup(source, dst0, lane, -1.0))


def owned_first(src_ref, height):
    return src_ref[1:2, :] < height


def table_kernel(height, devices, block, place, src_ref, dst_ref, own_ref, key_ref, table_ref):
    slots = 2 * src_ref.shape[1]
    me = place[0].astype(F32)
    source, content = slot_rows(height, me, src_ref, dst_ref)
    owner = jnp.zeros_like(source)
    for d in range(1, devices):
        owner = owner + jnp.where(source >= float(d * height), 1.0, 0.0)
    own_ref[...] = jnp.where(owner == 0, 1.0, 0.0)
    lane = lax.broadcasted_iota(I32, (slots, slots), 1).astype(F32)
    line = lax.broadcasted_iota(I32, (slots, slots), 0).astype(F32)
    rank = jnp.where((owner == as_row(owner)) & (lane < line), 1.0, 0.0).sum(1, keepdims=True)
    key = as_row(jnp.where(owner > 0, owner * slots + rank, -1.0))
    first = jnp.where(owned_first(src_ref, height), 1.0, 0.0)
    key_ref[...] = jnp.concatenate([key, jnp.concatenate([first, first], 1)] * 4)
    rest = jnp.where((owner == me) & (source >= slots), source - me * height, float(height))
    order = (as_row(rest) * slots + lane < rest * slots + line).astype(F32).sum(1, keepdims=True)
    sort = order == lane
    hole = jnp.where(sort, rest, 0.0).sum(0, keepdims=True)
    slot = jnp.where(sort, jnp.where(me == 0, content, rank), 0.0).sum(0, keepdims=True)
    begin = jnp.where(rest < lane * block, 1.0, 0.0).sum(0, keepdims=True)
    most = jnp.where(owner > 0, rank + 1.0, 0.0).max(0, keepdims=True)
    most = jnp.broadcast_to(most, (1, slots))
    table_ref[...] = jnp.concatenate([hole, slot, begin, most] * 2).astype(I32)


def tables(pivot_src, pivot_dst, place, height, devices, block):
    slots = 2 * pivot_src.shape[1]
    whole = lambda i, *_: (0, 0)
    return pl.pallas_call(
        functools.partial(table_kernel, height, devices, block),
        out_shape=(
            jax.ShapeDtypeStruct((slots, 1), F32),
            jax.ShapeDtypeStruct((8, slots), F32),
            jax.ShapeDtypeStruct((8, slots), I32),
        ),
        grid_spec=pltpu.PrefetchScalarGridSpec(
            num_scalar_prefetch=1,
            grid=(1,),
            in_specs=[pl.BlockSpec(pivot_src.shape, whole), pl.BlockSpec(pivot_dst.shape, whole)],
            out_specs=(
                pl.BlockSpec((slots, 1), whole),
                pl.BlockSpec((8, slots), whole),
                pl.BlockSpec((8, slots), whole),
            ),
        ),
        compiler_params=params(24),
    )(place, pivot_src, pivot_dst)


def gather_kernel(
    height, chunk, tiles, place, src_ref, dst_ref, p_ref, slab_ref, o_ref, a_ref, top_ref, low_ref, spread_ref, acc_ref, extra_ref, out_ref, sems, outs
):
    width = src_ref.shape[1]
    slots = 2 * width
    cols = a_ref.shape[1] // tiles
    part = o_ref.shape[2]
    tile = [slice(t * cols, (t + 1) * cols) for t in range(tiles)]
    copies = [pltpu.make_async_copy(slab_ref.at[:, at], a_ref.at[:, at], sems.at[t]) for t, at in enumerate(tile)]
    for copy in copies[:2]:
        copy.start()

    me = place[0].astype(F32)
    source, content = slot_rows(height, me, src_ref, dst_ref)
    here = source - me * height
    wanted = jnp.where((here >= 0) & (here < height), here, jnp.where(me == 0, content, -1.0))
    column = lax.broadcasted_iota(I32, (slots, slots), 1).astype(F32)
    top_ref[...] = jnp.where(column == wanted, 1.0, 0.0).astype(BF16)
    low = wanted >= slots
    before = jnp.where(column < lax.broadcasted_iota(I32, (slots, slots), 0).astype(F32), 1.0, 0.0)
    flag = jnp.where(low, 1.0, 0.0)
    rank = dot(before.astype(BF16), jnp.broadcast_to(flag, (slots, LANES)).astype(BF16))[:, :1]
    rank = jnp.where(low, rank, -1.0)
    rounds = (flag.sum().astype(I32) + chunk - 1) // chunk

    def build(r, carry):
        spot = lax.broadcasted_iota(I32, (slots, chunk), 1).astype(F32) + (r * chunk).astype(F32)
        spread = rank == spot
        spread_ref[r] = jnp.where(spread, 1.0, 0.0).astype(BF16)
        row = as_column(jnp.where(spread, wanted, 0.0).sum(0, keepdims=True))
        below = lax.broadcasted_iota(I32, low_ref.shape[1:], 1).astype(F32) + float(slots)
        low_ref[r] = jnp.where(below == row, 1.0, 0.0).astype(BF16)
        return carry

    lax.fori_loop(0, rounds, build, 0)

    src1 = as_column(src_ref[1:2, :].astype(F32))
    lane = lax.broadcasted_iota(I32, (1, width), 1).astype(F32)
    here = src1 - me * height
    moving = lookup(src1, dst_ref[1:2, :].astype(F32), lane + width, -1.0)
    chosen = jnp.where((here >= 0) & (here < height), here, jnp.where(me == 0, moving, -1.0))
    row = lax.broadcasted_iota(I32, (height, width), 0).astype(F32)
    hot = jnp.where(row == as_row(chosen), 1.0, 0.0).astype(BF16)
    taken = dot(p_ref[0], hot).astype(BF16)
    piece = taken.shape[0]
    for h in range(extra_ref.shape[0] // piece):
        have = min(part, width - h * part)
        extra_ref[h * piece : (h + 1) * piece, :have] = taken[:, h * part : h * part + have]

    sends = []
    for t in range(tiles):
        copies[t].wait()
        if t + 2 < tiles:
            copies[t + 2].start()
        at = tile[t]
        acc_ref[...] = dot(top_ref[...], a_ref[:slots, at])

        def add(r, carry, at=at):
            found = dot(low_ref[r], a_ref[slots:, at]).astype(BF16)
            acc_ref[...] += dot(spread_ref[r], found)
            return carry

        lax.fori_loop(0, rounds, add, 0)
        for b in range(cols // part):
            out_ref[t * (cols // part) + b, :slots, :] = acc_ref[:, b * part : (b + 1) * part].astype(BF16)
            out_ref[t * (cols // part) + b, slots:, :] = extra_ref[...]
        done = slice(t * (cols // part), (t + 1) * (cols // part))
        sends.append(pltpu.make_async_copy(out_ref.at[done], o_ref.at[done], outs.at[t]))
        sends[t].start()
    for send in sends:
        send.wait()


def gather(slab, panels, pivot_src, pivot_dst, place, devices):
    height, cols = slab.shape
    width = pivot_src.shape[1]
    slots, part = 2 * width, cols // devices
    chunk = min(LANES, slots)
    most = slots // chunk
    tiles = min(4, devices)
    piece = panels.shape[1]
    extra = piece * pl.cdiv(width, part)
    return pl.pallas_call(
        functools.partial(gather_kernel, height, chunk, tiles),
        out_shape=jax.ShapeDtypeStruct((devices, slots + extra, part), BF16),
        grid_spec=pltpu.PrefetchScalarGridSpec(
            num_scalar_prefetch=1,
            grid=(1,),
            in_specs=[
                pl.BlockSpec(pivot_src.shape, lambda i, *_: (0, 0)),
                pl.BlockSpec(pivot_dst.shape, lambda i, *_: (0, 0)),
                pl.BlockSpec((1, piece, height), lambda i, *_: (0, 0, 0)),
                pl.BlockSpec(memory_space=pl.ANY),
            ],
            out_specs=pl.BlockSpec(memory_space=pl.ANY),
            scratch_shapes=[
                pltpu.VMEM((height, cols), BF16),
                pltpu.VMEM((slots, slots), BF16),
                pltpu.VMEM((most, chunk, height - slots), BF16),
                pltpu.VMEM((most, slots, chunk), BF16),
                pltpu.VMEM((slots, cols // tiles), F32),
                pltpu.VMEM((extra, part), BF16),
                pltpu.VMEM((devices, slots + extra, part), BF16),
                pltpu.SemaphoreType.DMA((tiles,)),
                pltpu.SemaphoreType.DMA((tiles,)),
            ],
        ),
        compiler_params=params(58),
        cost_estimate=pl.CostEstimate(
            flops=slots * height * cols, bytes_accessed=2 * cols * (height + slots), transcendentals=0
        ),
    )(place, pivot_src, pivot_dst, panels, slab)


def invert_kernel(base, d_ref, o_ref):
    panels, width, _ = o_ref.shape
    count = width // base
    blocks = []
    for k in range(panels):
        for b in range(count):
            at = slice(b * base, (b + 1) * base)
            blocks.append(d_ref[at, k * width + b * base : k * width + (b + 1) * base].astype(F32))
    lower = jnp.stack(blocks)
    row = lax.broadcasted_iota(I32, lower.shape, 1)
    col = lax.broadcasted_iota(I32, lower.shape, 2)
    x = jnp.where(row == col, 1.0, 0.0).astype(F32)
    for c in range(base - 1):
        x = x - lower[:, :, c : c + 1] * x[:, c : c + 1, :]
    o_ref[...] = jnp.zeros(o_ref.shape, F32)
    for k in range(panels):
        for b in range(count):
            at = slice(b * base, (b + 1) * base)
            o_ref[k, at, at] = x[k * count + b]
    size = base
    while size < width:
        for k in range(panels):
            for o in range(0, width, 2 * size):
                up, down = slice(o, o + size), slice(o + size, o + 2 * size)
                inner = dot(d_ref[down, k * width + o : k * width + o + size].astype(F32), o_ref[k, up, up], NN, lax.Precision.HIGHEST)
                o_ref[k, down, up] = -dot(o_ref[k, down, down], inner, NN, lax.Precision.HIGHEST)
        size *= 2


def invert(lower):
    width = lower.shape[0]
    return pl.pallas_call(
        functools.partial(invert_kernel, min(32, width)),
        out_shape=jax.ShapeDtypeStruct((lower.shape[1] // width, width, width), F32),
        compiler_params=params(16),
        cost_estimate=pl.CostEstimate(flops=1 << 20, bytes_accessed=1 << 18, transcendentals=0),
    )(lower)


def apply_inverse(inverse, rows):
    total = None
    for _ in range(3):
        part = inverse.astype(BF16)
        inverse = inverse - part.astype(F32)
        term = dot(part, rows)
        total = term if total is None else total + term
    return total.astype(BF16)


def solve_kernel(
    width, piece, inv_ref, own_ref, key_ref, r_hbm, y_ref, small_ref, zero_ref, r_ref, u_ref, fill_ref, ins, outs
):
    devices, _, part = r_ref.shape
    slots = 2 * width
    loads = [pltpu.make_async_copy(r_hbm.at[s], r_ref.at[s], ins.at[s]) for s in range(devices)]
    for load in loads:
        load.start()
    want = lax.broadcasted_iota(I32, (devices * CAP, slots), 0)
    want = (want // CAP) * slots + want % CAP
    hot = jnp.where(want.astype(F32) == key_ref[0:1, :], 1.0, 0.0).astype(BF16)
    loads[0].wait()
    zero = r_ref[0, :slots, :]
    zero_ref[...] = zero
    fill_ref[...] = dot(hot, zero).astype(BF16)
    sends = []
    for d in range(devices):
        fills = fill_ref.at[d * CAP : (d + 1) * CAP]
        sends.append(pltpu.make_async_copy(fills, y_ref.at[d, slots:], outs.at[0, d]))
        sends[-1].start()
    total = jnp.where(own_ref[...] > 0, zero.astype(F32), 0.0)
    for s in range(1, devices):
        loads[s].wait()
        total = total + r_ref[s, :slots, :].astype(F32)
    rows = total.astype(BF16)
    for k in range(2):
        here = slice(k * width, (k + 1) * width)
        u_ref[here, :] = apply_inverse(inv_ref[k], rows[here])
        for d in range(devices):
            sends.append(pltpu.make_async_copy(u_ref.at[here], y_ref.at[d, here], outs.at[1 + k, d]))
            sends[-1].start()
    for h in range(pl.cdiv(width, part)):
        have = min(part, width - h * part)
        at = slice(slots + h * piece, slots + (h + 1) * piece)
        moving = r_ref[0, at, :have]
        picked = jnp.where(key_ref[1:2, h * part : h * part + have] > 0, moving.astype(F32), 0.0)
        for s in range(1, devices):
            picked = picked + r_ref[s, at, :have].astype(F32)
        small_ref[:, h * part : h * part + have] = picked.astype(BF16)
        small_ref[:, width + h * part : width + h * part + have] = moving
    for send in sends:
        send.wait()


def solve(inverse, own, key, received, width, piece):
    devices, _, part = received.shape
    vmem = pl.BlockSpec(memory_space=pltpu.VMEM)
    return pl.pallas_call(
        functools.partial(solve_kernel, width, piece),
        out_shape=(
            jax.ShapeDtypeStruct((devices, 2 * width + CAP, part), BF16),
            jax.ShapeDtypeStruct((piece, 2 * width), BF16),
            jax.ShapeDtypeStruct((2 * width, part), BF16),
        ),
        in_specs=[vmem, vmem, vmem, pl.BlockSpec(memory_space=pl.ANY)],
        out_specs=(pl.BlockSpec(memory_space=pl.ANY), vmem, vmem),
        scratch_shapes=[
            pltpu.VMEM(received.shape, BF16),
            pltpu.VMEM((2 * width, part), BF16),
            pltpu.VMEM((devices * CAP, part), BF16),
            pltpu.SemaphoreType.DMA((devices,)),
            pltpu.SemaphoreType.DMA((3, devices)),
        ],
        compiler_params=params(24),
        cost_estimate=pl.CostEstimate(flops=1 << 29, bytes_accessed=4 << 20, transcendentals=0),
    )(inverse, own, key, received)


def arrange_kernel(width, chips, origins, where, inv_ref, sel_ref, below_ref, land_ref, *refs):
    *piece_refs, o_ref, w_ref, moving_ref, l_ref = refs
    _, piece, cols = piece_refs[0].shape
    step = pl.program_id(0)
    for ref, (back, flip, start) in zip(piece_refs, origins):
        across = lax.rem(where[1] - back + chips, chips)
        column = 2 * across + lax.rem(where[2] + flip, 2)
        for k in range(ref.shape[0]):
            at = pl.multiple_of((start + k) * width + column * piece, piece)
            l_ref[pl.ds(at, piece), :] = ref[k]

    @pl.when((step == 0) & (where[0] == 0))
    def _():
        moving_ref[...] = l_ref[:width, width : 2 * width]

    @pl.when((step == 0) & (where[0] != 0))
    def _():
        moving_ref[...] = below_ref[...]

    here = lax.broadcasted_iota(I32, (width, cols), 1) + where[0] + step * cols
    landing = jnp.where(land_ref[...] == here, 1.0, 0.0)
    moved = dot(moving_ref[...], landing.astype(BF16))
    l_ref[:width, :] = jnp.where(
        landing.sum(0, keepdims=True) > 0, moved, l_ref[:width, :].astype(F32)
    ).astype(BF16)
    o_ref[...] = l_ref[...].T

    @pl.when(step == 0)
    def _():
        coupling = lax.dot_general(
            inv_ref[1], sel_ref[...].astype(F32), (((1,), (1,)), ((), ())),
            preferred_element_type=F32, precision=lax.Precision.HIGHEST,
        )
        w_ref[...] = coupling


def arrange(inverse, selected, below, landing, chips, origins, parts, where):
    panels, piece, height = parts[0].shape
    width = below.shape[0]
    cols = min(512, height)
    pieces = [pl.BlockSpec((part.shape[0], piece, cols), lambda i, *_: (0, 0, i)) for part in parts]
    return pl.pallas_call(
        functools.partial(arrange_kernel, width, chips, origins),
        out_shape=(
            pltpu.HBM((height, panels * width), BF16),
            pltpu.HBM((width, width), F32),
        ),
        grid_spec=pltpu.PrefetchScalarGridSpec(
            num_scalar_prefetch=1,
            grid=(height // cols,),
            in_specs=[
                pl.BlockSpec(inverse.shape, lambda i, *_: (0, 0, 0)),
                pl.BlockSpec(selected.shape, lambda i, *_: (0, 0)),
                pl.BlockSpec(below.shape, lambda i, *_: (0, 0)),
                pl.BlockSpec((width, 1), lambda i, *_: (0, 0)),
            ]
            + pieces,
            out_specs=(
                pl.BlockSpec((cols, panels * width), lambda i, *_: (i, 0)),
                pl.BlockSpec((width, width), lambda i, *_: (0, 0)),
            ),
            scratch_shapes=[pltpu.VMEM((width, width), BF16), pltpu.VMEM((panels * width, cols), BF16)],
        ),
        compiler_params=params(32),
        cost_estimate=pl.CostEstimate(flops=1 << 24, bytes_accessed=1 << 20, transcendentals=0),
    )(where, inverse, selected, below, landing[:, None], *parts)


def update_kernel(
    width, rows, table, place, w_ref, slab_ref, l_hbm, y_ref, rest_ref, o_ref, a_ref, l_ref, u_ref, d_ref, out_ref, ins, sems, load
):
    devices, _, part = y_ref.shape
    height, cols = a_ref.shape
    steps = height // rows
    wide = min(512, cols)
    first = place[0] == 0
    block = [slice(i * rows, (i + 1) * rows) for i in range(steps)]
    uppers, fills, loads = [], [], []
    for e in range(devices):
        at = slice(e * part, (e + 1) * part)
        uppers.append(pltpu.make_async_copy(y_ref.at[e, : 2 * width], u_ref.at[:, at], load.at[e]))
        fills.append(pltpu.make_async_copy(y_ref.at[e, 2 * width :], d_ref.at[:CAP, at], load.at[devices + e]))
    for i, here in enumerate(block):
        loads.append(
            (
                pltpu.make_async_copy(slab_ref.at[here], a_ref.at[here], ins.at[0, i]),
                pltpu.make_async_copy(l_hbm.at[here], l_ref.at[here], ins.at[1, i]),
            )
        )
    for copy in (*uppers, *fills, *loads[0]):
        copy.start()
    for copy in uppers:
        copy.wait()
    if steps > 1:
        for copy in loads[1]:
            copy.start()
    high = w_ref[...].astype(BF16)
    rest = (w_ref[...] - high.astype(F32)).astype(BF16)
    for c in range(0, cols, wide):
        at = slice(c, c + wide)
        upper = u_ref[:width, at]
        later = u_ref[width:, at].astype(F32) - (dot(high, upper) + dot(rest, upper))
        u_ref[width:, at] = later.astype(BF16)

    @pl.when(jnp.logical_not(first) & (table[2, steps] > CAP))
    def _():
        for e in range(devices):
            copy = pltpu.make_async_copy(
                rest_ref.at[e, CAP : 2 * width], d_ref.at[CAP:, e * part : (e + 1) * part], sems.at[0, 0]
            )
            copy.start()
            copy.wait()

    group = 16

    def put(from_ref, j):
        to, source = table[0, j], table[1, j]
        taken = from_ref[pl.ds(pl.multiple_of(source // group * group, group), group), :].astype(F32)
        lane = lax.broadcasted_iota(I32, taken.shape, 0)
        row = jnp.where(lane == source % group, taken, 0.0).sum(0, keepdims=True)
        target = pl.ds(pl.multiple_of(to // group * group, group), group)
        a_ref[target, :] = jnp.where(lane == to % group, row, a_ref[target, :].astype(F32)).astype(BF16)

    for copy in fills:
        copy.wait()
    copies = []
    for i, here in enumerate(block):
        for copy in loads[i]:
            copy.wait()
        if i + 2 < steps:
            for copy in loads[i + 2]:
                copy.start()
        slot = i % 2

        @pl.when(first)
        def _(i=i):
            pl.loop(table[2, i], table[2, i + 1])(lambda j: put(a_ref, j))

        @pl.when(jnp.logical_not(first))
        def _(i=i):
            pl.loop(table[2, i], table[2, i + 1])(lambda j: put(d_ref, j))

        if i >= 2:
            for copy in copies[i - 2]:
                copy.wait()
        copies.append([])
        for b, c in enumerate(range(0, cols, wide)):
            at = slice(c, c + wide)
            out_ref[slot, :, at] = (a_ref[here, at].astype(F32) - dot(l_ref[here, :], u_ref[:, at])).astype(BF16)
            if i == 0:

                @pl.when(first)
                def _(at=at):
                    out_ref[0, :, at] = u_ref[:, at]

            copies[i].append(pltpu.make_async_copy(out_ref.at[slot, :, at], o_ref.at[here, at], sems.at[slot, b]))
            copies[i][b].start()
    for copy in sum(copies[-2:], []):
        copy.wait()


def update(slab, lower, upper, coupling, rest, table, place, rows):
    height, cols = slab.shape
    width = lower.shape[1] // 2
    devices, steps = upper.shape[0], height // rows
    return pl.pallas_call(
        functools.partial(update_kernel, width, rows),
        out_shape=jax.ShapeDtypeStruct(slab.shape, BF16),
        grid_spec=pltpu.PrefetchScalarGridSpec(
            num_scalar_prefetch=2,
            grid=(1,),
            in_specs=[pl.BlockSpec(coupling.shape, lambda i, *_: (0, 0))] + [pl.BlockSpec(memory_space=pl.ANY)] * 4,
            out_specs=pl.BlockSpec(memory_space=pl.ANY),
            scratch_shapes=[
                pltpu.VMEM((height, cols), BF16),
                pltpu.VMEM(lower.shape, BF16),
                pltpu.VMEM((2 * width, cols), BF16),
                pltpu.VMEM((2 * width, cols), BF16),
                pltpu.VMEM((2, rows, cols), BF16),
                pltpu.SemaphoreType.DMA((2, steps)),
                pltpu.SemaphoreType.DMA((2, pl.cdiv(cols, 512))),
                pltpu.SemaphoreType.DMA((2 * devices,)),
            ],
        ),
        compiler_params=params(54),
        cost_estimate=pl.CostEstimate(
            flops=4 * height * cols * width, bytes_accessed=4 * height * cols, transcendentals=0
        ),
    )(table, place, coupling, slab, lower, upper, rest)


def exchange(x):
    return lax.all_to_all(x, "row", 0, 0)


def per_device(trailing, panels, diag_lower, pivot_src, pivot_dst):
    height, cols = trailing.shape
    width = diag_lower.shape[2]
    slots = 2 * width
    devices = lax.axis_size("row")
    place = lax.axis_index("row").astype(I32)
    offset = place * height
    received = gather(trailing, panels, pivot_src, pivot_dst, place[None], devices)
    received, diag_lower, panels = lax.optimization_barrier((received, diag_lower, panels))
    received = exchange(received)

    columns = lax.axis_size("col")
    chips = columns // 2
    across, core = lax.axis_index("col") // 2, lax.axis_index("col") % 2

    def forward(x, chips_on):
        return lax.ppermute(x, "col", [(d, (d + 2 * chips_on) % columns) for d in range(columns)])

    near = [forward(panels, s) for s in sorted({1, chips - 1} - {0} if chips > 1 else set())]
    diagonal = lax.all_gather(
        jnp.concatenate([diag_lower[0], diag_lower[1]], axis=1), "col", axis=0, tiled=True
    )
    diagonal, pivot_src, pivot_dst = lax.optimization_barrier((diagonal, pivot_src, pivot_dst))
    inverse = invert(diagonal)
    own, key, table = tables(pivot_src, pivot_dst, place[None], height, devices, slots)

    received, near = lax.optimization_barrier((received, near))
    sent, small, fills = solve(inverse, own, key, received, width, panels.shape[1])

    small = lax.all_gather(small, "col", axis=0, tiled=True)

    parts = [panels] + near
    origins = [(0, 0, 0)] + [(s, 0, 0) for s in ((1, chips - 1) if chips > 2 else (1,) if chips > 1 else ())]
    if chips == 4:
        parts += [forward(near[0][:1], 1), forward(near[1][1:], 3)]
        origins += [(2, 0, 0), (2, 0, 1)]
    parts += [lax.ppermute(part, "col", [(d, d ^ 1) for d in range(columns)]) for part in parts]
    origins += [(back, 1, start) for back, _, start in origins]

    selected, below = small[:, :width], small[:, width:slots]
    lower, coupling = arrange(
        inverse,
        selected,
        below,
        jnp.where(place == 0, pivot_dst[1], pivot_src[1]),
        chips,
        tuple(origins),
        parts,
        jnp.stack([offset, across, core]).astype(I32),
    )

    rounds = (table[3, 0] + CAP - 1) // CAP

    def fetch(state):
        r, found = state
        want = jnp.arange(devices * CAP, dtype=I32)
        want = want // CAP * slots + want % CAP + r * CAP
        part = dot((want[:, None] == key[:1].astype(I32)).astype(BF16), fills).astype(BF16)
        part = exchange(part.reshape(devices, CAP, -1))
        return r + 1, lax.dynamic_update_slice(found, part, (0, r * CAP, 0))

    found = lax.while_loop(lambda state: state[0] < rounds, fetch, (jnp.ones((), I32), received))[1]

    return update(trailing, lower, exchange(sent), coupling, found, table, place[None], slots)


def solution(mesh):
    placed = (P("row", "col"), P(None, "col", "row"), P(None, "col", None), P(), P())
    return jax.shard_map(
        per_device, mesh=mesh, in_specs=placed, out_specs=P("row", "col"), check_vma=False
    )
```

```python
import functools

import jax
import jax.numpy as jnp
from jax import lax
from jax.experimental import pallas as pl
from jax.experimental.pallas import tpu as pltpu
from jax.sharding import PartitionSpec as P

F32, BF16, I32 = jnp.float32, jnp.bfloat16, jnp.int32
TN = (((0,), (0,)), ((), ()))
NN = (((1,), (0,)), ((), ()))
CAP = 64
LANES = 128


def dot(a, b, dims=NN, precision=None):
    return lax.dot_general(a, b, dims, preferred_element_type=F32, precision=precision)


def params(mib):
    return pltpu.CompilerParams(vmem_limit_bytes=mib << 20)


def as_column(row):
    size = row.shape[1]
    eye = lax.broadcasted_iota(I32, (size, size), 0) == lax.broadcasted_iota(I32, (size, size), 1)
    return jnp.where(eye, row, 0.0).sum(1, keepdims=True)


def lookup(keys, table, values, other):
    hit = keys == table
    found = jnp.where(hit, values, 0.0).sum(1, keepdims=True)
    return jnp.where(jnp.where(hit, 1.0, 0.0).sum(1, keepdims=True) > 0, found, other)


def as_row(column):
    size = column.shape[0]
    eye = lax.broadcasted_iota(I32, (size, size), 0) == lax.broadcasted_iota(I32, (size, size), 1)
    return jnp.where(eye, column, 0.0).sum(0, keepdims=True)


def slot_rows(height, me, src_ref, dst_ref):
    width = src_ref.shape[1]
    dst0, dst1 = dst_ref[0:1, :].astype(F32), dst_ref[1:2, :].astype(F32)
    lane = lax.broadcasted_iota(I32, (1, width), 1).astype(F32)
    late = as_column(lane + width)
    late = as_row(lookup(late, dst0, lane, late))
    src1 = as_column(src_ref[1:2, :].astype(F32))
    source = jnp.concatenate([as_column(src_ref[0:1, :].astype(F32)), lookup(src1, dst0, lane, src1)])
    return source, lookup(source, dst1, late, lookup(source, dst0, lane, -1.0))


def owned_first(src_ref, height):
    return src_ref[1:2, :] < height


def table_kernel(height, devices, block, place, src_ref, dst_ref, own_ref, key_ref, table_ref):
    slots = 2 * src_ref.shape[1]
    me = place[0].astype(F32)
    source, content = slot_rows(height, me, src_ref, dst_ref)
    owner = jnp.zeros_like(source)
    for d in range(1, devices):
        owner = owner + jnp.where(source >= float(d * height), 1.0, 0.0)
    own_ref[...] = jnp.where(owner == 0, 1.0, 0.0)
    lane = lax.broadcasted_iota(I32, (slots, slots), 1).astype(F32)
    line = lax.broadcasted_iota(I32, (slots, slots), 0).astype(F32)
    rank = jnp.where((owner == as_row(owner)) & (lane < line), 1.0, 0.0).sum(1, keepdims=True)
    key = as_row(jnp.where(owner > 0, owner * slots + rank, -1.0))
    first = jnp.where(owned_first(src_ref, height), 1.0, 0.0)
    key_ref[...] = jnp.concatenate([key, jnp.concatenate([first, first], 1)] * 4)
    rest = jnp.where((owner == me) & (source >= slots), source - me * height, float(height))
    order = (as_row(rest) * slots + lane < rest * slots + line).astype(F32).sum(1, keepdims=True)
    sort = order == lane
    hole = jnp.where(sort, rest, 0.0).sum(0, keepdims=True)
    slot = jnp.where(sort, jnp.where(me == 0, content, rank), 0.0).sum(0, keepdims=True)
    begin = jnp.where(rest < lane * block, 1.0, 0.0).sum(0, keepdims=True)
    most = jnp.where(owner > 0, rank + 1.0, 0.0).max(0, keepdims=True)
    most = jnp.broadcast_to(most, (1, slots))
    table_ref[...] = jnp.concatenate([hole, slot, begin, most] * 2).astype(I32)


def tables(pivot_src, pivot_dst, place, height, devices, block):
    slots = 2 * pivot_src.shape[1]
    whole = lambda i, *_: (0, 0)
    return pl.pallas_call(
        functools.partial(table_kernel, height, devices, block),
        out_shape=(
            jax.ShapeDtypeStruct((slots, 1), F32),
            jax.ShapeDtypeStruct((8, slots), F32),
            jax.ShapeDtypeStruct((8, slots), I32),
        ),
        grid_spec=pltpu.PrefetchScalarGridSpec(
            num_scalar_prefetch=1,
            grid=(1,),
            in_specs=[pl.BlockSpec(pivot_src.shape, whole), pl.BlockSpec(pivot_dst.shape, whole)],
            out_specs=(
                pl.BlockSpec((slots, 1), whole),
                pl.BlockSpec((8, slots), whole),
                pl.BlockSpec((8, slots), whole),
            ),
        ),
        compiler_params=params(24),
    )(place, pivot_src, pivot_dst)


def gather_kernel(
    height, chunk, tiles, place, src_ref, dst_ref, p_ref, slab_ref, o_ref, a_ref, top_ref, low_ref, spread_ref, acc_ref, extra_ref, out_ref, sems, outs
):
    width = src_ref.shape[1]
    slots = 2 * width
    cols = a_ref.shape[1] // tiles
    part = o_ref.shape[2]
    tile = [slice(t * cols, (t + 1) * cols) for t in range(tiles)]
    copies = [pltpu.make_async_copy(slab_ref.at[:, at], a_ref.at[:, at], sems.at[t]) for t, at in enumerate(tile)]
    for copy in copies[:2]:
        copy.start()

    me = place[0].astype(F32)
    source, content = slot_rows(height, me, src_ref, dst_ref)
    here = source - me * height
    wanted = jnp.where((here >= 0) & (here < height), here, jnp.where(me == 0, content, -1.0))
    column = lax.broadcasted_iota(I32, (slots, slots), 1).astype(F32)
    top_ref[...] = jnp.where(column == wanted, 1.0, 0.0).astype(BF16)
    low = wanted >= slots
    before = jnp.where(column < lax.broadcasted_iota(I32, (slots, slots), 0).astype(F32), 1.0, 0.0)
    flag = jnp.where(low, 1.0, 0.0)
    rank = dot(before.astype(BF16), jnp.broadcast_to(flag, (slots, LANES)).astype(BF16))[:, :1]
    rank = jnp.where(low, rank, -1.0)
    rounds = (flag.sum().astype(I32) + chunk - 1) // chunk

    def build(r, carry):
        spot = lax.broadcasted_iota(I32, (slots, chunk), 1).astype(F32) + (r * chunk).astype(F32)
        spread = rank == spot
        spread_ref[r] = jnp.where(spread, 1.0, 0.0).astype(BF16)
        row = as_column(jnp.where(spread, wanted, 0.0).sum(0, keepdims=True))
        below = lax.broadcasted_iota(I32, low_ref.shape[1:], 1).astype(F32) + float(slots)
        low_ref[r] = jnp.where(below == row, 1.0, 0.0).astype(BF16)
        return carry

    lax.fori_loop(0, rounds, build, 0)

    src1 = as_column(src_ref[1:2, :].astype(F32))
    lane = lax.broadcasted_iota(I32, (1, width), 1).astype(F32)
    here = src1 - me * height
    moving = lookup(src1, dst_ref[1:2, :].astype(F32), lane + width, -1.0)
    chosen = jnp.where((here >= 0) & (here < height), here, jnp.where(me == 0, moving, -1.0))
    row = lax.broadcasted_iota(I32, (height, width), 0).astype(F32)
    hot = jnp.where(row == as_row(chosen), 1.0, 0.0).astype(BF16)
    taken = dot(p_ref[0], hot).astype(BF16)
    piece = taken.shape[0]
    for h in range(extra_ref.shape[0] // piece):
        have = min(part, width - h * part)
        extra_ref[h * piece : (h + 1) * piece, :have] = taken[:, h * part : h * part + have]

    sends = []
    for t in range(tiles):
        copies[t].wait()
        if t + 2 < tiles:
            copies[t + 2].start()
        at = tile[t]
        acc_ref[...] = dot(top_ref[...], a_ref[:slots, at])

        def add(r, carry, at=at):
            found = dot(low_ref[r], a_ref[slots:, at]).astype(BF16)
            acc_ref[...] += dot(spread_ref[r], found)
            return carry

        lax.fori_loop(0, rounds, add, 0)
        for b in range(cols // part):
            out_ref[t * (cols // part) + b, :slots, :] = acc_ref[:, b * part : (b + 1) * part].astype(BF16)
            out_ref[t * (cols // part) + b, slots:, :] = extra_ref[...]
        done = slice(t * (cols // part), (t + 1) * (cols // part))
        sends.append(pltpu.make_async_copy(out_ref.at[done], o_ref.at[done], outs.at[t]))
        sends[t].start()
    for send in sends:
        send.wait()


def gather(slab, panels, pivot_src, pivot_dst, place, devices):
    height, cols = slab.shape
    width = pivot_src.shape[1]
    slots, part = 2 * width, cols // devices
    chunk = min(LANES, slots)
    most = slots // chunk
    tiles = min(4, devices)
    piece = panels.shape[1]
    extra = piece * pl.cdiv(width, part)
    return pl.pallas_call(
        functools.partial(gather_kernel, height, chunk, tiles),
        out_shape=jax.ShapeDtypeStruct((devices, slots + extra, part), BF16),
        grid_spec=pltpu.PrefetchScalarGridSpec(
            num_scalar_prefetch=1,
            grid=(1,),
            in_specs=[
                pl.BlockSpec(pivot_src.shape, lambda i, *_: (0, 0)),
                pl.BlockSpec(pivot_dst.shape, lambda i, *_: (0, 0)),
                pl.BlockSpec((1, piece, height), lambda i, *_: (0, 0, 0)),
                pl.BlockSpec(memory_space=pl.ANY),
            ],
            out_specs=pl.BlockSpec(memory_space=pl.ANY),
            scratch_shapes=[
                pltpu.VMEM((height, cols), BF16),
                pltpu.VMEM((slots, slots), BF16),
                pltpu.VMEM((most, chunk, height - slots), BF16),
                pltpu.VMEM((most, slots, chunk), BF16),
                pltpu.VMEM((slots, cols // tiles), F32),
                pltpu.VMEM((extra, part), BF16),
                pltpu.VMEM((devices, slots + extra, part), BF16),
                pltpu.SemaphoreType.DMA((tiles,)),
                pltpu.SemaphoreType.DMA((tiles,)),
            ],
        ),
        compiler_params=params(58),
        cost_estimate=pl.CostEstimate(
            flops=slots * height * cols, bytes_accessed=2 * cols * (height + slots), transcendentals=0
        ),
    )(place, pivot_src, pivot_dst, panels, slab)


def invert_kernel(base, d_ref, o_ref):
    panels, width, _ = o_ref.shape
    count = width // base
    blocks = []
    for k in range(panels):
        for b in range(count):
            at = slice(b * base, (b + 1) * base)
            blocks.append(d_ref[at, k * width + b * base : k * width + (b + 1) * base].astype(F32))
    lower = jnp.stack(blocks)
    row = lax.broadcasted_iota(I32, lower.shape, 1)
    col = lax.broadcasted_iota(I32, lower.shape, 2)
    x = jnp.where(row == col, 1.0, 0.0).astype(F32)
    for c in range(base - 1):
        x = x - lower[:, :, c : c + 1] * x[:, c : c + 1, :]
    o_ref[...] = jnp.zeros(o_ref.shape, F32)
    for k in range(panels):
        for b in range(count):
            at = slice(b * base, (b + 1) * base)
            o_ref[k, at, at] = x[k * count + b]
    size = base
    while size < width:
        for k in range(panels):
            for o in range(0, width, 2 * size):
                up, down = slice(o, o + size), slice(o + size, o + 2 * size)
                inner = dot(d_ref[down, k * width + o : k * width + o + size].astype(F32), o_ref[k, up, up], NN, lax.Precision.HIGHEST)
                o_ref[k, down, up] = -dot(o_ref[k, down, down], inner, NN, lax.Precision.HIGHEST)
        size *= 2


def invert(lower):
    width = lower.shape[0]
    return pl.pallas_call(
        functools.partial(invert_kernel, min(32, width)),
        out_shape=jax.ShapeDtypeStruct((lower.shape[1] // width, width, width), F32),
        compiler_params=params(16),
        cost_estimate=pl.CostEstimate(flops=1 << 20, bytes_accessed=1 << 18, transcendentals=0),
    )(lower)


def apply_inverse(inverse, rows):
    total = None
    for _ in range(2):
        part = inverse.astype(BF16)
        inverse = inverse - part.astype(F32)
        term = dot(part, rows)
        total = term if total is None else total + term
    return total.astype(BF16)


def solve_kernel(
    width, piece, inv_ref, own_ref, key_ref, r_hbm, y_ref, small_ref, zero_ref, r_ref, u_ref, fill_ref, ins, outs
):
    devices, _, part = r_ref.shape
    slots = 2 * width
    loads = [pltpu.make_async_copy(r_hbm.at[s], r_ref.at[s], ins.at[s]) for s in range(devices)]
    for load in loads:
        load.start()
    want = lax.broadcasted_iota(I32, (devices * CAP, slots), 0)
    want = (want // CAP) * slots + want % CAP
    hot = jnp.where(want.astype(F32) == key_ref[0:1, :], 1.0, 0.0).astype(BF16)
    loads[0].wait()
    zero = r_ref[0, :slots, :]
    zero_ref[...] = zero
    fill_ref[...] = dot(hot, zero).astype(BF16)
    sends = []
    for d in range(devices):
        fills = fill_ref.at[d * CAP : (d + 1) * CAP]
        sends.append(pltpu.make_async_copy(fills, y_ref.at[d, slots:], outs.at[0, d]))
        sends[-1].start()
    rows = jnp.where(own_ref[...] > 0, zero.astype(F32), 0.0).astype(BF16)
    for s in range(1, devices):
        loads[s].wait()
        rows = rows + r_ref[s, :slots, :]
    for k in range(2):
        here = slice(k * width, (k + 1) * width)
        u_ref[here, :] = apply_inverse(inv_ref[k], rows[here])
        for d in range(devices):
            sends.append(pltpu.make_async_copy(u_ref.at[here], y_ref.at[d, here], outs.at[1 + k, d]))
            sends[-1].start()
    for h in range(pl.cdiv(width, part)):
        have = min(part, width - h * part)
        at = slice(slots + h * piece, slots + (h + 1) * piece)
        moving = r_ref[0, at, :have]
        picked = jnp.where(key_ref[1:2, h * part : h * part + have] > 0, moving.astype(F32), 0.0).astype(BF16)
        for s in range(1, devices):
            picked = picked + r_ref[s, at, :have]
        small_ref[:, h * part : h * part + have] = picked
        small_ref[:, width + h * part : width + h * part + have] = moving
    for send in sends:
        send.wait()


def solve(inverse, own, key, received, width, piece):
    devices, _, part = received.shape
    vmem = pl.BlockSpec(memory_space=pltpu.VMEM)
    return pl.pallas_call(
        functools.partial(solve_kernel, width, piece),
        out_shape=(
            jax.ShapeDtypeStruct((devices, 2 * width + CAP, part), BF16),
            jax.ShapeDtypeStruct((piece, 2 * width), BF16),
            jax.ShapeDtypeStruct((2 * width, part), BF16),
        ),
        in_specs=[vmem, vmem, vmem, pl.BlockSpec(memory_space=pl.ANY)],
        out_specs=(pl.BlockSpec(memory_space=pl.ANY), vmem, vmem),
        scratch_shapes=[
            pltpu.VMEM(received.shape, BF16),
            pltpu.VMEM((2 * width, part), BF16),
            pltpu.VMEM((devices * CAP, part), BF16),
            pltpu.SemaphoreType.DMA((devices,)),
            pltpu.SemaphoreType.DMA((3, devices)),
        ],
        compiler_params=params(24),
        cost_estimate=pl.CostEstimate(flops=1 << 29, bytes_accessed=4 << 20, transcendentals=0),
    )(inverse, own, key, received)


def arrange_kernel(width, chips, origins, where, inv_ref, sel_ref, below_ref, land_ref, *refs):
    *piece_refs, o_ref, w_ref, moving_ref, l_ref = refs
    _, piece, cols = piece_refs[0].shape
    step = pl.program_id(0)
    for ref, (back, flip, start) in zip(piece_refs, origins):
        across = lax.rem(where[1] - back + chips, chips)
        column = 2 * across + lax.rem(where[2] + flip, 2)
        for k in range(ref.shape[0]):
            at = pl.multiple_of((start + k) * width + column * piece, piece)
            l_ref[pl.ds(at, piece), :] = ref[k]

    @pl.when((step == 0) & (where[0] == 0))
    def _():
        moving_ref[...] = l_ref[:width, width : 2 * width]

    @pl.when((step == 0) & (where[0] != 0))
    def _():
        moving_ref[...] = below_ref[...]

    here = lax.broadcasted_iota(I32, (width, cols), 1) + where[0] + step * cols
    landing = jnp.where(land_ref[...] == here, 1.0, 0.0)
    moved = dot(moving_ref[...], landing.astype(BF16))
    l_ref[:width, :] = jnp.where(
        landing.sum(0, keepdims=True) > 0, moved, l_ref[:width, :].astype(F32)
    ).astype(BF16)
    o_ref[...] = l_ref[...].T

    @pl.when(step == 0)
    def _():
        coupling = lax.dot_general(
            inv_ref[1], sel_ref[...].astype(F32), (((1,), (1,)), ((), ())),
            preferred_element_type=F32, precision=lax.Precision.HIGHEST,
        )
        w_ref[...] = coupling


def arrange(inverse, selected, below, landing, chips, origins, parts, where):
    panels, piece, height = parts[0].shape
    width = below.shape[0]
    cols = min(512, height)
    pieces = [pl.BlockSpec((part.shape[0], piece, cols), lambda i, *_: (0, 0, i)) for part in parts]
    return pl.pallas_call(
        functools.partial(arrange_kernel, width, chips, origins),
        out_shape=(
            pltpu.HBM((height, panels * width), BF16),
            pltpu.HBM((width, width), F32),
        ),
        grid_spec=pltpu.PrefetchScalarGridSpec(
            num_scalar_prefetch=1,
            grid=(height // cols,),
            in_specs=[
                pl.BlockSpec(inverse.shape, lambda i, *_: (0, 0, 0)),
                pl.BlockSpec(selected.shape, lambda i, *_: (0, 0)),
                pl.BlockSpec(below.shape, lambda i, *_: (0, 0)),
                pl.BlockSpec((width, 1), lambda i, *_: (0, 0)),
            ]
            + pieces,
            out_specs=(
                pl.BlockSpec((cols, panels * width), lambda i, *_: (i, 0)),
                pl.BlockSpec((width, width), lambda i, *_: (0, 0)),
            ),
            scratch_shapes=[pltpu.VMEM((width, width), BF16), pltpu.VMEM((panels * width, cols), BF16)],
        ),
        compiler_params=params(32),
        cost_estimate=pl.CostEstimate(flops=1 << 24, bytes_accessed=1 << 20, transcendentals=0),
    )(where, inverse, selected, below, landing[:, None], *parts)


def update_kernel(
    width, rows, table, place, w_ref, slab_ref, l_hbm, y_ref, rest_ref, o_ref, a_ref, l_ref, u_ref, d_ref, f_ref, out_ref, ins, sems, load
):
    devices, _, part = y_ref.shape
    height, cols = a_ref.shape
    steps = height // rows
    wide = min(512, cols)
    first = place[0] == 0
    block = [slice(i * rows, (i + 1) * rows) for i in range(steps)]
    uppers, fills, loads = [], [], []
    for e in range(devices):
        at = slice(e * part, (e + 1) * part)
        uppers.append(pltpu.make_async_copy(y_ref.at[e, : 2 * width], u_ref.at[:, at], load.at[e]))
        fills.append(pltpu.make_async_copy(y_ref.at[e, 2 * width :], d_ref.at[:CAP, at], load.at[devices + e]))
    for i, here in enumerate(block):
        loads.append(
            (
                pltpu.make_async_copy(slab_ref.at[here], a_ref.at[here], ins.at[0, i]),
                pltpu.make_async_copy(l_hbm.at[here], l_ref.at[here], ins.at[1, i]),
            )
        )
    for copy in (*uppers, *fills):
        copy.start()
    for copy in (*uppers, *fills):
        copy.wait()
    for copy in sum((list(pair) for pair in loads[:2]), []):
        copy.start()
    high = w_ref[...].astype(BF16)
    rest = (w_ref[...] - high.astype(F32)).astype(BF16)
    for c in range(0, cols, wide):
        at = slice(c, c + wide)
        upper = u_ref[:width, at]
        later = u_ref[width:, at].astype(F32) - (dot(high, upper) + dot(rest, upper))
        u_ref[width:, at] = later.astype(BF16)

    @pl.when(jnp.logical_not(first) & (table[2, steps] > CAP))
    def _():
        for e in range(devices):
            copy = pltpu.make_async_copy(
                rest_ref.at[e, CAP : 2 * width], d_ref.at[CAP:, e * part : (e + 1) * part], sems.at[0, 0]
            )
            copy.start()
            copy.wait()

    group = 16

    def put(row, to):
        target = pl.ds(pl.multiple_of(to // group * group, group), group)
        old = a_ref[target, :].astype(F32)
        lane = lax.broadcasted_iota(I32, old.shape, 0)
        a_ref[target, :] = jnp.where(lane == to % group, row, old).astype(BF16)

    def put_from(from_ref, j):
        source = table[1, j]
        taken = from_ref[pl.ds(pl.multiple_of(source // group * group, group), group), :].astype(F32)
        lane = lax.broadcasted_iota(I32, taken.shape, 0)
        put(jnp.where(lane == source % group, taken, 0.0).sum(0, keepdims=True), table[0, j])

    @pl.when(jnp.logical_not(first))
    def _():
        f_ref[...] = d_ref[:CAP, :].astype(F32)

    few = table[2, steps] <= CAP

    copies = []
    for i, here in enumerate(block):
        for copy in loads[i]:
            copy.wait()
        if i + 2 < steps:
            for copy in loads[i + 2]:
                copy.start()
        slot = i % 2

        @pl.when(first)
        def _(i=i):
            pl.loop(table[2, i], table[2, i + 1])(lambda j: put_from(a_ref, j))

        @pl.when(jnp.logical_not(first) & few)
        def _(i=i):
            pl.loop(table[2, i], table[2, i + 1])(lambda j: put(f_ref[pl.ds(table[1, j], 1), :], table[0, j]))

        @pl.when(jnp.logical_not(first) & jnp.logical_not(few))
        def _(i=i):
            pl.loop(table[2, i], table[2, i + 1])(lambda j: put_from(d_ref, j))

        if i >= 2:
            for copy in copies[i - 2]:
                copy.wait()
        copies.append([])
        for b, c in enumerate(range(0, cols, wide)):
            at = slice(c, c + wide)
            out_ref[slot, :, at] = (a_ref[here, at].astype(F32) - dot(l_ref[here, :], u_ref[:, at])).astype(BF16)
            if i == 0:

                @pl.when(first)
                def _(at=at):
                    out_ref[0, :, at] = u_ref[:, at]

            copies[i].append(pltpu.make_async_copy(out_ref.at[slot, :, at], o_ref.at[here, at], sems.at[slot, b]))
            copies[i][b].start()
    for copy in sum(copies[-2:], []):
        copy.wait()


def update(slab, lower, upper, coupling, rest, table, place, rows):
    height, cols = slab.shape
    width = lower.shape[1] // 2
    devices, steps = upper.shape[0], height // rows
    return pl.pallas_call(
        functools.partial(update_kernel, width, rows),
        out_shape=jax.ShapeDtypeStruct(slab.shape, BF16),
        grid_spec=pltpu.PrefetchScalarGridSpec(
            num_scalar_prefetch=2,
            grid=(1,),
            in_specs=[pl.BlockSpec(coupling.shape, lambda i, *_: (0, 0))] + [pl.BlockSpec(memory_space=pl.ANY)] * 4,
            out_specs=pl.BlockSpec(memory_space=pl.ANY),
            scratch_shapes=[
                pltpu.VMEM((height, cols), BF16),
                pltpu.VMEM(lower.shape, BF16),
                pltpu.VMEM((2 * width, cols), BF16),
                pltpu.VMEM((2 * width, cols), BF16),
                pltpu.VMEM((CAP, cols), F32),
                pltpu.VMEM((2, rows, cols), BF16),
                pltpu.SemaphoreType.DMA((2, steps)),
                pltpu.SemaphoreType.DMA((2, pl.cdiv(cols, 512))),
                pltpu.SemaphoreType.DMA((2 * devices,)),
            ],
        ),
        compiler_params=params(54),
        cost_estimate=pl.CostEstimate(
            flops=4 * height * cols * width, bytes_accessed=4 * height * cols, transcendentals=0
        ),
    )(table, place, coupling, slab, lower, upper, rest)


def exchange(x):
    return lax.all_to_all(x, "row", 0, 0)


def per_device(trailing, panels, diag_lower, pivot_src, pivot_dst):
    height, cols = trailing.shape
    width = diag_lower.shape[2]
    slots = 2 * width
    devices = lax.axis_size("row")
    place = lax.axis_index("row").astype(I32)
    offset = place * height
    received = gather(trailing, panels, pivot_src, pivot_dst, place[None], devices)
    received, diag_lower, panels = lax.optimization_barrier((received, diag_lower, panels))
    received = exchange(received)

    columns = lax.axis_size("col")
    chips = columns // 2
    across, core = lax.axis_index("col") // 2, lax.axis_index("col") % 2

    def forward(x, chips_on):
        return lax.ppermute(x, "col", [(d, (d + 2 * chips_on) % columns) for d in range(columns)])

    near = [forward(panels, s) for s in sorted({1, chips - 1} - {0} if chips > 1 else set())]
    diagonal = lax.all_gather(
        jnp.concatenate([diag_lower[0], diag_lower[1]], axis=1), "col", axis=0, tiled=True
    )
    diagonal, pivot_src, pivot_dst = lax.optimization_barrier((diagonal, pivot_src, pivot_dst))
    inverse = invert(diagonal)
    own, key, table = tables(pivot_src, pivot_dst, place[None], height, devices, slots)

    received, near = lax.optimization_barrier((received, near))
    sent, small, fills = solve(inverse, own, key, received, width, panels.shape[1])

    small = lax.all_gather(small, "col", axis=0, tiled=True)

    parts = [panels] + near
    origins = [(0, 0, 0)] + [(s, 0, 0) for s in ((1, chips - 1) if chips > 2 else (1,) if chips > 1 else ())]
    if chips == 4:
        parts += [forward(near[0][:1], 1), forward(near[1][1:], 3)]
        origins += [(2, 0, 0), (2, 0, 1)]
    parts += [lax.ppermute(part, "col", [(d, d ^ 1) for d in range(columns)]) for part in parts]
    origins += [(back, 1, start) for back, _, start in origins]

    selected, below = small[:, :width], small[:, width:slots]
    lower, coupling = arrange(
        inverse,
        selected,
        below,
        jnp.where(place == 0, pivot_dst[1], pivot_src[1]),
        chips,
        tuple(origins),
        parts,
        jnp.stack([offset, across, core]).astype(I32),
    )

    rounds = (table[3, 0] + CAP - 1) // CAP

    def fetch(state):
        r, found = state
        want = jnp.arange(devices * CAP, dtype=I32)
        want = want // CAP * slots + want % CAP + r * CAP
        part = dot((want[:, None] == key[:1].astype(I32)).astype(BF16), fills).astype(BF16)
        part = exchange(part.reshape(devices, CAP, -1))
        return r + 1, lax.dynamic_update_slice(found, part, (0, r * CAP, 0))

    found = lax.while_loop(lambda state: state[0] < rounds, fetch, (jnp.ones((), I32), received))[1]

    return update(trailing, lower, exchange(sent), coupling, found, table, place[None], slots)


def solution(mesh):
    placed = (P("row", "col"), P(None, "col", "row"), P(None, "col", None), P(), P())
    return jax.shard_map(
        per_device, mesh=mesh, in_specs=placed, out_specs=P("row", "col"), check_vma=False
    )
```

```python
import functools

import jax
import jax.numpy as jnp
from jax import lax
from jax.experimental import pallas as pl
from jax.experimental.pallas import tpu as pltpu
from jax.sharding import PartitionSpec as P

F32, BF16, I32 = jnp.float32, jnp.bfloat16, jnp.int32
TN = (((0,), (0,)), ((), ()))
NN = (((1,), (0,)), ((), ()))
CAP = 64
LANES = 128


def dot(a, b, dims=NN, precision=None):
    return lax.dot_general(a, b, dims, preferred_element_type=F32, precision=precision)


def params(mib):
    return pltpu.CompilerParams(vmem_limit_bytes=mib << 20)


def as_column(row):
    size = row.shape[1]
    eye = lax.broadcasted_iota(I32, (size, size), 0) == lax.broadcasted_iota(I32, (size, size), 1)
    return jnp.where(eye, row, 0.0).sum(1, keepdims=True)


def lookup(keys, table, values, other):
    hit = keys == table
    found = jnp.where(hit, values, 0.0).sum(1, keepdims=True)
    return jnp.where(jnp.where(hit, 1.0, 0.0).sum(1, keepdims=True) > 0, found, other)


def as_row(column):
    size = column.shape[0]
    eye = lax.broadcasted_iota(I32, (size, size), 0) == lax.broadcasted_iota(I32, (size, size), 1)
    return jnp.where(eye, column, 0.0).sum(0, keepdims=True)


def slot_rows(height, me, src_ref, dst_ref):
    width = src_ref.shape[1]
    dst0, dst1 = dst_ref[0:1, :].astype(F32), dst_ref[1:2, :].astype(F32)
    lane = lax.broadcasted_iota(I32, (1, width), 1).astype(F32)
    late = as_column(lane + width)
    late = as_row(lookup(late, dst0, lane, late))
    src1 = as_column(src_ref[1:2, :].astype(F32))
    source = jnp.concatenate([as_column(src_ref[0:1, :].astype(F32)), lookup(src1, dst0, lane, src1)])
    return source, lookup(source, dst1, late, lookup(source, dst0, lane, -1.0))


def owned_first(src_ref, height):
    return src_ref[1:2, :] < height


def table_kernel(height, devices, block, place, src_ref, dst_ref, own_ref, key_ref, table_ref):
    slots = 2 * src_ref.shape[1]
    me = place[0].astype(F32)
    source, content = slot_rows(height, me, src_ref, dst_ref)
    owner = jnp.zeros_like(source)
    for d in range(1, devices):
        owner = owner + jnp.where(source >= float(d * height), 1.0, 0.0)
    own_ref[...] = jnp.where(owner == 0, 1.0, 0.0)
    lane = lax.broadcasted_iota(I32, (slots, slots), 1).astype(F32)
    line = lax.broadcasted_iota(I32, (slots, slots), 0).astype(F32)
    rank = jnp.where((owner == as_row(owner)) & (lane < line), 1.0, 0.0).sum(1, keepdims=True)
    key = as_row(jnp.where(owner > 0, owner * slots + rank, -1.0))
    first = jnp.where(owned_first(src_ref, height), 1.0, 0.0)
    key_ref[...] = jnp.concatenate([key, jnp.concatenate([first, first], 1)] * 4)
    rest = jnp.where((owner == me) & (source >= slots), source - me * height, float(height))
    order = (as_row(rest) * slots + lane < rest * slots + line).astype(F32).sum(1, keepdims=True)
    sort = order == lane
    hole = jnp.where(sort, rest, 0.0).sum(0, keepdims=True)
    slot = jnp.where(sort, jnp.where(me == 0, content, rank), 0.0).sum(0, keepdims=True)
    begin = jnp.where(rest < lane * block, 1.0, 0.0).sum(0, keepdims=True)
    most = jnp.where(owner > 0, rank + 1.0, 0.0).max(0, keepdims=True)
    most = jnp.broadcast_to(most, (1, slots))
    table_ref[...] = jnp.concatenate([hole, slot, begin, most] * 2).astype(I32)


def tables(pivot_src, pivot_dst, place, height, devices, block):
    slots = 2 * pivot_src.shape[1]
    whole = lambda i, *_: (0, 0)
    return pl.pallas_call(
        functools.partial(table_kernel, height, devices, block),
        out_shape=(
            jax.ShapeDtypeStruct((slots, 1), F32),
            jax.ShapeDtypeStruct((8, slots), F32),
            jax.ShapeDtypeStruct((8, slots), I32),
        ),
        grid_spec=pltpu.PrefetchScalarGridSpec(
            num_scalar_prefetch=1,
            grid=(1,),
            in_specs=[pl.BlockSpec(pivot_src.shape, whole), pl.BlockSpec(pivot_dst.shape, whole)],
            out_specs=(
                pl.BlockSpec((slots, 1), whole),
                pl.BlockSpec((8, slots), whole),
                pl.BlockSpec((8, slots), whole),
            ),
        ),
        compiler_params=params(24),
    )(place, pivot_src, pivot_dst)


def gather_kernel(
    height, chunk, tiles, place, src_ref, dst_ref, p_ref, slab_ref, o_ref, a_ref, top_ref, low_ref, spread_ref, acc_ref, extra_ref, out_ref, sems, outs
):
    width = src_ref.shape[1]
    slots = 2 * width
    cols = a_ref.shape[1] // tiles
    part = o_ref.shape[2]
    tile = [slice(t * cols, (t + 1) * cols) for t in range(tiles)]
    copies = [pltpu.make_async_copy(slab_ref.at[:, at], a_ref.at[:, at], sems.at[t]) for t, at in enumerate(tile)]
    for copy in copies[:2]:
        copy.start()

    me = place[0].astype(F32)
    source, content = slot_rows(height, me, src_ref, dst_ref)
    here = source - me * height
    wanted = jnp.where((here >= 0) & (here < height), here, jnp.where(me == 0, content, -1.0))
    column = lax.broadcasted_iota(I32, (slots, slots), 1).astype(F32)
    top_ref[...] = jnp.where(column == wanted, 1.0, 0.0).astype(BF16)
    low = wanted >= slots
    before = jnp.where(column < lax.broadcasted_iota(I32, (slots, slots), 0).astype(F32), 1.0, 0.0)
    flag = jnp.where(low, 1.0, 0.0)
    rank = dot(before.astype(BF16), jnp.broadcast_to(flag, (slots, LANES)).astype(BF16))[:, :1]
    rank = jnp.where(low, rank, -1.0)
    rounds = (flag.sum().astype(I32) + chunk - 1) // chunk

    def build(r, carry):
        spot = lax.broadcasted_iota(I32, (slots, chunk), 1).astype(F32) + (r * chunk).astype(F32)
        spread = rank == spot
        spread_ref[r] = jnp.where(spread, 1.0, 0.0).astype(BF16)
        row = as_column(jnp.where(spread, wanted, 0.0).sum(0, keepdims=True))
        below = lax.broadcasted_iota(I32, low_ref.shape[1:], 1).astype(F32) + float(slots)
        low_ref[r] = jnp.where(below == row, 1.0, 0.0).astype(BF16)
        return carry

    lax.fori_loop(0, rounds, build, 0)

    src1 = as_column(src_ref[1:2, :].astype(F32))
    lane = lax.broadcasted_iota(I32, (1, width), 1).astype(F32)
    here = src1 - me * height
    moving = lookup(src1, dst_ref[1:2, :].astype(F32), lane + width, -1.0)
    chosen = jnp.where((here >= 0) & (here < height), here, jnp.where(me == 0, moving, -1.0))
    row = lax.broadcasted_iota(I32, (height, width), 0).astype(F32)
    hot = jnp.where(row == as_row(chosen), 1.0, 0.0).astype(BF16)
    taken = dot(p_ref[0], hot).astype(BF16)
    piece = taken.shape[0]
    for h in range(extra_ref.shape[0] // piece):
        have = min(part, width - h * part)
        extra_ref[h * piece : (h + 1) * piece, :have] = taken[:, h * part : h * part + have]

    sends = []
    for t in range(tiles):
        copies[t].wait()
        if t + 2 < tiles:
            copies[t + 2].start()
        at = tile[t]
        acc_ref[...] = dot(top_ref[...], a_ref[:slots, at])

        def add(r, carry, at=at):
            found = dot(low_ref[r], a_ref[slots:, at]).astype(BF16)
            acc_ref[...] += dot(spread_ref[r], found)
            return carry

        lax.fori_loop(0, rounds, add, 0)
        for b in range(cols // part):
            out_ref[t * (cols // part) + b, :slots, :] = acc_ref[:, b * part : (b + 1) * part].astype(BF16)
            out_ref[t * (cols // part) + b, slots:, :] = extra_ref[...]
        done = slice(t * (cols // part), (t + 1) * (cols // part))
        sends.append(pltpu.make_async_copy(out_ref.at[done], o_ref.at[done], outs.at[t]))
        sends[t].start()
    for send in sends:
        send.wait()


def gather(slab, panels, pivot_src, pivot_dst, place, devices):
    height, cols = slab.shape
    width = pivot_src.shape[1]
    slots, part = 2 * width, cols // devices
    chunk = min(64, slots)
    most = slots // chunk
    tiles = min(4, devices)
    piece = panels.shape[1]
    extra = piece * pl.cdiv(width, part)
    return pl.pallas_call(
        functools.partial(gather_kernel, height, chunk, tiles),
        out_shape=jax.ShapeDtypeStruct((devices, slots + extra, part), BF16),
        grid_spec=pltpu.PrefetchScalarGridSpec(
            num_scalar_prefetch=1,
            grid=(1,),
            in_specs=[
                pl.BlockSpec(pivot_src.shape, lambda i, *_: (0, 0)),
                pl.BlockSpec(pivot_dst.shape, lambda i, *_: (0, 0)),
                pl.BlockSpec((1, piece, height), lambda i, *_: (0, 0, 0)),
                pl.BlockSpec(memory_space=pl.ANY),
            ],
            out_specs=pl.BlockSpec(memory_space=pl.ANY),
            scratch_shapes=[
                pltpu.VMEM((height, cols), BF16),
                pltpu.VMEM((slots, slots), BF16),
                pltpu.VMEM((most, chunk, height - slots), BF16),
                pltpu.VMEM((most, slots, chunk), BF16),
                pltpu.VMEM((slots, cols // tiles), F32),
                pltpu.VMEM((extra, part), BF16),
                pltpu.VMEM((devices, slots + extra, part), BF16),
                pltpu.SemaphoreType.DMA((tiles,)),
                pltpu.SemaphoreType.DMA((tiles,)),
            ],
        ),
        compiler_params=params(58),
        cost_estimate=pl.CostEstimate(
            flops=slots * height * cols, bytes_accessed=2 * cols * (height + slots), transcendentals=0
        ),
    )(place, pivot_src, pivot_dst, panels, slab)


def invert_kernel(base, d_ref, o_ref):
    panels, width, _ = o_ref.shape
    count = width // base
    blocks = []
    for k in range(panels):
        for b in range(count):
            at = slice(b * base, (b + 1) * base)
            blocks.append(d_ref[at, k * width + b * base : k * width + (b + 1) * base].astype(F32))
    lower = jnp.stack(blocks)
    row = lax.broadcasted_iota(I32, lower.shape, 1)
    col = lax.broadcasted_iota(I32, lower.shape, 2)
    x = jnp.where(row == col, 1.0, 0.0).astype(F32)
    for c in range(base - 1):
        x = x - lower[:, :, c : c + 1] * x[:, c : c + 1, :]
    o_ref[...] = jnp.zeros(o_ref.shape, F32)
    for k in range(panels):
        for b in range(count):
            at = slice(b * base, (b + 1) * base)
            o_ref[k, at, at] = x[k * count + b]
    size = base
    while size < width:
        for k in range(panels):
            for o in range(0, width, 2 * size):
                up, down = slice(o, o + size), slice(o + size, o + 2 * size)
                inner = dot(d_ref[down, k * width + o : k * width + o + size].astype(F32), o_ref[k, up, up], NN, lax.Precision.HIGHEST)
                o_ref[k, down, up] = -dot(o_ref[k, down, down], inner, NN, lax.Precision.HIGHEST)
        size *= 2


def invert(lower):
    width = lower.shape[0]
    return pl.pallas_call(
        functools.partial(invert_kernel, min(32, width)),
        out_shape=jax.ShapeDtypeStruct((lower.shape[1] // width, width, width), F32),
        compiler_params=params(16),
        cost_estimate=pl.CostEstimate(flops=1 << 20, bytes_accessed=1 << 18, transcendentals=0),
    )(lower)


def apply_inverse(inverse, rows):
    total = None
    for _ in range(2):
        part = inverse.astype(BF16)
        inverse = inverse - part.astype(F32)
        term = dot(part, rows)
        total = term if total is None else total + term
    return total.astype(BF16)


def solve_kernel(
    width, piece, inv_ref, own_ref, key_ref, r_hbm, y_ref, small_ref, zero_ref, r_ref, u_ref, fill_ref, ins, outs
):
    devices, _, part = r_ref.shape
    slots = 2 * width
    loads = [pltpu.make_async_copy(r_hbm.at[s], r_ref.at[s], ins.at[s]) for s in range(devices)]
    for load in loads:
        load.start()
    want = lax.broadcasted_iota(I32, (devices * CAP, slots), 0)
    want = (want // CAP) * slots + want % CAP
    hot = jnp.where(want.astype(F32) == key_ref[0:1, :], 1.0, 0.0).astype(BF16)
    loads[0].wait()
    zero = r_ref[0, :slots, :]
    zero_ref[...] = zero
    fill_ref[...] = dot(hot, zero).astype(BF16)
    sends = []
    for d in range(devices):
        fills = fill_ref.at[d * CAP : (d + 1) * CAP]
        sends.append(pltpu.make_async_copy(fills, y_ref.at[d, slots:], outs.at[0, d]))
        sends[-1].start()
    rows = jnp.where(own_ref[...] > 0, zero.astype(F32), 0.0).astype(BF16)
    for s in range(1, devices):
        loads[s].wait()
        rows = rows + r_ref[s, :slots, :]
    for k in range(2):
        here = slice(k * width, (k + 1) * width)
        u_ref[here, :] = apply_inverse(inv_ref[k], rows[here])
        for d in range(devices):
            sends.append(pltpu.make_async_copy(u_ref.at[here], y_ref.at[d, here], outs.at[1 + k, d]))
            sends[-1].start()
    for h in range(pl.cdiv(width, part)):
        have = min(part, width - h * part)
        at = slice(slots + h * piece, slots + (h + 1) * piece)
        moving = r_ref[0, at, :have]
        picked = jnp.where(key_ref[1:2, h * part : h * part + have] > 0, moving.astype(F32), 0.0).astype(BF16)
        for s in range(1, devices):
            picked = picked + r_ref[s, at, :have]
        small_ref[:, h * part : h * part + have] = picked
        small_ref[:, width + h * part : width + h * part + have] = moving
    for send in sends:
        send.wait()


def solve(inverse, own, key, received, width, piece):
    devices, _, part = received.shape
    vmem = pl.BlockSpec(memory_space=pltpu.VMEM)
    return pl.pallas_call(
        functools.partial(solve_kernel, width, piece),
        out_shape=(
            jax.ShapeDtypeStruct((devices, 2 * width + CAP, part), BF16),
            jax.ShapeDtypeStruct((piece, 2 * width), BF16),
            jax.ShapeDtypeStruct((2 * width, part), BF16),
        ),
        in_specs=[vmem, vmem, vmem, pl.BlockSpec(memory_space=pl.ANY)],
        out_specs=(pl.BlockSpec(memory_space=pl.ANY), vmem, vmem),
        scratch_shapes=[
            pltpu.VMEM(received.shape, BF16),
            pltpu.VMEM((2 * width, part), BF16),
            pltpu.VMEM((devices * CAP, part), BF16),
            pltpu.SemaphoreType.DMA((devices,)),
            pltpu.SemaphoreType.DMA((3, devices)),
        ],
        compiler_params=params(24),
        cost_estimate=pl.CostEstimate(flops=1 << 29, bytes_accessed=4 << 20, transcendentals=0),
    )(inverse, own, key, received)


def arrange_kernel(width, chips, origins, where, inv_ref, sel_ref, below_ref, land_ref, *refs):
    *piece_refs, o_ref, w_ref, moving_ref, l_ref = refs
    _, piece, cols = piece_refs[0].shape
    step = pl.program_id(0)
    for ref, (back, flip, start) in zip(piece_refs, origins):
        across = lax.rem(where[1] - back + chips, chips)
        column = 2 * across + lax.rem(where[2] + flip, 2)
        for k in range(ref.shape[0]):
            at = pl.multiple_of((start + k) * width + column * piece, piece)
            l_ref[pl.ds(at, piece), :] = ref[k]

    @pl.when((step == 0) & (where[0] == 0))
    def _():
        moving_ref[...] = l_ref[:width, width : 2 * width]

    @pl.when((step == 0) & (where[0] != 0))
    def _():
        moving_ref[...] = below_ref[...]

    here = lax.broadcasted_iota(I32, (width, cols), 1) + where[0] + step * cols
    landing = jnp.where(land_ref[...] == here, 1.0, 0.0)
    moved = dot(moving_ref[...], landing.astype(BF16))
    l_ref[:width, :] = jnp.where(
        landing.sum(0, keepdims=True) > 0, moved, l_ref[:width, :].astype(F32)
    ).astype(BF16)
    o_ref[...] = l_ref[...].T

    @pl.when(step == 0)
    def _():
        coupling = lax.dot_general(
            inv_ref[1], sel_ref[...].astype(F32), (((1,), (1,)), ((), ())),
            preferred_element_type=F32, precision=lax.Precision.HIGHEST,
        )
        w_ref[...] = coupling


def arrange(inverse, selected, below, landing, chips, origins, parts, where):
    panels, piece, height = parts[0].shape
    width = below.shape[0]
    cols = min(512, height)
    pieces = [pl.BlockSpec((part.shape[0], piece, cols), lambda i, *_: (0, 0, i)) for part in parts]
    return pl.pallas_call(
        functools.partial(arrange_kernel, width, chips, origins),
        out_shape=(
            pltpu.HBM((height, panels * width), BF16),
            pltpu.HBM((width, width), F32),
        ),
        grid_spec=pltpu.PrefetchScalarGridSpec(
            num_scalar_prefetch=1,
            grid=(height // cols,),
            in_specs=[
                pl.BlockSpec(inverse.shape, lambda i, *_: (0, 0, 0)),
                pl.BlockSpec(selected.shape, lambda i, *_: (0, 0)),
                pl.BlockSpec(below.shape, lambda i, *_: (0, 0)),
                pl.BlockSpec((width, 1), lambda i, *_: (0, 0)),
            ]
            + pieces,
            out_specs=(
                pl.BlockSpec((cols, panels * width), lambda i, *_: (i, 0)),
                pl.BlockSpec((width, width), lambda i, *_: (0, 0)),
            ),
            scratch_shapes=[pltpu.VMEM((width, width), BF16), pltpu.VMEM((panels * width, cols), BF16)],
        ),
        compiler_params=params(32),
        cost_estimate=pl.CostEstimate(flops=1 << 24, bytes_accessed=1 << 20, transcendentals=0),
    )(where, inverse, selected, below, landing[:, None], *parts)


def update_kernel(
    width, rows, table, place, w_ref, slab_ref, l_hbm, y_ref, rest_ref, o_ref, a_ref, l_ref, u_ref, d_ref, f_ref, out_ref, ins, sems, load
):
    devices, _, part = y_ref.shape
    height, cols = a_ref.shape
    steps = height // rows
    wide = min(512, cols)
    first = place[0] == 0
    block = [slice(i * rows, (i + 1) * rows) for i in range(steps)]
    uppers, fills, loads = [], [], []
    for e in range(devices):
        at = slice(e * part, (e + 1) * part)
        uppers.append(pltpu.make_async_copy(y_ref.at[e, : 2 * width], u_ref.at[:, at], load.at[e]))
        fills.append(pltpu.make_async_copy(y_ref.at[e, 2 * width :], d_ref.at[:CAP, at], load.at[devices + e]))
    for i, here in enumerate(block):
        loads.append(
            (
                pltpu.make_async_copy(slab_ref.at[here], a_ref.at[here], ins.at[0, i]),
                pltpu.make_async_copy(l_hbm.at[here], l_ref.at[here], ins.at[1, i]),
            )
        )
    ahead = 3
    for copy in (*uppers, *fills, *loads[0]):
        copy.start()
    for copy in (*uppers, *fills):
        copy.wait()
    for copy in sum((list(pair) for pair in loads[1:ahead]), []):
        copy.start()
    high = w_ref[...].astype(BF16)
    rest = (w_ref[...] - high.astype(F32)).astype(BF16)
    for c in range(0, cols, wide):
        at = slice(c, c + wide)
        upper = u_ref[:width, at]
        later = u_ref[width:, at].astype(F32) - (dot(high, upper) + dot(rest, upper))
        u_ref[width:, at] = later.astype(BF16)

    @pl.when(jnp.logical_not(first) & (table[2, steps] > CAP))
    def _():
        for e in range(devices):
            copy = pltpu.make_async_copy(
                rest_ref.at[e, CAP : 2 * width], d_ref.at[CAP:, e * part : (e + 1) * part], sems.at[0, 0]
            )
            copy.start()
            copy.wait()

    group = 16

    def put(row, to):
        target = pl.ds(pl.multiple_of(to // group * group, group), group)
        old = a_ref[target, :].astype(F32)
        lane = lax.broadcasted_iota(I32, old.shape, 0)
        a_ref[target, :] = jnp.where(lane == to % group, row, old).astype(BF16)

    def put_from(from_ref, j):
        source = table[1, j]
        taken = from_ref[pl.ds(pl.multiple_of(source // group * group, group), group), :].astype(F32)
        lane = lax.broadcasted_iota(I32, taken.shape, 0)
        put(jnp.where(lane == source % group, taken, 0.0).sum(0, keepdims=True), table[0, j])

    @pl.when(jnp.logical_not(first))
    def _():
        f_ref[...] = d_ref[:CAP, :].astype(F32)

    few = table[2, steps] <= CAP

    copies = []
    for i, here in enumerate(block):
        for copy in loads[i]:
            copy.wait()
        if i + ahead < steps:
            for copy in loads[i + ahead]:
                copy.start()
        slot = i % 2

        @pl.when(first)
        def _(i=i):
            pl.loop(table[2, i], table[2, i + 1])(lambda j: put_from(a_ref, j))

        @pl.when(jnp.logical_not(first) & few)
        def _(i=i):
            pl.loop(table[2, i], table[2, i + 1])(lambda j: put(f_ref[pl.ds(table[1, j], 1), :], table[0, j]))

        @pl.when(jnp.logical_not(first) & jnp.logical_not(few))
        def _(i=i):
            pl.loop(table[2, i], table[2, i + 1])(lambda j: put_from(d_ref, j))

        if i >= 2:
            for copy in copies[i - 2]:
                copy.wait()
        copies.append([])
        for b, c in enumerate(range(0, cols, wide)):
            at = slice(c, c + wide)
            out_ref[slot, :, at] = (a_ref[here, at].astype(F32) - dot(l_ref[here, :], u_ref[:, at])).astype(BF16)
            if i == 0:

                @pl.when(first)
                def _(at=at):
                    out_ref[0, :, at] = u_ref[:, at]

            copies[i].append(pltpu.make_async_copy(out_ref.at[slot, :, at], o_ref.at[here, at], sems.at[slot, b]))
            copies[i][b].start()
    for copy in sum(copies[-2:], []):
        copy.wait()


def update(slab, lower, upper, coupling, rest, table, place, rows):
    height, cols = slab.shape
    width = lower.shape[1] // 2
    devices, steps = upper.shape[0], height // rows
    return pl.pallas_call(
        functools.partial(update_kernel, width, rows),
        out_shape=jax.ShapeDtypeStruct(slab.shape, BF16),
        grid_spec=pltpu.PrefetchScalarGridSpec(
            num_scalar_prefetch=2,
            grid=(1,),
            in_specs=[pl.BlockSpec(coupling.shape, lambda i, *_: (0, 0))] + [pl.BlockSpec(memory_space=pl.ANY)] * 4,
            out_specs=pl.BlockSpec(memory_space=pl.ANY),
            scratch_shapes=[
                pltpu.VMEM((height, cols), BF16),
                pltpu.VMEM(lower.shape, BF16),
                pltpu.VMEM((2 * width, cols), BF16),
                pltpu.VMEM((2 * width, cols), BF16),
                pltpu.VMEM((CAP, cols), F32),
                pltpu.VMEM((2, rows, cols), BF16),
                pltpu.SemaphoreType.DMA((2, steps)),
                pltpu.SemaphoreType.DMA((2, pl.cdiv(cols, 512))),
                pltpu.SemaphoreType.DMA((2 * devices,)),
            ],
        ),
        compiler_params=params(54),
        cost_estimate=pl.CostEstimate(
            flops=4 * height * cols * width, bytes_accessed=4 * height * cols, transcendentals=0
        ),
    )(table, place, coupling, slab, lower, upper, rest)


def exchange(x):
    return lax.all_to_all(x, "row", 0, 0)


def per_device(trailing, panels, diag_lower, pivot_src, pivot_dst):
    height, cols = trailing.shape
    width = diag_lower.shape[2]
    slots = 2 * width
    devices = lax.axis_size("row")
    place = lax.axis_index("row").astype(I32)
    offset = place * height
    received = gather(trailing, panels, pivot_src, pivot_dst, place[None], devices)
    received, diag_lower, panels = lax.optimization_barrier((received, diag_lower, panels))
    received = exchange(received)

    columns = lax.axis_size("col")
    chips = columns // 2
    across, core = lax.axis_index("col") // 2, lax.axis_index("col") % 2

    def forward(x, chips_on):
        return lax.ppermute(x, "col", [(d, (d + 2 * chips_on) % columns) for d in range(columns)])

    near = [forward(panels, s) for s in sorted({1, chips - 1} - {0} if chips > 1 else set())]
    diagonal = lax.all_gather(
        jnp.concatenate([diag_lower[0], diag_lower[1]], axis=1), "col", axis=0, tiled=True
    )
    diagonal, pivot_src, pivot_dst = lax.optimization_barrier((diagonal, pivot_src, pivot_dst))
    inverse = invert(diagonal)
    own, key, table = tables(pivot_src, pivot_dst, place[None], height, devices, slots)

    received, near = lax.optimization_barrier((received, near))
    sent, small, fills = solve(inverse, own, key, received, width, panels.shape[1])

    small = lax.all_gather(small, "col", axis=0, tiled=True)

    parts = [panels] + near
    origins = [(0, 0, 0)] + [(s, 0, 0) for s in ((1, chips - 1) if chips > 2 else (1,) if chips > 1 else ())]
    if chips == 4:
        parts += [forward(near[0][:1], 1), forward(near[1][1:], 3)]
        origins += [(2, 0, 0), (2, 0, 1)]
    parts += [lax.ppermute(part, "col", [(d, d ^ 1) for d in range(columns)]) for part in parts]
    origins += [(back, 1, start) for back, _, start in origins]

    selected, below = small[:, :width], small[:, width:slots]
    lower, coupling = arrange(
        inverse,
        selected,
        below,
        jnp.where(place == 0, pivot_dst[1], pivot_src[1]),
        chips,
        tuple(origins),
        parts,
        jnp.stack([offset, across, core]).astype(I32),
    )

    rounds = (table[3, 0] + CAP - 1) // CAP

    def fetch(state):
        r, found = state
        want = jnp.arange(devices * CAP, dtype=I32)
        want = want // CAP * slots + want % CAP + r * CAP
        part = dot((want[:, None] == key[:1].astype(I32)).astype(BF16), fills).astype(BF16)
        part = exchange(part.reshape(devices, CAP, -1))
        return r + 1, lax.dynamic_update_slice(found, part, (0, r * CAP, 0))

    found = lax.while_loop(lambda state: state[0] < rounds, fetch, (jnp.ones((), I32), received))[1]

    return update(trailing, lower, exchange(sent), coupling, found, table, place[None], slots)


def solution(mesh):
    placed = (P("row", "col"), P(None, "col", "row"), P(None, "col", None), P(), P())
    return jax.shard_map(
        per_device, mesh=mesh, in_specs=placed, out_specs=P("row", "col"), check_vma=False
    )
```

```python
import functools

import jax
import jax.numpy as jnp
from jax import lax
from jax.experimental import pallas as pl
from jax.experimental.pallas import tpu as pltpu
from jax.sharding import PartitionSpec as P

F32, BF16, I32 = jnp.float32, jnp.bfloat16, jnp.int32
TN = (((0,), (0,)), ((), ()))
NN = (((1,), (0,)), ((), ()))
CAP = 64
LANES = 128


def dot(a, b, dims=NN, precision=None):
    return lax.dot_general(a, b, dims, preferred_element_type=F32, precision=precision)


def params(mib):
    return pltpu.CompilerParams(vmem_limit_bytes=mib << 20)


def as_column(row):
    size = row.shape[1]
    eye = lax.broadcasted_iota(I32, (size, size), 0) == lax.broadcasted_iota(I32, (size, size), 1)
    return jnp.where(eye, row, 0.0).sum(1, keepdims=True)


def lookup(keys, table, values, other):
    hit = keys == table
    found = jnp.where(hit, values, 0.0).sum(1, keepdims=True)
    return jnp.where(jnp.where(hit, 1.0, 0.0).sum(1, keepdims=True) > 0, found, other)


def as_row(column):
    size = column.shape[0]
    eye = lax.broadcasted_iota(I32, (size, size), 0) == lax.broadcasted_iota(I32, (size, size), 1)
    return jnp.where(eye, column, 0.0).sum(0, keepdims=True)


def slot_rows(height, me, src_ref, dst_ref):
    width = src_ref.shape[1]
    dst0, dst1 = dst_ref[0:1, :].astype(F32), dst_ref[1:2, :].astype(F32)
    lane = lax.broadcasted_iota(I32, (1, width), 1).astype(F32)
    late = as_column(lane + width)
    late = as_row(lookup(late, dst0, lane, late))
    src1 = as_column(src_ref[1:2, :].astype(F32))
    source = jnp.concatenate([as_column(src_ref[0:1, :].astype(F32)), lookup(src1, dst0, lane, src1)])
    return source, lookup(source, dst1, late, lookup(source, dst0, lane, -1.0))


def owned_first(src_ref, height):
    return src_ref[1:2, :] < height


def table_kernel(height, devices, block, place, src_ref, dst_ref, own_ref, key_ref, table_ref):
    slots = 2 * src_ref.shape[1]
    me = place[0].astype(F32)
    source, content = slot_rows(height, me, src_ref, dst_ref)
    owner = jnp.zeros_like(source)
    for d in range(1, devices):
        owner = owner + jnp.where(source >= float(d * height), 1.0, 0.0)
    own_ref[...] = jnp.where(owner == 0, 1.0, 0.0)
    lane = lax.broadcasted_iota(I32, (slots, slots), 1).astype(F32)
    line = lax.broadcasted_iota(I32, (slots, slots), 0).astype(F32)
    rank = jnp.where((owner == as_row(owner)) & (lane < line), 1.0, 0.0).sum(1, keepdims=True)
    key = as_row(jnp.where(owner > 0, owner * slots + rank, -1.0))
    first = jnp.where(owned_first(src_ref, height), 1.0, 0.0)
    key_ref[...] = jnp.concatenate([key, jnp.concatenate([first, first], 1)] * 4)
    rest = jnp.where((owner == me) & (source >= slots), source - me * height, float(height))
    order = (as_row(rest) * slots + lane < rest * slots + line).astype(F32).sum(1, keepdims=True)
    sort = order == lane
    hole = jnp.where(sort, rest, 0.0).sum(0, keepdims=True)
    slot = jnp.where(sort, jnp.where(me == 0, content, rank), 0.0).sum(0, keepdims=True)
    begin = jnp.where(rest < lane * block, 1.0, 0.0).sum(0, keepdims=True)
    most = jnp.where(owner > 0, rank + 1.0, 0.0).max(0, keepdims=True)
    most = jnp.broadcast_to(most, (1, slots))
    table_ref[...] = jnp.concatenate([hole, slot, begin, most] * 2).astype(I32)


def tables(pivot_src, pivot_dst, place, height, devices, block):
    slots = 2 * pivot_src.shape[1]
    whole = lambda i, *_: (0, 0)
    return pl.pallas_call(
        functools.partial(table_kernel, height, devices, block),
        out_shape=(
            jax.ShapeDtypeStruct((slots, 1), F32),
            jax.ShapeDtypeStruct((8, slots), F32),
            jax.ShapeDtypeStruct((8, slots), I32),
        ),
        grid_spec=pltpu.PrefetchScalarGridSpec(
            num_scalar_prefetch=1,
            grid=(1,),
            in_specs=[pl.BlockSpec(pivot_src.shape, whole), pl.BlockSpec(pivot_dst.shape, whole)],
            out_specs=(
                pl.BlockSpec((slots, 1), whole),
                pl.BlockSpec((8, slots), whole),
                pl.BlockSpec((8, slots), whole),
            ),
        ),
        compiler_params=params(24),
    )(place, pivot_src, pivot_dst)


def gather_kernel(
    height, chunk, tiles, place, src_ref, dst_ref, p_ref, slab_ref, o_ref, a_ref, top_ref, low_ref, spread_ref, acc_ref, extra_ref, out_ref, sems, outs
):
    width = src_ref.shape[1]
    slots = 2 * width
    cols = a_ref.shape[1] // tiles
    part = o_ref.shape[2]
    tile = [slice(t * cols, (t + 1) * cols) for t in range(tiles)]
    copies = [pltpu.make_async_copy(slab_ref.at[:, at], a_ref.at[:, at], sems.at[t]) for t, at in enumerate(tile)]
    for copy in copies[:2]:
        copy.start()

    me = place[0].astype(F32)
    source, content = slot_rows(height, me, src_ref, dst_ref)
    here = source - me * height
    wanted = jnp.where((here >= 0) & (here < height), here, jnp.where(me == 0, content, -1.0))
    column = lax.broadcasted_iota(I32, (slots, slots), 1).astype(F32)
    top_ref[...] = jnp.where(column == wanted, 1.0, 0.0).astype(BF16)
    low = wanted >= slots
    before = jnp.where(column < lax.broadcasted_iota(I32, (slots, slots), 0).astype(F32), 1.0, 0.0)
    flag = jnp.where(low, 1.0, 0.0)
    rank = dot(before.astype(BF16), jnp.broadcast_to(flag, (slots, LANES)).astype(BF16))[:, :1]
    rank = jnp.where(low, rank, -1.0)
    rounds = (flag.sum().astype(I32) + chunk - 1) // chunk

    def build(r, carry):
        spot = lax.broadcasted_iota(I32, (slots, chunk), 1).astype(F32) + (r * chunk).astype(F32)
        spread = rank == spot
        spread_ref[r] = jnp.where(spread, 1.0, 0.0).astype(BF16)
        row = as_column(jnp.where(spread, wanted, 0.0).sum(0, keepdims=True))
        below = lax.broadcasted_iota(I32, low_ref.shape[1:], 1).astype(F32) + float(slots)
        low_ref[r] = jnp.where(below == row, 1.0, 0.0).astype(BF16)
        return carry

    lax.fori_loop(0, rounds, build, 0)

    src1 = as_column(src_ref[1:2, :].astype(F32))
    lane = lax.broadcasted_iota(I32, (1, width), 1).astype(F32)
    here = src1 - me * height
    moving = lookup(src1, dst_ref[1:2, :].astype(F32), lane + width, -1.0)
    chosen = jnp.where((here >= 0) & (here < height), here, jnp.where(me == 0, moving, -1.0))
    row = lax.broadcasted_iota(I32, (height, width), 0).astype(F32)
    hot = jnp.where(row == as_row(chosen), 1.0, 0.0).astype(BF16)
    taken = dot(p_ref[0], hot).astype(BF16)
    piece = taken.shape[0]
    for h in range(extra_ref.shape[0] // piece):
        have = min(part, width - h * part)
        extra_ref[h * piece : (h + 1) * piece, :have] = taken[:, h * part : h * part + have]

    sends = []
    for t in range(tiles):
        copies[t].wait()
        if t + 2 < tiles:
            copies[t + 2].start()
        at = tile[t]
        acc_ref[...] = dot(top_ref[...], a_ref[:slots, at])

        def add(r, carry, at=at):
            found = dot(low_ref[r], a_ref[slots:, at]).astype(BF16)
            acc_ref[...] += dot(spread_ref[r], found)
            return carry

        lax.fori_loop(0, rounds, add, 0)
        for b in range(cols // part):
            out_ref[t * (cols // part) + b, :slots, :] = acc_ref[:, b * part : (b + 1) * part].astype(BF16)
            out_ref[t * (cols // part) + b, slots:, :] = extra_ref[...]
        done = slice(t * (cols // part), (t + 1) * (cols // part))
        sends.append(pltpu.make_async_copy(out_ref.at[done], o_ref.at[done], outs.at[t]))
        sends[t].start()
    for send in sends:
        send.wait()


def gather(slab, panels, pivot_src, pivot_dst, place, devices):
    height, cols = slab.shape
    width = pivot_src.shape[1]
    slots, part = 2 * width, cols // devices
    chunk = min(LANES, slots)
    most = slots // chunk
    tiles = min(4, devices)
    piece = panels.shape[1]
    extra = piece * pl.cdiv(width, part)
    return pl.pallas_call(
        functools.partial(gather_kernel, height, chunk, tiles),
        out_shape=jax.ShapeDtypeStruct((devices, slots + extra, part), BF16),
        grid_spec=pltpu.PrefetchScalarGridSpec(
            num_scalar_prefetch=1,
            grid=(1,),
            in_specs=[
                pl.BlockSpec(pivot_src.shape, lambda i, *_: (0, 0)),
                pl.BlockSpec(pivot_dst.shape, lambda i, *_: (0, 0)),
                pl.BlockSpec((1, piece, height), lambda i, *_: (0, 0, 0)),
                pl.BlockSpec(memory_space=pl.ANY),
            ],
            out_specs=pl.BlockSpec(memory_space=pl.ANY),
            scratch_shapes=[
                pltpu.VMEM((height, cols), BF16),
                pltpu.VMEM((slots, slots), BF16),
                pltpu.VMEM((most, chunk, height - slots), BF16),
                pltpu.VMEM((most, slots, chunk), BF16),
                pltpu.VMEM((slots, cols // tiles), F32),
                pltpu.VMEM((extra, part), BF16),
                pltpu.VMEM((devices, slots + extra, part), BF16),
                pltpu.SemaphoreType.DMA((tiles,)),
                pltpu.SemaphoreType.DMA((tiles,)),
            ],
        ),
        compiler_params=params(58),
        cost_estimate=pl.CostEstimate(
            flops=slots * height * cols, bytes_accessed=2 * cols * (height + slots), transcendentals=0
        ),
    )(place, pivot_src, pivot_dst, panels, slab)


def invert_kernel(base, d_ref, o_ref):
    panels, width, _ = o_ref.shape
    count = width // base
    blocks = []
    for k in range(panels):
        for b in range(count):
            at = slice(b * base, (b + 1) * base)
            blocks.append(d_ref[at, k * width + b * base : k * width + (b + 1) * base].astype(F32))
    lower = jnp.stack(blocks)
    row = lax.broadcasted_iota(I32, lower.shape, 1)
    col = lax.broadcasted_iota(I32, lower.shape, 2)
    x = jnp.where(row == col, 1.0, 0.0).astype(F32)
    for c in range(base - 1):
        x = x - lower[:, :, c : c + 1] * x[:, c : c + 1, :]
    o_ref[...] = jnp.zeros(o_ref.shape, F32)
    for k in range(panels):
        for b in range(count):
            at = slice(b * base, (b + 1) * base)
            o_ref[k, at, at] = x[k * count + b]
    size = base
    while size < width:
        for k in range(panels):
            for o in range(0, width, 2 * size):
                up, down = slice(o, o + size), slice(o + size, o + 2 * size)
                inner = dot(d_ref[down, k * width + o : k * width + o + size].astype(F32), o_ref[k, up, up], NN, lax.Precision.HIGHEST)
                o_ref[k, down, up] = -dot(o_ref[k, down, down], inner, NN, lax.Precision.HIGHEST)
        size *= 2


def invert(lower):
    width = lower.shape[0]
    return pl.pallas_call(
        functools.partial(invert_kernel, min(32, width)),
        out_shape=jax.ShapeDtypeStruct((lower.shape[1] // width, width, width), F32),
        compiler_params=params(16),
        cost_estimate=pl.CostEstimate(flops=1 << 20, bytes_accessed=1 << 18, transcendentals=0),
    )(lower)


def apply_inverse(inverse, rows):
    total = None
    for _ in range(2):
        part = inverse.astype(BF16)
        inverse = inverse - part.astype(F32)
        term = dot(part, rows)
        total = term if total is None else total + term
    return total.astype(BF16)


def solve_kernel(
    width, piece, inv_ref, own_ref, key_ref, r_hbm, y_ref, small_ref, zero_ref, r_ref, u_ref, fill_ref, ins, outs
):
    devices, _, part = r_ref.shape
    slots = 2 * width
    loads = [pltpu.make_async_copy(r_hbm.at[s], r_ref.at[s], ins.at[s]) for s in range(devices)]
    for load in loads:
        load.start()
    want = lax.broadcasted_iota(I32, (devices * CAP, slots), 0)
    want = (want // CAP) * slots + want % CAP
    hot = jnp.where(want.astype(F32) == key_ref[0:1, :], 1.0, 0.0).astype(BF16)
    loads[0].wait()
    zero = r_ref[0, :slots, :]
    zero_ref[...] = zero
    fill_ref[...] = dot(hot, zero).astype(BF16)
    sends = []
    for d in range(devices):
        fills = fill_ref.at[d * CAP : (d + 1) * CAP]
        sends.append(pltpu.make_async_copy(fills, y_ref.at[d, slots:], outs.at[0, d]))
        sends[-1].start()
    rows = jnp.where(own_ref[...] > 0, zero.astype(F32), 0.0).astype(BF16)
    for s in range(1, devices):
        loads[s].wait()
        rows = rows + r_ref[s, :slots, :]
    for k in range(2):
        here = slice(k * width, (k + 1) * width)
        u_ref[here, :] = apply_inverse(inv_ref[k], rows[here])
        for d in range(devices):
            sends.append(pltpu.make_async_copy(u_ref.at[here], y_ref.at[d, here], outs.at[1 + k, d]))
            sends[-1].start()
    for h in range(pl.cdiv(width, part)):
        have = min(part, width - h * part)
        at = slice(slots + h * piece, slots + (h + 1) * piece)
        moving = r_ref[0, at, :have]
        picked = jnp.where(key_ref[1:2, h * part : h * part + have] > 0, moving.astype(F32), 0.0).astype(BF16)
        for s in range(1, devices):
            picked = picked + r_ref[s, at, :have]
        small_ref[:, h * part : h * part + have] = picked
        small_ref[:, width + h * part : width + h * part + have] = moving
    for send in sends:
        send.wait()


def solve(inverse, own, key, received, width, piece):
    devices, _, part = received.shape
    vmem = pl.BlockSpec(memory_space=pltpu.VMEM)
    return pl.pallas_call(
        functools.partial(solve_kernel, width, piece),
        out_shape=(
            jax.ShapeDtypeStruct((devices, 2 * width + CAP, part), BF16),
            jax.ShapeDtypeStruct((piece, 2 * width), BF16),
            jax.ShapeDtypeStruct((2 * width, part), BF16),
        ),
        in_specs=[vmem, vmem, vmem, pl.BlockSpec(memory_space=pl.ANY)],
        out_specs=(pl.BlockSpec(memory_space=pl.ANY), vmem, vmem),
        scratch_shapes=[
            pltpu.VMEM(received.shape, BF16),
            pltpu.VMEM((2 * width, part), BF16),
            pltpu.VMEM((devices * CAP, part), BF16),
            pltpu.SemaphoreType.DMA((devices,)),
            pltpu.SemaphoreType.DMA((3, devices)),
        ],
        compiler_params=params(24),
        cost_estimate=pl.CostEstimate(flops=1 << 29, bytes_accessed=4 << 20, transcendentals=0),
    )(inverse, own, key, received)


def arrange_kernel(width, chips, origins, where, inv_ref, sel_ref, below_ref, land_ref, *refs):
    *piece_refs, o_ref, w_ref, moving_ref, l_ref = refs
    _, piece, cols = piece_refs[0].shape
    step = pl.program_id(0)
    for ref, (back, flip, start) in zip(piece_refs, origins):
        across = lax.rem(where[1] - back + chips, chips)
        column = 2 * across + lax.rem(where[2] + flip, 2)
        for k in range(ref.shape[0]):
            at = pl.multiple_of((start + k) * width + column * piece, piece)
            l_ref[pl.ds(at, piece), :] = ref[k]

    @pl.when((step == 0) & (where[0] == 0))
    def _():
        moving_ref[...] = l_ref[:width, width : 2 * width]

    @pl.when((step == 0) & (where[0] != 0))
    def _():
        moving_ref[...] = below_ref[...]

    here = lax.broadcasted_iota(I32, (width, cols), 1) + where[0] + step * cols
    landing = jnp.where(land_ref[...] == here, 1.0, 0.0)
    moved = dot(moving_ref[...], landing.astype(BF16))
    l_ref[:width, :] = jnp.where(
        landing.sum(0, keepdims=True) > 0, moved, l_ref[:width, :].astype(F32)
    ).astype(BF16)
    o_ref[...] = l_ref[...].T

    @pl.when(step == 0)
    def _():
        coupling = lax.dot_general(
            inv_ref[1], sel_ref[...].astype(F32), (((1,), (1,)), ((), ())),
            preferred_element_type=F32, precision=lax.Precision.HIGHEST,
        )
        w_ref[...] = coupling


def arrange(inverse, selected, below, landing, chips, origins, parts, where):
    panels, piece, height = parts[0].shape
    width = below.shape[0]
    cols = min(512, height)
    pieces = [pl.BlockSpec((part.shape[0], piece, cols), lambda i, *_: (0, 0, i)) for part in parts]
    return pl.pallas_call(
        functools.partial(arrange_kernel, width, chips, origins),
        out_shape=(
            pltpu.HBM((height, panels * width), BF16),
            pltpu.HBM((width, width), F32),
        ),
        grid_spec=pltpu.PrefetchScalarGridSpec(
            num_scalar_prefetch=1,
            grid=(height // cols,),
            in_specs=[
                pl.BlockSpec(inverse.shape, lambda i, *_: (0, 0, 0)),
                pl.BlockSpec(selected.shape, lambda i, *_: (0, 0)),
                pl.BlockSpec(below.shape, lambda i, *_: (0, 0)),
                pl.BlockSpec((width, 1), lambda i, *_: (0, 0)),
            ]
            + pieces,
            out_specs=(
                pl.BlockSpec((cols, panels * width), lambda i, *_: (i, 0)),
                pl.BlockSpec((width, width), lambda i, *_: (0, 0)),
            ),
            scratch_shapes=[pltpu.VMEM((width, width), BF16), pltpu.VMEM((panels * width, cols), BF16)],
        ),
        compiler_params=params(32),
        cost_estimate=pl.CostEstimate(flops=1 << 24, bytes_accessed=1 << 20, transcendentals=0),
    )(where, inverse, selected, below, landing[:, None], *parts)


def update_kernel(
    width, rows, table, place, w_ref, slab_ref, l_hbm, y_ref, rest_ref, o_ref, a_ref, l_ref, u_ref, d_ref, out_ref, ins, sems, load
):
    devices, _, part = y_ref.shape
    height, cols = a_ref.shape
    steps = height // rows
    wide = min(512, cols)
    first = place[0] == 0
    block = [slice(i * rows, (i + 1) * rows) for i in range(steps)]
    uppers, fills, loads = [], [], []
    for e in range(devices):
        at = slice(e * part, (e + 1) * part)
        uppers.append(pltpu.make_async_copy(y_ref.at[e, : 2 * width], u_ref.at[:, at], load.at[e]))
        fills.append(pltpu.make_async_copy(y_ref.at[e, 2 * width :], d_ref.at[:CAP, at], load.at[devices + e]))
    for i, here in enumerate(block):
        loads.append(
            (
                pltpu.make_async_copy(slab_ref.at[here], a_ref.at[here], ins.at[0, i]),
                pltpu.make_async_copy(l_hbm.at[here], l_ref.at[here], ins.at[1, i]),
            )
        )
    for copy in (*uppers, *fills, *loads[0]):
        copy.start()
    for copy in uppers:
        copy.wait()
    if steps > 1:
        for copy in loads[1]:
            copy.start()
    high = w_ref[...].astype(BF16)
    rest = (w_ref[...] - high.astype(F32)).astype(BF16)
    for c in range(0, cols, wide):
        at = slice(c, c + wide)
        upper = u_ref[:width, at]
        later = u_ref[width:, at].astype(F32) - (dot(high, upper) + dot(rest, upper))
        u_ref[width:, at] = later.astype(BF16)

    @pl.when(jnp.logical_not(first) & (table[2, steps] > CAP))
    def _():
        for e in range(devices):
            copy = pltpu.make_async_copy(
                rest_ref.at[e, CAP : 2 * width], d_ref.at[CAP:, e * part : (e + 1) * part], sems.at[0, 0]
            )
            copy.start()
            copy.wait()

    group = 16

    def put(from_ref, j):
        to, source = table[0, j], table[1, j]
        taken = from_ref[pl.ds(pl.multiple_of(source // group * group, group), group), :].astype(F32)
        lane = lax.broadcasted_iota(I32, taken.shape, 0)
        row = jnp.where(lane == source % group, taken, 0.0).sum(0, keepdims=True)
        target = pl.ds(pl.multiple_of(to // group * group, group), group)
        a_ref[target, :] = jnp.where(lane == to % group, row, a_ref[target, :].astype(F32)).astype(BF16)

    for copy in fills:
        copy.wait()
    copies = []
    for i, here in enumerate(block):
        for copy in loads[i]:
            copy.wait()
        if i + 2 < steps:
            for copy in loads[i + 2]:
                copy.start()
        slot = i % 2

        @pl.when(first)
        def _(i=i):
            pl.loop(table[2, i], table[2, i + 1])(lambda j: put(a_ref, j))

        @pl.when(jnp.logical_not(first))
        def _(i=i):
            pl.loop(table[2, i], table[2, i + 1])(lambda j: put(d_ref, j))

        if i >= 2:
            for copy in copies[i - 2]:
                copy.wait()
        copies.append([])
        for b, c in enumerate(range(0, cols, wide)):
            at = slice(c, c + wide)
            out_ref[slot, :, at] = (a_ref[here, at].astype(F32) - dot(l_ref[here, :], u_ref[:, at])).astype(BF16)
            if i == 0:

                @pl.when(first)
                def _(at=at):
                    out_ref[0, :, at] = u_ref[:, at]

            copies[i].append(pltpu.make_async_copy(out_ref.at[slot, :, at], o_ref.at[here, at], sems.at[slot, b]))
            copies[i][b].start()
    for copy in sum(copies[-2:], []):
        copy.wait()


def update(slab, lower, upper, coupling, rest, table, place, rows):
    height, cols = slab.shape
    width = lower.shape[1] // 2
    devices, steps = upper.shape[0], height // rows
    return pl.pallas_call(
        functools.partial(update_kernel, width, rows),
        out_shape=jax.ShapeDtypeStruct(slab.shape, BF16),
        grid_spec=pltpu.PrefetchScalarGridSpec(
            num_scalar_prefetch=2,
            grid=(1,),
            in_specs=[pl.BlockSpec(coupling.shape, lambda i, *_: (0, 0))] + [pl.BlockSpec(memory_space=pl.ANY)] * 4,
            out_specs=pl.BlockSpec(memory_space=pl.ANY),
            scratch_shapes=[
                pltpu.VMEM((height, cols), BF16),
                pltpu.VMEM(lower.shape, BF16),
                pltpu.VMEM((2 * width, cols), BF16),
                pltpu.VMEM((2 * width, cols), BF16),
                pltpu.VMEM((2, rows, cols), BF16),
                pltpu.SemaphoreType.DMA((2, steps)),
                pltpu.SemaphoreType.DMA((2, pl.cdiv(cols, 512))),
                pltpu.SemaphoreType.DMA((2 * devices,)),
            ],
        ),
        compiler_params=params(54),
        cost_estimate=pl.CostEstimate(
            flops=4 * height * cols * width, bytes_accessed=4 * height * cols, transcendentals=0
        ),
    )(table, place, coupling, slab, lower, upper, rest)


def exchange(x):
    return lax.all_to_all(x, "row", 0, 0)


def per_device(trailing, panels, diag_lower, pivot_src, pivot_dst):
    height, cols = trailing.shape
    width = diag_lower.shape[2]
    slots = 2 * width
    devices = lax.axis_size("row")
    place = lax.axis_index("row").astype(I32)
    offset = place * height
    received = gather(trailing, panels, pivot_src, pivot_dst, place[None], devices)
    received, diag_lower, panels = lax.optimization_barrier((received, diag_lower, panels))
    received = exchange(received)

    columns = lax.axis_size("col")
    chips = columns // 2
    across, core = lax.axis_index("col") // 2, lax.axis_index("col") % 2

    def forward(x, chips_on):
        return lax.ppermute(x, "col", [(d, (d + 2 * chips_on) % columns) for d in range(columns)])

    near = [forward(panels, s) for s in sorted({1, chips - 1} - {0} if chips > 1 else set())]
    diagonal = lax.all_gather(
        jnp.concatenate([diag_lower[0], diag_lower[1]], axis=1), "col", axis=0, tiled=True
    )
    diagonal, pivot_src, pivot_dst = lax.optimization_barrier((diagonal, pivot_src, pivot_dst))
    inverse = invert(diagonal)
    own, key, table = tables(pivot_src, pivot_dst, place[None], height, devices, slots)

    received, near = lax.optimization_barrier((received, near))
    sent, small, fills = solve(inverse, own, key, received, width, panels.shape[1])

    small = lax.all_gather(small, "col", axis=0, tiled=True)

    parts = [panels] + near
    origins = [(0, 0, 0)] + [(s, 0, 0) for s in ((1, chips - 1) if chips > 2 else (1,) if chips > 1 else ())]
    if chips == 4:
        parts += [forward(near[0][:1], 1), forward(near[1][1:], 3)]
        origins += [(2, 0, 0), (2, 0, 1)]
    parts += [lax.ppermute(part, "col", [(d, d ^ 1) for d in range(columns)]) for part in parts]
    origins += [(back, 1, start) for back, _, start in origins]

    selected, below = small[:, :width], small[:, width:slots]
    lower, coupling = arrange(
        inverse,
        selected,
        below,
        jnp.where(place == 0, pivot_dst[1], pivot_src[1]),
        chips,
        tuple(origins),
        parts,
        jnp.stack([offset, across, core]).astype(I32),
    )

    rounds = (table[3, 0] + CAP - 1) // CAP

    def fetch(state):
        r, found = state
        want = jnp.arange(devices * CAP, dtype=I32)
        want = want // CAP * slots + want % CAP + r * CAP
        part = dot((want[:, None] == key[:1].astype(I32)).astype(BF16), fills).astype(BF16)
        part = exchange(part.reshape(devices, CAP, -1))
        return r + 1, lax.dynamic_update_slice(found, part, (0, r * CAP, 0))

    found = lax.while_loop(lambda state: state[0] < rounds, fetch, (jnp.ones((), I32), received))[1]

    return update(trailing, lower, exchange(sent), coupling, found, table, place[None], slots)


def solution(mesh):
    placed = (P("row", "col"), P(None, "col", "row"), P(None, "col", None), P(), P())
    return jax.shard_map(
        per_device, mesh=mesh, in_specs=placed, out_specs=P("row", "col"), check_vma=False
    )
```
